32 devices in a mesh: dp: 8 (over z, x), seq: 4 (over y, core).
Axes of the slice: x: 2, y: 2, z: 4, core: 2. Of those that a mesh axis runs over, the one named last changes fastest.
Arguments:
- inputs: float32 [64, 1024, 256], P('dp', 'seq'), may hold values from -5 to 5
- encoded: float32 [64, 128, 256], P('dp'), may hold values from -5 to 5
- durations: int32 [64, 128], P('dp'), may hold values from 1 to 14
- lengths: int32 [64], P('dp'), may hold values from 512 to 1024, as said below
- time_embed: float32 [64, 1024], P('dp'), may hold values from -6 to 6
- cotangent: float32 [64, 1024, 256], P('dp', 'seq'), may hold values from -12 to 12
- res_master: float32 [722944], P(('dp', 'seq')), may hold values from -2 to 2
- res_moment: float32 [722944], P(('dp', 'seq'))
- res_average: float32 [722944], P(('dp', 'seq')), may hold values from -2 to 2
- tf_master: float32 [659968], P(('dp', 'seq')), may hold values from -2 to 2
- tf_moment: float32 [659968], P(('dp', 'seq'))
- tf_average: float32 [659968], P(('dp', 'seq')), may hold values from -2 to 2
Outputs:
- outputs: float32 [64, 1024, 256], P('dp', 'seq')
- grad_inputs: float32 [64, 1024, 256], P('dp', 'seq')
- res_grad: float32 [722944], P(('dp', 'seq'))
- tf_grad: float32 [659968], P(('dp', 'seq'))
- res_new: float32 [722944], P(('dp', 'seq'))
- tf_new: float32 [659968], P(('dp', 'seq'))
- res_moment_new: float32 [722944], P(('dp', 'seq'))
- tf_moment_new: float32 [659968], P(('dp', 'seq'))
- res_average_new: float32 [722944], P(('dp', 'seq'))
- tf_average_new: float32 [659968], P(('dp', 'seq'))
- res_low: bfloat16 [722944], P(('dp', 'seq'))
- tf_low: bfloat16 [659968], P(('dp', 'seq'))
The draws below stay inside these ranges and needn't reach their ends.
Inputs may be any that keep to these rules, and one draw needn't show every extreme that they name: `lengths`: valid frames of an utterance; in every draw some utterance has all 1024 frames valid.
All inputs are finite; a program needn't handle non-finite values.
Results may differ from the reference program's by a relative error of at most 0.014.
The reference program's roundings to bfloat16 on the way count: a program that leaves them out, or rounds other values in their place, can miss the bound.
Values may be sent and summed in bfloat16 or wider, within the bound.
A program may use at most 192 MiB of HBM per device.

```python
import math
import jax
import jax.numpy as jnp
from jax import lax

C = 256
GROUPS = 8
TE = 1024
HEADS = 2
HD = 64
F = 1024
L = 1024
P_SIZE = 128
UTTS = 64
TOKENS = 65536
RES_USED = 722944
TF_USED = 659968


def res_layout():
    bias_piece = (C, 0.3, 0.0)
    gain_piece = (C, 0.1, 1.0)
    return [(3 * C * C, 1.0 / math.sqrt(3 * C), 0.0), (3 * C * C, 1.0 / math.sqrt(3 * C), 0.0), (C * C, 1.0 / math.sqrt(C), 0.0), (TE * C, 1.0 / math.sqrt(TE), 0.0), bias_piece, gain_piece, bias_piece, bias_piece, gain_piece, bias_piece, bias_piece, bias_piece]


def tf_layout():
    inner = HEADS * HD
    bias_piece = (C, 0.3, 0.0)
    gain_piece = (C, 0.1, 1.0)
    wide_piece = (F, 0.3, 0.0)
    return [(3 * C * inner, 1.4 / math.sqrt(C), 0.0), (inner * C, math.sqrt(8.0 / inner), 0.0), (C * F, 1.0 / math.sqrt(C), 0.0), (F * C, 1.0 / math.sqrt(F), 0.0), gain_piece, bias_piece, bias_piece, gain_piece, bias_piece, bias_piece, wide_piece, wide_piece, wide_piece]


def draw_pieces(key, layout):
    pieces = []
    for position, piece in enumerate(layout):
        sub_key = jax.random.fold_in(key, position)
        unit = jnp.clip(jax.random.normal(sub_key, (piece[0],), jnp.float32), -5.0, 5.0)
        pieces.append(piece[2] + piece[1] * unit)
    return jnp.concatenate(pieces)


def draw_moment(key, length_total):
    scale_now = 0.5 * math.sqrt(TOKENS)
    unit = jnp.clip(jax.random.normal(key, (length_total,), jnp.float32), -5.0, 5.0)
    return scale_now * unit


def draw_res_master(key, part):
    return draw_pieces(jax.random.fold_in(key, 101), res_layout())


def draw_res_average(key, part):
    return draw_pieces(jax.random.fold_in(key, 102), res_layout())


def draw_res_moment(key, part):
    return draw_moment(jax.random.fold_in(key, 103), RES_USED)


def draw_tf_master(key, part):
    return draw_pieces(jax.random.fold_in(key, 201), tf_layout())


def draw_tf_average(key, part):
    return draw_pieces(jax.random.fold_in(key, 202), tf_layout())


def draw_tf_moment(key, part):
    return draw_moment(jax.random.fold_in(key, 203), TF_USED)


def draw_lengths(key, part):
    first_key, second_key = jax.random.split(jax.random.fold_in(key, 301))
    drawn = jax.random.randint(first_key, (UTTS,), L // 2, L + 1)
    chosen = jax.random.randint(second_key, (), 0, UTTS)
    return jnp.where(jnp.arange(UTTS) == chosen, L, drawn).astype(jnp.int32)


def draw_cotangent(key, part):
    first_key = jax.random.fold_in(jax.random.fold_in(key, 401), 0)
    rows_now = jnp.arange(UTTS, dtype=jnp.float32) / max(UTTS - 1, 1)
    row_scale = 0.5 * jnp.exp(rows_now * math.log(4.0))
    base = jnp.clip(jax.random.normal(first_key, (UTTS, L, C), jnp.float32), -5.0, 5.0)
    return base * row_scale[:, None, None]


def touch_ends(values, rng, smallest, largest):
    shape = values.shape
    spot = [jax.random.randint(jax.random.fold_in(rng, axis), (), 0, shape[axis]) for axis in range(len(shape))]
    values = values.at[tuple(spot)].set(smallest)
    longest = shape.index(max(shape))
    spot[longest] = (spot[longest] + 1) % shape[longest]
    return values.at[tuple(spot)].set(largest)


def block_scale(own_key, shape, cuts, low, largest):
    gain = 1.0
    for axis_at, blocks in cuts:
        steps = jax.random.uniform(jax.random.fold_in(jax.random.fold_in(own_key, 6), axis_at), (blocks,), jnp.float32, low / len(cuts), largest / len(cuts))
        gain = gain * jnp.repeat(jnp.exp(steps), shape[axis_at] // blocks).reshape((-1,) + (1,) * (len(shape) - 1 - axis_at))
    return gain


def normal_values(stream_key, dims, scale, reach, shards=(), kind=jnp.bfloat16):
    values = jax.random.normal(stream_key, dims, jnp.float32) * scale
    if len(shards) > 0:
        values = block_scale(stream_key, dims, shards, -0.22, 0.18) * values
    return jnp.clip(values, min=-reach, max=reach).astype(kind)


def setup_inputs(seed: int = 0) -> dict:
    splits = jax.random.split(jax.random.key(seed), 13)
    return {
        "inputs": normal_values(splits[0], (UTTS, L, C), 0.7, 5.0, ((0, 8), (1, 4)), jnp.float32),
        "encoded": normal_values(splits[1], (UTTS, P_SIZE, C), 0.7, 5.0, ((0, 8),), jnp.float32),
        "durations": touch_ends(jax.random.randint(splits[2], (UTTS, P_SIZE), 1, 15), jax.random.fold_in(splits[2], 1), 1, 14).astype(jnp.int32),
        "lengths": draw_lengths(jax.random.fold_in(splits[12], 71), 0),
        "time_embed": normal_values(splits[4], (UTTS, TE), 1.0, 6.0, ((0, 8),), jnp.float32),
        "cotangent": draw_cotangent(jax.random.fold_in(splits[12], 71), 0),
        "res_master": draw_res_master(jax.random.fold_in(splits[12], 71), 0),
        "res_moment": draw_res_moment(jax.random.fold_in(splits[12], 71), 0),
        "res_average": draw_res_average(jax.random.fold_in(splits[12], 71), 0),
        "tf_master": draw_tf_master(jax.random.fold_in(splits[12], 71), 0),
        "tf_moment": draw_tf_moment(jax.random.fold_in(splits[12], 71), 0),
        "tf_average": draw_tf_average(jax.random.fold_in(splits[12], 71), 0),
    }


EPSILON = 1e-05
SCORE_SCALE = 0.125
MOMENTUM = 0.9
AVERAGE_DECAY = 0.99
LEARN_BASE = 0.015
MASK_FILL = -1e+30

@jax.custom_vjp
def low(v):
    return lax.optimization_barrier(v.astype(jnp.bfloat16)).astype(jnp.float32)

@jax.custom_vjp
def low_back(v):
    return v

def low_keep(v):
    return (low(v), None)

def low_pass(kept, grad):
    return (grad,)

def back_keep(v):
    return (v, None)

def back_low(kept, grad):
    return (low(grad),)
low.defvjp(low_keep, low_pass)
low_back.defvjp(back_keep, back_low)

def highest(left, right):
    return jnp.matmul(left, right, precision=lax.Precision.HIGHEST)

def soft_plus(signal):
    return jnp.log1p(jnp.exp(-jnp.abs(signal))) + jnp.maximum(signal, 0.0)

def mish_fn(signal):
    return signal * jnp.tanh(soft_plus(signal))

def snake_fn(signal, alpha_row, beta_row):
    return signal + jnp.sin(signal * jnp.exp(alpha_row)) ** 2 / (jnp.exp(beta_row) + 1e-09)

def layer_norm(signal, gain_row, shift_row):
    center = signal - lax.optimization_barrier(jnp.mean(signal, axis=-1, keepdims=True))
    spread = lax.optimization_barrier(jnp.mean(center * center, axis=-1, keepdims=True))
    return center * lax.rsqrt(spread + EPSILON) * gain_row + shift_row

def unpack_res(flat):
    square = C * C
    conv_one = flat[0:3 * square].reshape(3, C, C)
    conv_two = flat[3 * square:6 * square].reshape(3, C, C)
    res_weight = flat[6 * square:7 * square].reshape(C, C)
    time_weight = flat[7 * square:7 * square + TE * C].reshape(TE, C)
    offset = 7 * square + TE * C
    small_rows = flat[offset:offset + 8 * C].reshape(8, C)
    return (conv_one, conv_two, res_weight, time_weight, small_rows)

def unpack_tf(flat):
    inner = HEADS * HD
    qkv_weight = flat[0:3 * C * inner].reshape(C, 3 * inner)
    offset = 3 * C * inner
    out_weight = flat[offset:offset + inner * C].reshape(inner, C)
    offset = offset + inner * C
    up_weight = flat[offset:offset + C * F].reshape(C, F)
    offset = offset + C * F
    down_weight = flat[offset:offset + F * C].reshape(F, C)
    offset = offset + F * C
    small_rows = flat[offset:offset + 6 * C].reshape(6, C)
    offset = offset + 6 * C
    wide_rows = flat[offset:offset + 3 * F].reshape(3, F)
    return (qkv_weight, out_weight, up_weight, down_weight, small_rows, wide_rows)

def conv_apply(signal, weight):
    padded = jnp.pad(signal, ((0, 0), (1, 1), (0, 0)))
    return highest(padded[:, :-2], weight[0]) + highest(padded[:, 1:-1], weight[1]) + highest(padded[:, 2:], weight[2])

def group_norm(signal, frame_mask, valid_count, gain_row, shift_row):
    width = C // GROUPS
    shape_now = signal.shape
    grouped = (signal * frame_mask[:, :, None]).reshape(shape_now[0], shape_now[1], GROUPS, width)
    total = lax.optimization_barrier(jnp.sum(grouped, axis=(1, 3)))
    squares = lax.optimization_barrier(jnp.sum(grouped * grouped, axis=(1, 3)))
    number = valid_count[:, None] * width
    mean_now = total / number
    inv_std = lax.rsqrt(squares / number - mean_now * mean_now + EPSILON)
    mean_wide = jnp.repeat(mean_now, width, axis=1)[:, None, :]
    inv_wide = jnp.repeat(inv_std, width, axis=1)[:, None, :]
    return (signal - mean_wide) * inv_wide * gain_row + shift_row

def take_rows(phone_table, phone_rows):
    return phone_table[phone_rows]

def forward(res_flat, tf_flat, start_in, encoded, durations, lengths, time_embed):
    conv_one, conv_two, res_weight, time_weight, res_rows = unpack_res(low(res_flat))
    qkv_weight, out_weight, up_weight, down_weight, tf_rows, wide_rows = unpack_tf(low(tf_flat))
    frame_ids = jnp.arange(L, dtype=jnp.int32)
    frame_mask = (frame_ids[None, :] < lengths[:, None]).astype(jnp.float32)
    valid_count = lengths.astype(jnp.float32)
    boundary = jnp.cumsum(durations, axis=1).astype(jnp.int32)
    phone = lax.optimization_barrier(jnp.sum((boundary[:, None, :] <= frame_ids[None, :, None]).astype(jnp.int32), axis=2)).astype(jnp.int32)
    phone = jnp.minimum(phone, P_SIZE - 1).astype(jnp.int32)
    start_state = start_in + jax.vmap(take_rows)(encoded, phone)
    wide_mask = frame_mask[:, :, None]
    masked_in = low(start_state * wide_mask)
    z_one = low_back(conv_apply(masked_in, conv_one) + res_rows[0])
    act_one = mish_fn(group_norm(z_one, frame_mask, valid_count, res_rows[1], res_rows[2])) * wide_mask
    time_act = low(mish_fn(time_embed))
    time_proj = highest(time_act, time_weight) + res_rows[7]
    masked_two = low((act_one + time_proj[:, None, :]) * wide_mask)
    z_two = low_back(conv_apply(masked_two, conv_two) + res_rows[3])
    act_two = mish_fn(group_norm(z_two, frame_mask, valid_count, res_rows[4], res_rows[5])) * wide_mask
    skip_out = low_back(highest(masked_in, res_weight) + res_rows[6])
    block_out = act_two + skip_out
    inner = HEADS * HD
    utt_here = start_in.shape[0]
    attn_in = low(layer_norm(block_out, tf_rows[0], tf_rows[1]))
    qkv_all = low(low_back(highest(attn_in, qkv_weight)))
    queries = qkv_all[:, :, :inner].reshape(utt_here, L, HEADS, HD)
    keys = qkv_all[:, :, inner:2 * inner].reshape(utt_here, L, HEADS, HD)
    values = qkv_all[:, :, 2 * inner:].reshape(utt_here, L, HEADS, HD)
    scores = low_back(jnp.einsum('uqhd,ukhd->uhqk', queries, keys, precision=lax.Precision.HIGHEST) * SCORE_SCALE)
    key_mask = frame_ids[None, :] < lengths[:, None]
    scores = jnp.where(key_mask[:, None, None, :], scores, MASK_FILL)
    top_score = lax.optimization_barrier(jnp.max(scores, axis=-1, keepdims=True))
    expo = jnp.exp(scores - top_score)
    probs = low(expo / lax.optimization_barrier(jnp.sum(expo, axis=-1, keepdims=True)))
    mixed = jnp.einsum('uhqk,ukhd->uqhd', probs, values, precision=lax.Precision.HIGHEST)
    attn_vals = low(low_back(mixed.reshape(utt_here, L, inner)))
    attn_out = low_back(highest(attn_vals, out_weight) + tf_rows[2])
    mid_state = block_out + attn_out
    ff_in = low(layer_norm(mid_state, tf_rows[3], tf_rows[4]))
    up_out = low_back(highest(ff_in, up_weight) + wide_rows[0])
    snake_out = low(snake_fn(up_out, wide_rows[1], wide_rows[2]))
    ff_out = low_back(highest(snake_out, down_weight) + tf_rows[5])
    return (mid_state + ff_out) * wide_mask

def update(master, moment, average, grad):
    rate = LEARN_BASE / math.sqrt(TOKENS)
    moment_new = MOMENTUM * moment + grad
    master_new = master - rate * (grad + MOMENTUM * moment_new)
    average_new = AVERAGE_DECAY * average + (1.0 - AVERAGE_DECAY) * master_new
    return (master_new, moment_new, average_new, master_new.astype(jnp.bfloat16))

def reference(inputs, encoded, durations, lengths, time_embed, cotangent, res_master, res_moment, res_average, tf_master, tf_moment, tf_average):
    group_size = math.gcd(UTTS, 4)
    step_count = UTTS // group_size

    def regroup(array):
        return array.reshape((step_count, group_size) + array.shape[1:])

    def one_group(carry, item):
        res_sum, tf_sum = carry
        part_in, part_enc, part_dur, part_len, part_time, part_cot = item

        def local_forward(res_flat, tf_flat, start_in):
            return forward(res_flat, tf_flat, start_in, part_enc, part_dur, part_len, part_time)
        result, pull_back = jax.vjp(local_forward, res_master, tf_master, part_in)
        grad_res, grad_tf, grad_in = pull_back(part_cot)
        return ((res_sum + grad_res, tf_sum + grad_tf), (result, grad_in))
    initial = (jnp.zeros_like(res_master), jnp.zeros_like(tf_master))
    items = (regroup(inputs), regroup(encoded), regroup(durations), regroup(lengths), regroup(time_embed), regroup(cotangent))
    (res_grad, tf_grad), (results, grad_parts) = lax.scan(one_group, initial, items)
    outputs = results.reshape(UTTS, L, C)
    grad_inputs = grad_parts.reshape(UTTS, L, C)
    res_new, res_moment_new, res_average_new, res_low = update(res_master, res_moment, res_average, res_grad)
    tf_new, tf_moment_new, tf_average_new, tf_low = update(tf_master, tf_moment, tf_average, tf_grad)
    return (outputs, grad_inputs, res_grad, tf_grad, res_new, tf_new, res_moment_new, tf_moment_new, res_average_new, tf_average_new, res_low, tf_low)
```

```python
import math

import jax
import jax.numpy as jnp
from jax import lax
from jax.sharding import PartitionSpec as P

C = 256
GROUPS = 8
TE = 1024
HEADS = 2
HD = 64
F = 1024


EPSILON = 1e-05
SCORE_SCALE = 0.125
MOMENTUM = 0.9
AVERAGE_DECAY = 0.99
LEARN_BASE = 0.015
MASK_FILL = -1e30


def soft_plus(signal):
    return jnp.log1p(jnp.exp(-jnp.abs(signal))) + jnp.maximum(signal, 0.0)


def mish_fn(signal):
    return signal * jnp.tanh(soft_plus(signal))


def snake_fn(signal, alpha_row, beta_row):
    return signal + jnp.sin(signal * jnp.exp(alpha_row)) ** 2 / (jnp.exp(beta_row) + 1e-09)


def layer_norm(signal, gain_row, shift_row):
    center = signal - jnp.mean(signal, axis=-1, keepdims=True)
    spread = jnp.mean(center * center, axis=-1, keepdims=True)
    return center * lax.rsqrt(spread + EPSILON) * gain_row + shift_row


def unpack_res(flat):
    square = C * C
    conv_one = flat[0 : 3 * square].reshape(3, C, C)
    conv_two = flat[3 * square : 6 * square].reshape(3, C, C)
    res_weight = flat[6 * square : 7 * square].reshape(C, C)
    time_weight = flat[7 * square : 7 * square + TE * C].reshape(TE, C)
    offset = 7 * square + TE * C
    small_rows = flat[offset : offset + 8 * C].reshape(8, C)
    return (conv_one, conv_two, res_weight, time_weight, small_rows)


def unpack_tf(flat):
    inner = HEADS * HD
    qkv_weight = flat[0 : 3 * C * inner].reshape(C, 3 * inner)
    offset = 3 * C * inner
    out_weight = flat[offset : offset + inner * C].reshape(inner, C)
    offset = offset + inner * C
    up_weight = flat[offset : offset + C * F].reshape(C, F)
    offset = offset + C * F
    down_weight = flat[offset : offset + F * C].reshape(F, C)
    offset = offset + F * C
    small_rows = flat[offset : offset + 6 * C].reshape(6, C)
    offset = offset + 6 * C
    wide_rows = flat[offset : offset + 3 * F].reshape(3, F)
    return (qkv_weight, out_weight, up_weight, down_weight, small_rows, wide_rows)


def take_rows(phone_table, phone_rows):
    return phone_table[phone_rows]


def rim_pad(signal):
    return jnp.pad(signal, ((0, 0), (1, 1), (0, 0)))


def conv_apply(padded, weight):
    length_here = padded.shape[1] - 2
    result = jnp.dot(padded[:, 0:length_here], weight[0], preferred_element_type=jnp.float32)
    result = result + jnp.dot(
        padded[:, 1 : length_here + 1], weight[1], preferred_element_type=jnp.float32
    )
    return result + jnp.dot(padded[:, 2:], weight[2], preferred_element_type=jnp.float32)


def conv_weight_grad(padded, grad_low):
    length_here = grad_low.shape[1]
    return jnp.stack(
        [
            jnp.einsum(
                "utc,utd->cd",
                padded[:, tap_index : tap_index + length_here],
                grad_low,
                preferred_element_type=jnp.float32,
            )
            for tap_index in range(3)
        ]
    )


def conv_input_grad(grad_low, weight):
    padded = rim_pad(grad_low)
    length_here = grad_low.shape[1]
    result = jnp.einsum("utd,cd->utc", padded[:, 2:], weight[0], preferred_element_type=jnp.float32)
    result = result + jnp.einsum(
        "utd,cd->utc", padded[:, 1 : length_here + 1], weight[1], preferred_element_type=jnp.float32
    )
    return result + jnp.einsum(
        "utd,cd->utc", padded[:, 0:length_here], weight[2], preferred_element_type=jnp.float32
    )


def norm_forward(signal, frame_mask, valid_count, gain_row, shift_row):
    width = C // GROUPS
    shape_now = signal.shape
    grouped = (signal * frame_mask[:, :, None]).reshape(shape_now[0], shape_now[1], GROUPS, width)
    total = jnp.sum(grouped, axis=(1, 3))
    squares = jnp.sum(grouped * grouped, axis=(1, 3))
    number = valid_count[:, None] * width
    mean_now = total / number
    inv_std = lax.rsqrt(squares / number - mean_now * mean_now + EPSILON)
    mean_wide = jnp.repeat(mean_now, width, axis=1)[:, None, :]
    inv_wide = jnp.repeat(inv_std, width, axis=1)[:, None, :]
    normed = (signal - mean_wide) * inv_wide
    return (normed * gain_row + shift_row, normed, inv_wide)


def norm_backward(grad_out, normed, inv_wide, frame_mask, valid_count, gain_row):
    width = C // GROUPS
    shape_now = grad_out.shape
    grad_norm = grad_out * gain_row
    first_sum = jnp.sum(grad_norm.reshape(shape_now[0], shape_now[1], GROUPS, width), axis=(1, 3))
    second_sum = jnp.sum(
        (grad_norm * normed).reshape(shape_now[0], shape_now[1], GROUPS, width), axis=(1, 3)
    )
    number = valid_count[:, None] * width
    first_wide = jnp.repeat(first_sum / number, width, axis=1)[:, None, :]
    second_wide = jnp.repeat(second_sum / number, width, axis=1)[:, None, :]
    grad_signal = inv_wide * (
        grad_norm - frame_mask[:, :, None] * (first_wide + normed * second_wide)
    )
    grad_gain = jnp.sum(grad_out * normed, axis=(0, 1))
    grad_shift = jnp.sum(grad_out, axis=(0, 1))
    return (grad_signal, grad_gain, grad_shift)


def update(master, moment, average, grad, rate):
    moment_new = MOMENTUM * moment + grad
    master_new = master - rate * (grad + MOMENTUM * moment_new)
    average_new = AVERAGE_DECAY * average + (1.0 - AVERAGE_DECAY) * master_new
    return (master_new, moment_new, average_new, master_new.astype(jnp.bfloat16))


def pad_width(length_now):
    return -(-length_now // 1024) * 1024


def gather_weights(res_master, tf_master):
    res_len, tf_len = res_master.shape[0], tf_master.shape[0]
    width = pad_width(res_len + tf_len)
    flat = jnp.concatenate([res_master, tf_master]).astype(jnp.bfloat16)
    flat = jnp.pad(flat, (0, width - res_len - tf_len))
    whole = lax.all_gather(flat, ("dp", "seq"), axis=0, tiled=True).reshape(-1, width)
    return (whole[:, :res_len].reshape(-1), whole[:, res_len : res_len + tf_len].reshape(-1))


def scatter_grads(res_grad, tf_grad):
    count = lax.axis_size("dp") * lax.axis_size("seq")
    res_grad, tf_grad = res_grad.reshape(count, -1), tf_grad.reshape(count, -1)
    res_len, tf_len = res_grad.shape[1], tf_grad.shape[1]
    width = pad_width(res_len + tf_len)
    rows = jnp.concatenate(
        [res_grad, tf_grad, jnp.zeros((count, width - res_len - tf_len), jnp.float32)], axis=1
    )
    share = lax.psum_scatter(rows.reshape(-1), ("dp", "seq"), scatter_dimension=0, tiled=True)
    return (share[:res_len], share[res_len : res_len + tf_len])


def to_utts(cells):
    return lax.all_to_all(cells, "seq", split_axis=0, concat_axis=1, tiled=True)


def to_frames(cells):
    low = cells.astype(jnp.bfloat16)
    return lax.all_to_all(low, "seq", split_axis=1, concat_axis=0, tiled=True).astype(jnp.float32)


def per_device(
    inputs,
    encoded,
    durations,
    lengths,
    time_embed,
    cotangent,
    res_master,
    res_moment,
    res_average,
    tf_master,
    tf_moment,
    tf_average,
):
    utts_here, local_len, _ = inputs.shape
    seq_size = lax.axis_size("seq")
    key_total = local_len * seq_size
    utt_count = utts_here // seq_size
    inner = HEADS * HD
    seq_index = lax.axis_index("seq")
    frame_ids = seq_index * local_len + jnp.arange(local_len, dtype=jnp.int32)
    local_mask = (frame_ids[None, :] < lengths[:, None]).astype(jnp.float32)[:, :, None]
    boundary = jnp.cumsum(durations, axis=1)
    phone = jnp.sum((boundary[:, None, :] <= frame_ids[None, :, None]).astype(jnp.int32), axis=2)
    phone = jnp.minimum(phone, durations.shape[1] - 1)
    start_state = inputs + jax.vmap(take_rows)(encoded, phone)
    res_whole, tf_whole = gather_weights(res_master, tf_master)
    masked_in = to_utts((start_state * local_mask).astype(jnp.bfloat16))
    grad_ff = to_utts((cotangent * local_mask).astype(jnp.bfloat16))
    lengths = lax.dynamic_slice_in_dim(lengths, seq_index * utt_count, utt_count)
    time_embed = lax.dynamic_slice_in_dim(time_embed, seq_index * utt_count, utt_count)
    frame_mask = (jnp.arange(key_total)[None, :] < lengths[:, None]).astype(jnp.float32)
    wide_mask = frame_mask[:, :, None]
    key_mask = jnp.arange(key_total, dtype=jnp.int32)[None, :] < lengths[:, None]
    valid_count = lengths.astype(jnp.float32)
    conv_one, conv_two, res_weight, time_weight, res_rows = unpack_res(res_whole)
    res_small = res_rows.astype(jnp.float32)
    padded_one = rim_pad(masked_in)
    z_one = conv_apply(padded_one, conv_one) + res_small[0]
    norm_one, normed_one, inv_one = norm_forward(
        z_one, frame_mask, valid_count, res_small[1], res_small[2]
    )
    act_one = mish_fn(norm_one) * wide_mask
    time_act = mish_fn(time_embed).astype(jnp.bfloat16)
    time_proj = jnp.dot(time_act, time_weight, preferred_element_type=jnp.float32) + res_small[7]
    masked_two = ((act_one + time_proj[:, None, :]) * wide_mask).astype(jnp.bfloat16)
    padded_two = rim_pad(masked_two)
    z_two = conv_apply(padded_two, conv_two) + res_small[3]
    norm_two, normed_two, inv_two = norm_forward(
        z_two, frame_mask, valid_count, res_small[4], res_small[5]
    )
    act_two = mish_fn(norm_two) * wide_mask
    skip_out = jnp.dot(masked_in, res_weight, preferred_element_type=jnp.float32) + res_small[6]
    block_out = act_two + skip_out
    qkv_weight, out_weight, up_weight, down_weight, tf_rows, wide_rows = unpack_tf(tf_whole)
    tf_small = tf_rows.astype(jnp.float32)
    wide_small = wide_rows.astype(jnp.float32)
    attn_in = layer_norm(block_out, tf_small[0], tf_small[1]).astype(jnp.bfloat16)
    qkv_all = jnp.dot(attn_in, qkv_weight, preferred_element_type=jnp.float32).astype(jnp.bfloat16)
    queries = qkv_all[:, :, :inner].reshape(utt_count, key_total, HEADS, HD)
    kv_whole = qkv_all[:, :, inner:]
    keys = kv_whole[:, :, :inner].reshape(utt_count, key_total, HEADS, HD)
    values = kv_whole[:, :, inner:].reshape(utt_count, key_total, HEADS, HD)
    scores = (
        jnp.einsum("uqhd,ukhd->uhqk", queries, keys, preferred_element_type=jnp.float32)
        * SCORE_SCALE
    )
    scores = jnp.where(key_mask[:, None, None, :], scores, MASK_FILL)
    top_score = jnp.max(scores, axis=-1, keepdims=True)
    expo = jnp.exp(scores - top_score)
    row_total = jnp.sum(expo, axis=-1, keepdims=True)
    log_total = top_score + jnp.log(row_total)
    probs_low = (expo / row_total).astype(jnp.bfloat16)
    attn_vals = jnp.einsum("uhqk,ukhd->uqhd", probs_low, values, preferred_element_type=jnp.float32)
    attn_vals = attn_vals.reshape(utt_count, key_total, inner).astype(jnp.bfloat16)
    attn_out = jnp.dot(attn_vals, out_weight, preferred_element_type=jnp.float32) + tf_small[2]
    mid_state = block_out + attn_out
    ff_in = layer_norm(mid_state, tf_small[3], tf_small[4]).astype(jnp.bfloat16)
    up_out = jnp.dot(ff_in, up_weight, preferred_element_type=jnp.float32) + wide_small[0]
    snake_out = snake_fn(up_out, wide_small[1], wide_small[2]).astype(jnp.bfloat16)
    ff_out = jnp.dot(snake_out, down_weight, preferred_element_type=jnp.float32) + tf_small[5]
    final = (mid_state + ff_out) * wide_mask
    grad_final = grad_ff.astype(jnp.float32)
    grad_down_w = jnp.einsum("utf,utc->fc", snake_out, grad_ff, preferred_element_type=jnp.float32)
    grad_down_b = jnp.sum(grad_ff, axis=(0, 1), dtype=jnp.float32)
    grad_snake = jnp.einsum("utc,fc->utf", grad_ff, down_weight, preferred_element_type=jnp.float32)
    snake_value, snake_pull = jax.vjp(snake_fn, up_out, wide_small[1], wide_small[2])
    grad_up_f, grad_alpha, grad_beta = snake_pull(grad_snake)
    grad_up = grad_up_f.astype(jnp.bfloat16)
    grad_up_w = jnp.einsum("utc,utf->cf", ff_in, grad_up, preferred_element_type=jnp.float32)
    grad_up_b = jnp.sum(grad_up, axis=(0, 1), dtype=jnp.float32)
    grad_ff_in = jnp.einsum("utf,cf->utc", grad_up, up_weight, preferred_element_type=jnp.float32)
    norm_value, norm_pull = jax.vjp(layer_norm, mid_state, tf_small[3], tf_small[4])
    grad_mid_ln, grad_ln3_g, grad_ln3_b = norm_pull(grad_ff_in)
    grad_mid = grad_final + grad_mid_ln
    grad_attn = grad_mid.astype(jnp.bfloat16)
    grad_out_w = jnp.einsum("uti,utc->ic", attn_vals, grad_attn, preferred_element_type=jnp.float32)
    grad_out_b = jnp.sum(grad_attn, axis=(0, 1), dtype=jnp.float32)
    grad_vals = jnp.einsum("utc,ic->uti", grad_attn, out_weight, preferred_element_type=jnp.float32)
    grad_vals = grad_vals.astype(jnp.bfloat16).reshape(utt_count, key_total, HEADS, HD)
    scores = (
        jnp.einsum("uqhd,ukhd->uhqk", queries, keys, preferred_element_type=jnp.float32)
        * SCORE_SCALE
    )
    scores = jnp.where(key_mask[:, None, None, :], scores, MASK_FILL)
    probs = jnp.exp(scores - log_total)
    probs_low = probs.astype(jnp.bfloat16)
    grad_probs = jnp.einsum(
        "uqhd,ukhd->uhqk", grad_vals, values, preferred_element_type=jnp.float32
    )
    row_dot = jnp.sum(probs * grad_probs, axis=-1, keepdims=True)
    grad_scores = (probs * (grad_probs - row_dot)).astype(jnp.bfloat16)
    grad_query = (
        jnp.einsum("uhqk,ukhd->uqhd", grad_scores, keys, preferred_element_type=jnp.float32)
        * SCORE_SCALE
    )
    grad_key = (
        jnp.einsum("uhqk,uqhd->ukhd", grad_scores, queries, preferred_element_type=jnp.float32)
        * SCORE_SCALE
    )
    grad_value = jnp.einsum(
        "uhqk,uqhd->ukhd", probs_low, grad_vals, preferred_element_type=jnp.float32
    )
    grad_kv = jnp.concatenate(
        [
            grad_key.reshape(utt_count, key_total, inner),
            grad_value.reshape(utt_count, key_total, inner),
        ],
        axis=2,
    )
    grad_kv_local = grad_kv
    grad_qkv = jnp.concatenate(
        [grad_query.reshape(utt_count, key_total, inner), grad_kv_local], axis=2
    ).astype(jnp.bfloat16)
    grad_qkv_w = jnp.einsum("utc,utd->cd", attn_in, grad_qkv, preferred_element_type=jnp.float32)
    grad_attn_in = jnp.einsum(
        "utd,cd->utc", grad_qkv, qkv_weight, preferred_element_type=jnp.float32
    )
    block_value, block_pull = jax.vjp(layer_norm, block_out, tf_small[0], tf_small[1])
    grad_block_ln, grad_ln1_g, grad_ln1_b = block_pull(grad_attn_in)
    grad_block = grad_mid + grad_block_ln
    tf_grad_local = jnp.concatenate(
        [
            grad_qkv_w.reshape(-1),
            grad_out_w.reshape(-1),
            grad_up_w.reshape(-1),
            grad_down_w.reshape(-1),
            jnp.stack(
                [grad_ln1_g, grad_ln1_b, grad_out_b, grad_ln3_g, grad_ln3_b, grad_down_b]
            ).reshape(-1),
            jnp.stack([grad_up_b, grad_alpha, grad_beta]).reshape(-1),
        ]
    )
    grad_skip = grad_block.astype(jnp.bfloat16)
    grad_res_w = jnp.einsum("utc,utd->cd", masked_in, grad_skip, preferred_element_type=jnp.float32)
    grad_res_b = jnp.sum(grad_skip, axis=(0, 1), dtype=jnp.float32)
    grad_masked_in = jnp.einsum(
        "utd,cd->utc", grad_skip, res_weight, preferred_element_type=jnp.float32
    )
    mish_two, mish_pull_two = jax.vjp(mish_fn, norm_two)
    (grad_norm_two,) = mish_pull_two(grad_block * wide_mask)
    grad_z_two, grad_gn2_g, grad_gn2_b = norm_backward(
        grad_norm_two, normed_two, inv_two, frame_mask, valid_count, res_small[4]
    )
    grad_z_two = grad_z_two.astype(jnp.bfloat16)
    grad_conv_two = conv_weight_grad(padded_two, grad_z_two)
    grad_conv_two_b = jnp.sum(grad_z_two, axis=(0, 1), dtype=jnp.float32)
    grad_hidden = conv_input_grad(grad_z_two, conv_two) * wide_mask
    grad_time_proj = jnp.sum(grad_hidden, axis=1)
    grad_time_w = jnp.dot(
        time_act.astype(jnp.float32).T, grad_time_proj, precision=lax.Precision.HIGHEST
    )
    grad_time_b = jnp.sum(grad_time_proj, axis=0)
    mish_one, mish_pull_one = jax.vjp(mish_fn, norm_one)
    (grad_norm_one,) = mish_pull_one(grad_hidden * wide_mask)
    grad_z_one, grad_gn1_g, grad_gn1_b = norm_backward(
        grad_norm_one, normed_one, inv_one, frame_mask, valid_count, res_small[1]
    )
    grad_z_one = grad_z_one.astype(jnp.bfloat16)
    grad_conv_one = conv_weight_grad(padded_one, grad_z_one)
    grad_conv_one_b = jnp.sum(grad_z_one, axis=(0, 1), dtype=jnp.float32)
    grad_masked_in = grad_masked_in + conv_input_grad(grad_z_one, conv_one)
    grad_inputs = grad_masked_in * wide_mask
    res_grad_local = jnp.concatenate(
        [
            grad_conv_one.reshape(-1),
            grad_conv_two.reshape(-1),
            grad_res_w.reshape(-1),
            grad_time_w.reshape(-1),
            jnp.stack(
                [
                    grad_conv_one_b,
                    grad_gn1_g,
                    grad_gn1_b,
                    grad_conv_two_b,
                    grad_gn2_g,
                    grad_gn2_b,
                    grad_res_b,
                    grad_time_b,
                ]
            ).reshape(-1),
        ]
    )
    res_share, tf_share = scatter_grads(res_grad_local, tf_grad_local)
    tokens_total = utts_here * key_total * lax.axis_size("dp")
    rate = LEARN_BASE / math.sqrt(tokens_total)
    res_new, res_moment_new, res_average_new, res_low = update(
        res_master, res_moment, res_average, res_share, rate
    )
    tf_new, tf_moment_new, tf_average_new, tf_low = update(
        tf_master, tf_moment, tf_average, tf_share, rate
    )
    return (
        to_frames(final),
        to_frames(grad_inputs),
        res_share,
        tf_share,
        res_new,
        tf_new,
        res_moment_new,
        tf_moment_new,
        res_average_new,
        tf_average_new,
        res_low,
        tf_low,
    )


def solution(mesh):
    placed = (
        P("dp", "seq", None),
        P("dp", None, None),
        P("dp", None),
        P("dp"),
        P("dp", None),
        P("dp", "seq", None),
        P(("dp", "seq")),
        P(("dp", "seq")),
        P(("dp", "seq")),
        P(("dp", "seq")),
        P(("dp", "seq")),
        P(("dp", "seq")),
    )
    return jax.shard_map(
        per_device,
        mesh=mesh,
        in_specs=placed,
        out_specs=(
            P("dp", "seq", None),
            P("dp", "seq", None),
            P(("dp", "seq")),
            P(("dp", "seq")),
            P(("dp", "seq")),
            P(("dp", "seq")),
            P(("dp", "seq")),
            P(("dp", "seq")),
            P(("dp", "seq")),
            P(("dp", "seq")),
            P(("dp", "seq")),
            P(("dp", "seq")),
        ),
        check_vma=False,
    )
```

```python
import functools
import math

import jax
import jax.numpy as jnp
from jax import lax
from jax.experimental import pallas as pl
from jax.experimental.pallas import tpu as pltpu
from jax.sharding import PartitionSpec as P

C = 256
GROUPS = 8
TE = 1024
HEADS = 2
HD = 64
F = 1024


EPSILON = 1e-05
SCORE_SCALE = 0.125
MOMENTUM = 0.9
AVERAGE_DECAY = 0.99
LEARN_BASE = 0.015
MASK_FILL = -1e30


def soft_plus(signal):
    return jnp.log1p(jnp.exp(-jnp.abs(signal))) + jnp.maximum(signal, 0.0)


def mish_fn(signal):
    return signal * jnp.tanh(soft_plus(signal))


def snake_fn(signal, alpha_row, beta_row):
    return signal + jnp.sin(signal * jnp.exp(alpha_row)) ** 2 / (jnp.exp(beta_row) + 1e-09)


def layer_norm(signal, gain_row, shift_row):
    center = signal - jnp.mean(signal, axis=-1, keepdims=True)
    spread = jnp.mean(center * center, axis=-1, keepdims=True)
    return center * lax.rsqrt(spread + EPSILON) * gain_row + shift_row


def take_rows(phone_table, phone_rows):
    return phone_table[phone_rows]


def rim_pad(signal):
    return jnp.pad(signal, ((0, 0), (1, 1), (0, 0)))


def conv_apply(padded, weight):
    length_here = padded.shape[1] - 2
    result = jnp.dot(padded[:, 0:length_here], weight[0], preferred_element_type=jnp.float32)
    result = result + jnp.dot(
        padded[:, 1 : length_here + 1], weight[1], preferred_element_type=jnp.float32
    )
    return result + jnp.dot(padded[:, 2:], weight[2], preferred_element_type=jnp.float32)


def conv_weight_grad(padded, grad_low):
    length_here = grad_low.shape[1]
    return jnp.stack(
        [
            jnp.einsum(
                "utc,utd->cd",
                padded[:, tap_index : tap_index + length_here],
                grad_low,
                preferred_element_type=jnp.float32,
            )
            for tap_index in range(3)
        ]
    )


def conv_input_grad(grad_low, weight):
    padded = rim_pad(grad_low)
    length_here = grad_low.shape[1]
    result = jnp.einsum("utd,cd->utc", padded[:, 2:], weight[0], preferred_element_type=jnp.float32)
    result = result + jnp.einsum(
        "utd,cd->utc", padded[:, 1 : length_here + 1], weight[1], preferred_element_type=jnp.float32
    )
    return result + jnp.einsum(
        "utd,cd->utc", padded[:, 0:length_here], weight[2], preferred_element_type=jnp.float32
    )


def norm_forward(signal, frame_mask, valid_count, gain_row, shift_row):
    width = C // GROUPS
    shape_now = signal.shape
    grouped = (signal * frame_mask[:, :, None]).reshape(shape_now[0], shape_now[1], GROUPS, width)
    total = jnp.sum(grouped, axis=(1, 3))
    squares = jnp.sum(grouped * grouped, axis=(1, 3))
    number = valid_count[:, None] * width
    mean_now = total / number
    inv_std = lax.rsqrt(squares / number - mean_now * mean_now + EPSILON)
    mean_wide = jnp.repeat(mean_now, width, axis=1)[:, None, :]
    inv_wide = jnp.repeat(inv_std, width, axis=1)[:, None, :]
    normed = (signal - mean_wide) * inv_wide
    return (normed * gain_row + shift_row, normed, inv_wide)


def norm_backward(grad_out, normed, inv_wide, frame_mask, valid_count, gain_row):
    width = C // GROUPS
    shape_now = grad_out.shape
    grad_norm = grad_out * gain_row
    first_sum = jnp.sum(grad_norm.reshape(shape_now[0], shape_now[1], GROUPS, width), axis=(1, 3))
    second_sum = jnp.sum(
        (grad_norm * normed).reshape(shape_now[0], shape_now[1], GROUPS, width), axis=(1, 3)
    )
    number = valid_count[:, None] * width
    first_wide = jnp.repeat(first_sum / number, width, axis=1)[:, None, :]
    second_wide = jnp.repeat(second_sum / number, width, axis=1)[:, None, :]
    grad_signal = inv_wide * (
        grad_norm - frame_mask[:, :, None] * (first_wide + normed * second_wide)
    )
    grad_gain = jnp.sum(grad_out * normed, axis=(0, 1))
    grad_shift = jnp.sum(grad_out, axis=(0, 1))
    return (grad_signal, grad_gain, grad_shift)


def update(master, moment, average, grad, rate):
    moment_new = MOMENTUM * moment + grad
    master_new = master - rate * (grad + MOMENTUM * moment_new)
    average_new = AVERAGE_DECAY * average + (1.0 - AVERAGE_DECAY) * master_new
    return (master_new, moment_new, average_new, master_new.astype(jnp.bfloat16))


def axis_bits(mesh_sizes):
    bits = []
    for name, size in mesh_sizes:
        weight = size // 2
        while weight >= 1:
            bits.append((name, weight))
            weight //= 2
    return bits


def part_orders(mesh_sizes):
    first = axis_bits(mesh_sizes)
    second = list(first)
    if len(second) >= 3:
        second[-3], second[-2] = second[-2], second[-3]
    return (first, second)


def owner_place(order, mesh_sizes, owner):
    strides, stride = {}, 1
    for name, size in reversed(mesh_sizes):
        strides[name] = (stride, size)
        stride *= size
    place = 0
    for step, (name, weight) in enumerate(order):
        base, size = strides[name]
        place += ((owner // base) % size // weight % 2) << step
    return place


def window_rows(length_now, count):
    most = max((i * length_now) % 128 + length_now for i in range(count))
    return -(-most // (128 * 16)) * 16


def bit_of(name, weight):
    return (lax.axis_index(name) // weight) % 2


def partner_of(name, weight):
    return {name: lax.axis_index(name) + (1 - 2 * bit_of(name, weight)) * weight}


def greet(orders):
    barrier = pltpu.get_barrier_semaphore()
    for name, weight in orders[0]:
        pl.semaphore_signal(
            barrier,
            inc=1,
            device_id=partner_of(name, weight),
            device_id_type=pl.DeviceIdType.MESH,
        )
    pl.semaphore_wait(barrier, len(orders[0]))


def gather_kernel(orders, in_a, in_b, out_a, out_b, local_sem, send_sem, recv_sem):
    ins, outs = (in_a, in_b), (out_a, out_b)
    stage_count = len(orders[0])
    offsets = []
    for part in range(2):
        offset = 0
        for step, (name, weight) in enumerate(orders[part]):
            offset = offset + bit_of(name, weight) * (1 << step)
        offsets.append(offset)
    locals_now = [
        pltpu.make_async_copy(ins[part], outs[part].at[offsets[part]], local_sem.at[part])
        for part in range(2)
    ]
    for copy in locals_now:
        copy.start()
    greet(orders)
    for copy in locals_now:
        copy.wait()
    copies = []
    for step in range(stage_count):
        held = 1 << step
        for part in range(2):
            name, weight = orders[part][step]
            start = offsets[part]
            block = outs[part].at[pl.ds(start, held)]
            copy = pltpu.make_async_remote_copy(
                src_ref=block,
                dst_ref=block,
                send_sem=send_sem.at[part, step],
                recv_sem=recv_sem.at[part, step],
                device_id=partner_of(name, weight),
                device_id_type=pl.DeviceIdType.MESH,
            )
            copy.start()
            copies.append(copy)
        for part in range(2):
            copies[2 * step + part].wait_recv()
            name, weight = orders[part][step]
            offsets[part] = offsets[part] - bit_of(name, weight) * held
    for copy in copies:
        copy.wait_send()


def gather_windows(orders, win_a, win_b):
    count = 1 << len(orders[0])
    stages = len(orders[0])
    return pl.pallas_call(
        functools.partial(gather_kernel, orders),
        out_shape=(
            jax.ShapeDtypeStruct((count,) + win_a.shape, win_a.dtype),
            jax.ShapeDtypeStruct((count,) + win_b.shape, win_b.dtype),
        ),
        in_specs=[pl.BlockSpec(memory_space=pltpu.VMEM)] * 2,
        out_specs=[pl.BlockSpec(memory_space=pltpu.VMEM)] * 2,
        scratch_shapes=[
            pltpu.SemaphoreType.DMA((2,)),
            pltpu.SemaphoreType.DMA((2, stages)),
            pltpu.SemaphoreType.DMA((2, stages)),
        ],
        compiler_params=pltpu.CompilerParams(
            collective_id=0, has_side_effects=True, vmem_limit_bytes=32 * 1024 * 1024
        ),
    )(win_a, win_b)


def reduce_kernel(orders, in_a, in_b, out_a, out_b, land_a, land_b, send_sem, recv_sem):
    ins, outs, lands = (in_a, in_b), (out_a, out_b), (land_a, land_b)
    stage_count = len(orders[0])
    greet(orders)
    copies = []

    def source(part, step, keep):
        name, weight = orders[part][stage_count - 1 - step]
        held = 1 << (stage_count - 1 - step)
        side = bit_of(name, weight)
        side = side if keep else 1 - side
        if step == 0:
            return ins[part].at[pl.ds(side * held, held)]
        base = (1 << stage_count) - (1 << (stage_count - step + 1))
        return lands[part].at[pl.ds(base + side * held, held)]

    for step in range(stage_count):
        held = 1 << (stage_count - 1 - step)
        base = (1 << stage_count) - (1 << (stage_count - step))
        for part in range(2):
            name, weight = orders[part][stage_count - 1 - step]
            copy = pltpu.make_async_remote_copy(
                src_ref=source(part, step, False),
                dst_ref=lands[part].at[pl.ds(base, held)],
                send_sem=send_sem.at[part, step],
                recv_sem=recv_sem.at[part, step],
                device_id=partner_of(name, weight),
                device_id_type=pl.DeviceIdType.MESH,
            )
            copy.start()
            copies.append(copy)
        for part in range(2):
            copies[2 * step + part].wait_recv()
            mine = source(part, step, True)
            if step == stage_count - 1:
                outs[part][...] = mine[0].astype(jnp.float32) + lands[part][base].astype(
                    jnp.float32
                )
            else:

                def add_one(index, carry, mine=mine, part=part, base=base):
                    land = lands[part].at[base + index]
                    total = mine[index].astype(jnp.float32) + land[...].astype(jnp.float32)
                    land[...] = total.astype(land.dtype)
                    return carry

                lax.fori_loop(0, held, add_one, 0)
    for copy in copies:
        copy.wait_send()


def reduce_windows(orders, rows_a, rows_b):
    count = 1 << len(orders[0])
    stages = len(orders[0])
    return pl.pallas_call(
        functools.partial(reduce_kernel, orders),
        out_shape=(
            jax.ShapeDtypeStruct(rows_a.shape[1:], jnp.float32),
            jax.ShapeDtypeStruct(rows_b.shape[1:], jnp.float32),
        ),
        in_specs=[pl.BlockSpec(memory_space=pltpu.VMEM)] * 2,
        out_specs=[pl.BlockSpec(memory_space=pltpu.VMEM)] * 2,
        scratch_shapes=[
            pltpu.VMEM((count - 1,) + rows_a.shape[1:], rows_a.dtype),
            pltpu.VMEM((count - 1,) + rows_b.shape[1:], rows_b.dtype),
            pltpu.SemaphoreType.DMA((2, stages)),
            pltpu.SemaphoreType.DMA((2, stages)),
        ],
        compiler_params=pltpu.CompilerParams(
            collective_id=1, has_side_effects=True, vmem_limit_bytes=32 * 1024 * 1024
        ),
    )(rows_a, rows_b)


RES_SQUARES = 7 * C * C
RES_ROWS = (RES_SQUARES + TE * C + 8 * C) // 128
INNER = HEADS * HD
TF_SIZES = (3 * C * INNER, INNER * C, C * F, F * C, 6 * C, 3 * F)
TF_ROWS = sum(TF_SIZES) // 128


def place_maps(orders, mesh_sizes):
    count = 1 << len(orders[0])
    return [[owner_place(orders[part], mesh_sizes, i) for i in range(count)] for part in range(2)]


def matrix_views():
    views = []
    row = 0
    for rows, width in ((6 * C, C), (C, C), (TE, C), (8, C)):
        views.append((0, row, rows, width))
        row += rows * width // 128
    row = 0
    for rows, width in ((C, 3 * INNER), (INNER, C), (C, F), (F, C), (6, C), (3, F)):
        views.append((1, row, rows, width))
        row += rows * width // 128
    return views


def assemble_kernel(places, lengths_now, in_a, in_b, *refs):
    outs, flats = refs[:10], refs[10:12]
    count = len(places[0])
    for part, ref in enumerate((in_a, in_b)):
        flat = flats[part]
        for i in range(count):
            start, lead = divmod(i * lengths_now[part], 128)
            rows = -(-(lead + lengths_now[part]) // 128)
            if lead:
                edge = flat[start : start + 1, :]
            flat[start : start + rows, :] = ref[places[part][i]].astype(jnp.float32)[:rows]
            if lead:
                flat[start : start + 1, :] = flat[start : start + 1, :] + edge
    for out, (part, row, rows, width) in zip(outs, matrix_views()):
        stride = width // 128
        for lane in range(stride):
            piece = flats[part][pl.ds(row + lane, rows, stride=stride), :]
            out[:, lane * 128 : (lane + 1) * 128] = piece.astype(out.dtype)


def assemble_weights(places, lengths_now, win_a, win_b):
    shapes = []
    for index, (part, row, rows, width) in enumerate(matrix_views()):
        kind = jnp.float32 if index in (3, 8, 9) else jnp.bfloat16
        shapes.append(jax.ShapeDtypeStruct((rows, width), kind))
    return pl.pallas_call(
        functools.partial(assemble_kernel, places, lengths_now),
        out_shape=shapes,
        in_specs=[pl.BlockSpec(memory_space=pltpu.VMEM)] * 2,
        out_specs=[pl.BlockSpec(memory_space=pltpu.VMEM)] * 10,
        scratch_shapes=[
            pltpu.VMEM((RES_ROWS + 8, 128), jnp.float32),
            pltpu.VMEM((TF_ROWS + 12, 128), jnp.float32),
        ],
        compiler_params=pltpu.CompilerParams(vmem_limit_bytes=32 * 1024 * 1024),
    )(win_a, win_b)


def cut_kernel(places, lengths_now, *refs):
    ins, outs, flats = refs[:10], refs[10:12], refs[12:14]
    count = len(places[0])
    for ref, (part, row, rows, width) in zip(ins, matrix_views()):
        stride = width // 128
        for lane in range(stride):
            flats[part][pl.ds(row + lane, rows, stride=stride), :] = ref[
                :, lane * 128 : (lane + 1) * 128
            ]
    for part in range(2):
        for i in range(count):
            start, lead = divmod(i * lengths_now[part], 128)
            rows = outs[part].shape[1]
            outs[part][places[part][i]] = flats[part][start : start + rows, :].astype(
                outs[part].dtype
            )


def cut_grads(places, lengths_now, window_sizes, grads):
    count = len(places[0])
    return pl.pallas_call(
        functools.partial(cut_kernel, places, lengths_now),
        out_shape=[
            jax.ShapeDtypeStruct((count, rows, 128), jnp.bfloat16) for rows in window_sizes
        ],
        in_specs=[pl.BlockSpec(memory_space=pltpu.VMEM)] * 10,
        out_specs=[pl.BlockSpec(memory_space=pltpu.VMEM)] * 2,
        scratch_shapes=[
            pltpu.VMEM((RES_ROWS + 24, 128), jnp.float32),
            pltpu.VMEM((TF_ROWS + 28, 128), jnp.float32),
        ],
        compiler_params=pltpu.CompilerParams(vmem_limit_bytes=40 * 1024 * 1024),
    )(*grads)


def flat_index(mesh_sizes):
    index = 0
    for name, size in mesh_sizes:
        index = index * size + lax.axis_index(name)
    return index


def to_window(master, rows, owner):
    lead = (owner * master.shape[0]) % 128
    window = jnp.zeros((rows * 128,), jnp.bfloat16)
    return lax.dynamic_update_slice(window, master.astype(jnp.bfloat16), (lead,)).reshape(rows, 128)


def from_window(window, length_now, owner):
    lead = (owner * length_now) % 128
    return lax.dynamic_slice(window.reshape(-1), (lead,), (length_now,))


def to_utts(cells):
    return lax.all_to_all(cells, "seq", split_axis=0, concat_axis=1, tiled=True)


def to_frames(cells):
    low = cells.astype(jnp.bfloat16)
    return lax.all_to_all(low, "seq", split_axis=1, concat_axis=0, tiled=True).astype(jnp.float32)


def per_device(
    inputs,
    encoded,
    durations,
    lengths,
    time_embed,
    cotangent,
    res_master,
    res_moment,
    res_average,
    tf_master,
    tf_moment,
    tf_average,
):
    utts_here, local_len, _ = inputs.shape
    seq_size = lax.axis_size("seq")
    key_total = local_len * seq_size
    utt_count = utts_here // seq_size
    inner = HEADS * HD
    seq_index = lax.axis_index("seq")
    frame_ids = seq_index * local_len + jnp.arange(local_len, dtype=jnp.int32)
    local_mask = (frame_ids[None, :] < lengths[:, None]).astype(jnp.float32)[:, :, None]
    boundary = jnp.cumsum(durations, axis=1)
    phone = jnp.sum((boundary[:, None, :] <= frame_ids[None, :, None]).astype(jnp.int32), axis=2)
    phone = jnp.minimum(phone, durations.shape[1] - 1)
    start_state = inputs + jax.vmap(take_rows)(encoded, phone)
    mesh_sizes = [(name, lax.axis_size(name)) for name in ("dp", "seq")]
    orders = part_orders(mesh_sizes)
    places = place_maps(orders, mesh_sizes)
    owner = flat_index(mesh_sizes)
    shard_lengths = (res_master.shape[0], tf_master.shape[0])
    window_sizes = [window_rows(size, len(places[0])) for size in shard_lengths]
    gathered = gather_windows(
        orders,
        to_window(res_master, window_sizes[0], owner),
        to_window(tf_master, window_sizes[1], owner),
    )
    (
        convs,
        res_weight,
        time_weight,
        res_small,
        qkv_weight,
        out_weight,
        up_weight,
        down_weight,
        tf_small,
        wide_small,
    ) = assemble_weights(places, shard_lengths, *gathered)
    conv_one = convs[: 3 * C].reshape(3, C, C)
    conv_two = convs[3 * C :].reshape(3, C, C)
    masked_in = to_utts((start_state * local_mask).astype(jnp.bfloat16))
    grad_ff = to_utts((cotangent * local_mask).astype(jnp.bfloat16))
    lengths = lax.dynamic_slice_in_dim(lengths, seq_index * utt_count, utt_count)
    time_embed = lax.dynamic_slice_in_dim(time_embed, seq_index * utt_count, utt_count)
    frame_mask = (jnp.arange(key_total)[None, :] < lengths[:, None]).astype(jnp.float32)
    wide_mask = frame_mask[:, :, None]
    key_mask = jnp.arange(key_total, dtype=jnp.int32)[None, :] < lengths[:, None]
    valid_count = lengths.astype(jnp.float32)
    padded_one = rim_pad(masked_in)
    z_one = conv_apply(padded_one, conv_one) + res_small[0]
    norm_one, normed_one, inv_one = norm_forward(
        z_one, frame_mask, valid_count, res_small[1], res_small[2]
    )
    act_one = mish_fn(norm_one) * wide_mask
    time_act = mish_fn(time_embed).astype(jnp.bfloat16)
    time_proj = jnp.dot(time_act, time_weight, preferred_element_type=jnp.float32) + res_small[7]
    masked_two = ((act_one + time_proj[:, None, :]) * wide_mask).astype(jnp.bfloat16)
    padded_two = rim_pad(masked_two)
    z_two = conv_apply(padded_two, conv_two) + res_small[3]
    norm_two, normed_two, inv_two = norm_forward(
        z_two, frame_mask, valid_count, res_small[4], res_small[5]
    )
    act_two = mish_fn(norm_two) * wide_mask
    skip_out = jnp.dot(masked_in, res_weight, preferred_element_type=jnp.float32) + res_small[6]
    block_out = act_two + skip_out
    attn_in = layer_norm(block_out, tf_small[0], tf_small[1]).astype(jnp.bfloat16)
    qkv_all = jnp.dot(attn_in, qkv_weight, preferred_element_type=jnp.float32).astype(jnp.bfloat16)
    queries = qkv_all[:, :, :inner].reshape(utt_count, key_total, HEADS, HD)
    kv_whole = qkv_all[:, :, inner:]
    keys = kv_whole[:, :, :inner].reshape(utt_count, key_total, HEADS, HD)
    values = kv_whole[:, :, inner:].reshape(utt_count, key_total, HEADS, HD)
    scores = (
        jnp.einsum("uqhd,ukhd->uhqk", queries, keys, preferred_element_type=jnp.float32)
        * SCORE_SCALE
    )
    scores = jnp.where(key_mask[:, None, None, :], scores, MASK_FILL)
    top_score = jnp.max(scores, axis=-1, keepdims=True)
    expo = jnp.exp(scores - top_score)
    row_total = jnp.sum(expo, axis=-1, keepdims=True)
    log_total = top_score + jnp.log(row_total)
    probs_low = (expo / row_total).astype(jnp.bfloat16)
    attn_vals = jnp.einsum("uhqk,ukhd->uqhd", probs_low, values, preferred_element_type=jnp.float32)
    attn_vals = attn_vals.reshape(utt_count, key_total, inner).astype(jnp.bfloat16)
    attn_out = jnp.dot(attn_vals, out_weight, preferred_element_type=jnp.float32) + tf_small[2]
    mid_state = block_out + attn_out
    ff_in = layer_norm(mid_state, tf_small[3], tf_small[4]).astype(jnp.bfloat16)
    up_out = jnp.dot(ff_in, up_weight, preferred_element_type=jnp.float32) + wide_small[0]
    snake_out = snake_fn(up_out, wide_small[1], wide_small[2]).astype(jnp.bfloat16)
    ff_out = jnp.dot(snake_out, down_weight, preferred_element_type=jnp.float32) + tf_small[5]
    final = (mid_state + ff_out) * wide_mask
    grad_final = grad_ff.astype(jnp.float32)
    grad_down_w = jnp.einsum("utf,utc->fc", snake_out, grad_ff, preferred_element_type=jnp.float32)
    grad_down_b = jnp.sum(grad_ff, axis=(0, 1), dtype=jnp.float32)
    grad_snake = jnp.einsum("utc,fc->utf", grad_ff, down_weight, preferred_element_type=jnp.float32)
    snake_value, snake_pull = jax.vjp(snake_fn, up_out, wide_small[1], wide_small[2])
    grad_up_f, grad_alpha, grad_beta = snake_pull(grad_snake)
    grad_up = grad_up_f.astype(jnp.bfloat16)
    grad_up_w = jnp.einsum("utc,utf->cf", ff_in, grad_up, preferred_element_type=jnp.float32)
    grad_up_b = jnp.sum(grad_up, axis=(0, 1), dtype=jnp.float32)
    grad_ff_in = jnp.einsum("utf,cf->utc", grad_up, up_weight, preferred_element_type=jnp.float32)
    norm_value, norm_pull = jax.vjp(layer_norm, mid_state, tf_small[3], tf_small[4])
    grad_mid_ln, grad_ln3_g, grad_ln3_b = norm_pull(grad_ff_in)
    grad_mid = grad_final + grad_mid_ln
    grad_attn = grad_mid.astype(jnp.bfloat16)
    grad_out_w = jnp.einsum("uti,utc->ic", attn_vals, grad_attn, preferred_element_type=jnp.float32)
    grad_out_b = jnp.sum(grad_attn, axis=(0, 1), dtype=jnp.float32)
    grad_vals = jnp.einsum("utc,ic->uti", grad_attn, out_weight, preferred_element_type=jnp.float32)
    grad_vals = grad_vals.astype(jnp.bfloat16).reshape(utt_count, key_total, HEADS, HD)
    scores = (
        jnp.einsum("uqhd,ukhd->uhqk", queries, keys, preferred_element_type=jnp.float32)
        * SCORE_SCALE
    )
    scores = jnp.where(key_mask[:, None, None, :], scores, MASK_FILL)
    probs = jnp.exp(scores - log_total)
    probs_low = probs.astype(jnp.bfloat16)
    grad_probs = jnp.einsum(
        "uqhd,ukhd->uhqk", grad_vals, values, preferred_element_type=jnp.float32
    )
    row_dot = jnp.sum(probs * grad_probs, axis=-1, keepdims=True)
    grad_scores = (probs * (grad_probs - row_dot)).astype(jnp.bfloat16)
    grad_query = (
        jnp.einsum("uhqk,ukhd->uqhd", grad_scores, keys, preferred_element_type=jnp.float32)
        * SCORE_SCALE
    )
    grad_key = (
        jnp.einsum("uhqk,uqhd->ukhd", grad_scores, queries, preferred_element_type=jnp.float32)
        * SCORE_SCALE
    )
    grad_value = jnp.einsum(
        "uhqk,uqhd->ukhd", probs_low, grad_vals, preferred_element_type=jnp.float32
    )
    grad_kv = jnp.concatenate(
        [
            grad_key.reshape(utt_count, key_total, inner),
            grad_value.reshape(utt_count, key_total, inner),
        ],
        axis=2,
    )
    grad_kv_local = grad_kv
    grad_qkv = jnp.concatenate(
        [grad_query.reshape(utt_count, key_total, inner), grad_kv_local], axis=2
    ).astype(jnp.bfloat16)
    grad_qkv_w = jnp.einsum("utc,utd->cd", attn_in, grad_qkv, preferred_element_type=jnp.float32)
    grad_attn_in = jnp.einsum(
        "utd,cd->utc", grad_qkv, qkv_weight, preferred_element_type=jnp.float32
    )
    block_value, block_pull = jax.vjp(layer_norm, block_out, tf_small[0], tf_small[1])
    grad_block_ln, grad_ln1_g, grad_ln1_b = block_pull(grad_attn_in)
    grad_block = grad_mid + grad_block_ln
    grad_skip = grad_block.astype(jnp.bfloat16)
    grad_res_w = jnp.einsum("utc,utd->cd", masked_in, grad_skip, preferred_element_type=jnp.float32)
    grad_res_b = jnp.sum(grad_skip, axis=(0, 1), dtype=jnp.float32)
    grad_masked_in = jnp.einsum(
        "utd,cd->utc", grad_skip, res_weight, preferred_element_type=jnp.float32
    )
    mish_two, mish_pull_two = jax.vjp(mish_fn, norm_two)
    (grad_norm_two,) = mish_pull_two(grad_block * wide_mask)
    grad_z_two, grad_gn2_g, grad_gn2_b = norm_backward(
        grad_norm_two, normed_two, inv_two, frame_mask, valid_count, res_small[4]
    )
    grad_z_two = grad_z_two.astype(jnp.bfloat16)
    grad_conv_two = conv_weight_grad(padded_two, grad_z_two)
    grad_conv_two_b = jnp.sum(grad_z_two, axis=(0, 1), dtype=jnp.float32)
    grad_hidden = conv_input_grad(grad_z_two, conv_two) * wide_mask
    grad_time_proj = jnp.sum(grad_hidden, axis=1)
    grad_time_w = jnp.dot(
        time_act.astype(jnp.float32).T, grad_time_proj, precision=lax.Precision.HIGHEST
    )
    grad_time_b = jnp.sum(grad_time_proj, axis=0)
    mish_one, mish_pull_one = jax.vjp(mish_fn, norm_one)
    (grad_norm_one,) = mish_pull_one(grad_hidden * wide_mask)
    grad_z_one, grad_gn1_g, grad_gn1_b = norm_backward(
        grad_norm_one, normed_one, inv_one, frame_mask, valid_count, res_small[1]
    )
    grad_z_one = grad_z_one.astype(jnp.bfloat16)
    grad_conv_one = conv_weight_grad(padded_one, grad_z_one)
    grad_conv_one_b = jnp.sum(grad_z_one, axis=(0, 1), dtype=jnp.float32)
    grad_masked_in = grad_masked_in + conv_input_grad(grad_z_one, conv_one)
    grad_inputs = grad_masked_in * wide_mask
    grads = (
        jnp.concatenate([grad_conv_one.reshape(-1, C), grad_conv_two.reshape(-1, C)]),
        grad_res_w,
        grad_time_w,
        jnp.stack(
            [
                grad_conv_one_b,
                grad_gn1_g,
                grad_gn1_b,
                grad_conv_two_b,
                grad_gn2_g,
                grad_gn2_b,
                grad_res_b,
                grad_time_b,
            ]
        ),
        grad_qkv_w,
        grad_out_w,
        grad_up_w,
        grad_down_w,
        jnp.stack([grad_ln1_g, grad_ln1_b, grad_out_b, grad_ln3_g, grad_ln3_b, grad_down_b]),
        jnp.stack([grad_up_b, grad_alpha, grad_beta]),
    )
    summed = reduce_windows(orders, *cut_grads(places, shard_lengths, window_sizes, grads))
    res_share = from_window(summed[0], shard_lengths[0], owner)
    tf_share = from_window(summed[1], shard_lengths[1], owner)
    tokens_total = utts_here * key_total * lax.axis_size("dp")
    rate = LEARN_BASE / math.sqrt(tokens_total)
    res_new, res_moment_new, res_average_new, res_low = update(
        res_master, res_moment, res_average, res_share, rate
    )
    tf_new, tf_moment_new, tf_average_new, tf_low = update(
        tf_master, tf_moment, tf_average, tf_share, rate
    )
    return (
        to_frames(final),
        to_frames(grad_inputs),
        res_share,
        tf_share,
        res_new,
        tf_new,
        res_moment_new,
        tf_moment_new,
        res_average_new,
        tf_average_new,
        res_low,
        tf_low,
    )


def solution(mesh):
    placed = (
        P("dp", "seq", None),
        P("dp", None, None),
        P("dp", None),
        P("dp"),
        P("dp", None),
        P("dp", "seq", None),
        P(("dp", "seq")),
        P(("dp", "seq")),
        P(("dp", "seq")),
        P(("dp", "seq")),
        P(("dp", "seq")),
        P(("dp", "seq")),
    )
    return jax.shard_map(
        per_device,
        mesh=mesh,
        in_specs=placed,
        out_specs=(
            P("dp", "seq", None),
            P("dp", "seq", None),
            P(("dp", "seq")),
            P(("dp", "seq")),
            P(("dp", "seq")),
            P(("dp", "seq")),
            P(("dp", "seq")),
            P(("dp", "seq")),
            P(("dp", "seq")),
            P(("dp", "seq")),
            P(("dp", "seq")),
            P(("dp", "seq")),
        ),
        check_vma=False,
    )
```

```python
import functools
import math

import jax
import jax.numpy as jnp
from jax import lax
from jax.experimental import pallas as pl
from jax.experimental.pallas import tpu as pltpu
from jax.sharding import PartitionSpec as P

C = 256
GROUPS = 8
TE = 1024
HEADS = 2
HD = 64
F = 1024


EPSILON = 1e-05
SCORE_SCALE = 0.125
MOMENTUM = 0.9
AVERAGE_DECAY = 0.99
LEARN_BASE = 0.015
MASK_FILL = -1e30


def soft_plus(signal):
    return jnp.log1p(jnp.exp(-jnp.abs(signal))) + jnp.maximum(signal, 0.0)


def mish_fn(signal):
    return signal * jnp.tanh(soft_plus(signal))


def snake_fn(signal, alpha_row, beta_row):
    return signal + jnp.sin(signal * jnp.exp(alpha_row)) ** 2 / (jnp.exp(beta_row) + 1e-09)


def layer_norm(signal, gain_row, shift_row):
    center = signal - jnp.mean(signal, axis=-1, keepdims=True)
    spread = jnp.mean(center * center, axis=-1, keepdims=True)
    return center * lax.rsqrt(spread + EPSILON) * gain_row + shift_row


def take_rows(phone_table, phone_rows):
    return phone_table[phone_rows]


def rim_pad(signal):
    return jnp.pad(signal, ((0, 0), (1, 1), (0, 0)))


def conv_apply(padded, weight):
    length_here = padded.shape[1] - 2
    result = jnp.dot(padded[:, 0:length_here], weight[0], preferred_element_type=jnp.float32)
    result = result + jnp.dot(
        padded[:, 1 : length_here + 1], weight[1], preferred_element_type=jnp.float32
    )
    return result + jnp.dot(padded[:, 2:], weight[2], preferred_element_type=jnp.float32)


def conv_weight_grad(padded, grad_low):
    length_here = grad_low.shape[1]
    return jnp.stack(
        [
            jnp.einsum(
                "utc,utd->cd",
                padded[:, tap_index : tap_index + length_here],
                grad_low,
                preferred_element_type=jnp.float32,
            )
            for tap_index in range(3)
        ]
    )


def conv_input_grad(grad_low, weight):
    padded = rim_pad(grad_low)
    length_here = grad_low.shape[1]
    result = jnp.einsum("utd,cd->utc", padded[:, 2:], weight[0], preferred_element_type=jnp.float32)
    result = result + jnp.einsum(
        "utd,cd->utc", padded[:, 1 : length_here + 1], weight[1], preferred_element_type=jnp.float32
    )
    return result + jnp.einsum(
        "utd,cd->utc", padded[:, 0:length_here], weight[2], preferred_element_type=jnp.float32
    )


def norm_forward(signal, frame_mask, valid_count, gain_row, shift_row):
    width = C // GROUPS
    shape_now = signal.shape
    grouped = (signal * frame_mask[:, :, None]).reshape(shape_now[0], shape_now[1], GROUPS, width)
    total = jnp.sum(grouped, axis=(1, 3))
    squares = jnp.sum(grouped * grouped, axis=(1, 3))
    number = valid_count[:, None] * width
    mean_now = total / number
    inv_std = lax.rsqrt(squares / number - mean_now * mean_now + EPSILON)
    mean_wide = jnp.repeat(mean_now, width, axis=1)[:, None, :]
    inv_wide = jnp.repeat(inv_std, width, axis=1)[:, None, :]
    normed = (signal - mean_wide) * inv_wide
    return (normed * gain_row + shift_row, normed, inv_wide)


def norm_backward(grad_out, normed, inv_wide, frame_mask, valid_count, gain_row):
    width = C // GROUPS
    shape_now = grad_out.shape
    grad_norm = grad_out * gain_row
    first_sum = jnp.sum(grad_norm.reshape(shape_now[0], shape_now[1], GROUPS, width), axis=(1, 3))
    second_sum = jnp.sum(
        (grad_norm * normed).reshape(shape_now[0], shape_now[1], GROUPS, width), axis=(1, 3)
    )
    number = valid_count[:, None] * width
    first_wide = jnp.repeat(first_sum / number, width, axis=1)[:, None, :]
    second_wide = jnp.repeat(second_sum / number, width, axis=1)[:, None, :]
    grad_signal = inv_wide * (
        grad_norm - frame_mask[:, :, None] * (first_wide + normed * second_wide)
    )
    grad_gain = jnp.sum(grad_out * normed, axis=(0, 1))
    grad_shift = jnp.sum(grad_out, axis=(0, 1))
    return (grad_signal, grad_gain, grad_shift)


def update(master, moment, average, grad, rate):
    moment_new = MOMENTUM * moment + grad
    master_new = master - rate * (grad + MOMENTUM * moment_new)
    average_new = AVERAGE_DECAY * average + (1.0 - AVERAGE_DECAY) * master_new
    return (master_new, moment_new, average_new, master_new.astype(jnp.bfloat16))


def axis_bits(mesh_sizes):
    bits = []
    for name, size in mesh_sizes:
        weight = size // 2
        while weight >= 1:
            bits.append((name, weight))
            weight //= 2
    return bits


def part_orders(mesh_sizes):
    first = axis_bits(mesh_sizes)
    second = list(first)
    if len(second) >= 3:
        second[-3], second[-2] = second[-2], second[-3]
    return (first, second)


def owner_place(order, mesh_sizes, owner):
    strides, stride = {}, 1
    for name, size in reversed(mesh_sizes):
        strides[name] = (stride, size)
        stride *= size
    place = 0
    for step, (name, weight) in enumerate(order):
        base, size = strides[name]
        place += ((owner // base) % size // weight % 2) << step
    return place


def window_rows(length_now, count):
    most = max((i * length_now) % 128 + length_now for i in range(count))
    return -(-most // (128 * 16)) * 16


def bit_of(name, weight):
    return (lax.axis_index(name) // weight) % 2


def partner_of(name, weight):
    return {name: lax.axis_index(name) + (1 - 2 * bit_of(name, weight)) * weight}


def greet(orders):
    barrier = pltpu.get_barrier_semaphore()
    for name, weight in orders[0]:
        pl.semaphore_signal(
            barrier,
            inc=1,
            device_id=partner_of(name, weight),
            device_id_type=pl.DeviceIdType.MESH,
        )
    pl.semaphore_wait(barrier, len(orders[0]))


def gather_kernel(orders, in_a, in_b, out_a, out_b, local_sem, send_sem, recv_sem):
    ins, outs = (in_a, in_b), (out_a, out_b)
    stage_count = len(orders[0])
    offsets = []
    for part in range(2):
        offset = 0
        for step, (name, weight) in enumerate(orders[part]):
            offset = offset + bit_of(name, weight) * (1 << step)
        offsets.append(offset)
    locals_now = [
        pltpu.make_async_copy(ins[part], outs[part].at[offsets[part]], local_sem.at[part])
        for part in range(2)
    ]
    for copy in locals_now:
        copy.start()
    greet(orders)
    for copy in locals_now:
        copy.wait()
    copies = []
    for step in range(stage_count):
        held = 1 << step
        for part in range(2):
            name, weight = orders[part][step]
            start = offsets[part]
            block = outs[part].at[pl.ds(start, held)]
            copy = pltpu.make_async_remote_copy(
                src_ref=block,
                dst_ref=block,
                send_sem=send_sem.at[part, step],
                recv_sem=recv_sem.at[part, step],
                device_id=partner_of(name, weight),
                device_id_type=pl.DeviceIdType.MESH,
            )
            copy.start()
            copies.append(copy)
        for part in range(2):
            copies[2 * step + part].wait_recv()
            name, weight = orders[part][step]
            offsets[part] = offsets[part] - bit_of(name, weight) * held
    for copy in copies:
        copy.wait_send()


def gather_windows(orders, win_a, win_b):
    count = 1 << len(orders[0])
    stages = len(orders[0])
    return pl.pallas_call(
        functools.partial(gather_kernel, orders),
        out_shape=(
            jax.ShapeDtypeStruct((count,) + win_a.shape, win_a.dtype),
            jax.ShapeDtypeStruct((count,) + win_b.shape, win_b.dtype),
        ),
        in_specs=[pl.BlockSpec(memory_space=pltpu.VMEM)] * 2,
        out_specs=[pl.BlockSpec(memory_space=pltpu.VMEM)] * 2,
        scratch_shapes=[
            pltpu.SemaphoreType.DMA((2,)),
            pltpu.SemaphoreType.DMA((2, stages)),
            pltpu.SemaphoreType.DMA((2, stages)),
        ],
        compiler_params=pltpu.CompilerParams(
            collective_id=0, has_side_effects=True, vmem_limit_bytes=32 * 1024 * 1024
        ),
    )(win_a, win_b)


def reduce_kernel(orders, in_a, in_b, out_a, out_b, land_a, land_b, send_sem, recv_sem):
    ins, outs, lands = (in_a, in_b), (out_a, out_b), (land_a, land_b)
    stage_count = len(orders[0])
    greet(orders)
    copies = []

    def source(part, step, keep):
        name, weight = orders[part][stage_count - 1 - step]
        held = 1 << (stage_count - 1 - step)
        side = bit_of(name, weight)
        side = side if keep else 1 - side
        if step == 0:
            return ins[part].at[pl.ds(side * held, held)]
        base = (1 << stage_count) - (1 << (stage_count - step + 1))
        return lands[part].at[pl.ds(base + side * held, held)]

    for step in range(stage_count):
        held = 1 << (stage_count - 1 - step)
        base = (1 << stage_count) - (1 << (stage_count - step))
        for part in range(2):
            name, weight = orders[part][stage_count - 1 - step]
            copy = pltpu.make_async_remote_copy(
                src_ref=source(part, step, False),
                dst_ref=lands[part].at[pl.ds(base, held)],
                send_sem=send_sem.at[part, step],
                recv_sem=recv_sem.at[part, step],
                device_id=partner_of(name, weight),
                device_id_type=pl.DeviceIdType.MESH,
            )
            copy.start()
            copies.append(copy)
        for part in range(2):
            copies[2 * step + part].wait_recv()
            mine = source(part, step, True)
            if step == stage_count - 1:
                outs[part][...] = mine[0].astype(jnp.float32) + lands[part][base].astype(
                    jnp.float32
                )
            else:

                def add_one(index, carry, mine=mine, part=part, base=base):
                    land = lands[part].at[base + index]
                    total = mine[index].astype(jnp.float32) + land[...].astype(jnp.float32)
                    land[...] = total.astype(land.dtype)
                    return carry

                lax.fori_loop(0, held, add_one, 0)
    for copy in copies:
        copy.wait_send()


def reduce_windows(orders, rows_a, rows_b):
    count = 1 << len(orders[0])
    stages = len(orders[0])
    return pl.pallas_call(
        functools.partial(reduce_kernel, orders),
        out_shape=(
            jax.ShapeDtypeStruct(rows_a.shape[1:], jnp.float32),
            jax.ShapeDtypeStruct(rows_b.shape[1:], jnp.float32),
        ),
        in_specs=[pl.BlockSpec(memory_space=pltpu.VMEM)] * 2,
        out_specs=[pl.BlockSpec(memory_space=pltpu.VMEM)] * 2,
        scratch_shapes=[
            pltpu.VMEM((count - 1,) + rows_a.shape[1:], rows_a.dtype),
            pltpu.VMEM((count - 1,) + rows_b.shape[1:], rows_b.dtype),
            pltpu.SemaphoreType.DMA((2, stages)),
            pltpu.SemaphoreType.DMA((2, stages)),
        ],
        compiler_params=pltpu.CompilerParams(
            collective_id=1, has_side_effects=True, vmem_limit_bytes=32 * 1024 * 1024
        ),
    )(rows_a, rows_b)


RES_SQUARES = 7 * C * C
RES_ROWS = (RES_SQUARES + TE * C + 8 * C) // 128
INNER = HEADS * HD
TF_SIZES = (3 * C * INNER, INNER * C, C * F, F * C, 6 * C, 3 * F)
TF_ROWS = sum(TF_SIZES) // 128


def place_maps(orders, mesh_sizes):
    count = 1 << len(orders[0])
    return [[owner_place(orders[part], mesh_sizes, i) for i in range(count)] for part in range(2)]


def matrix_views():
    views = []
    row = 0
    for rows, width in ((6 * C, C), (C, C), (TE, C), (8, C)):
        views.append((0, row, rows, width))
        row += rows * width // 128
    row = 0
    for rows, width in ((C, 3 * INNER), (INNER, C), (C, F), (F, C), (6, C), (3, F)):
        views.append((1, row, rows, width))
        row += rows * width // 128
    return views


def assemble_kernel(places, lengths_now, in_a, in_b, *refs):
    outs, flats = refs[:10], refs[10:12]
    count = len(places[0])
    for part, ref in enumerate((in_a, in_b)):
        flat = flats[part]
        for i in range(count):
            start, lead = divmod(i * lengths_now[part], 128)
            rows = -(-(lead + lengths_now[part]) // 128)
            if lead:
                edge = flat[start : start + 1, :]
            flat[start : start + rows, :] = ref[places[part][i]].astype(jnp.float32)[:rows]
            if lead:
                flat[start : start + 1, :] = flat[start : start + 1, :] + edge
    for out, (part, row, rows, width) in zip(outs, matrix_views()):
        stride = width // 128
        for lane in range(stride):
            piece = flats[part][pl.ds(row + lane, rows, stride=stride), :]
            out[:, lane * 128 : (lane + 1) * 128] = piece.astype(out.dtype)


def assemble_weights(places, lengths_now, win_a, win_b):
    shapes = []
    for index, (part, row, rows, width) in enumerate(matrix_views()):
        kind = jnp.float32 if index in (3, 8, 9) else jnp.bfloat16
        shapes.append(jax.ShapeDtypeStruct((rows, width), kind))
    return pl.pallas_call(
        functools.partial(assemble_kernel, places, lengths_now),
        out_shape=shapes,
        in_specs=[pl.BlockSpec(memory_space=pltpu.VMEM)] * 2,
        out_specs=[pl.BlockSpec(memory_space=pltpu.VMEM)] * 10,
        scratch_shapes=[
            pltpu.VMEM((RES_ROWS + 8, 128), jnp.float32),
            pltpu.VMEM((TF_ROWS + 12, 128), jnp.float32),
        ],
        compiler_params=pltpu.CompilerParams(vmem_limit_bytes=32 * 1024 * 1024),
    )(win_a, win_b)


def cut_kernel(places, lengths_now, *refs):
    ins, outs, flats = refs[:10], refs[10:12], refs[12:14]
    count = len(places[0])
    for ref, (part, row, rows, width) in zip(ins, matrix_views()):
        stride = width // 128
        for lane in range(stride):
            flats[part][pl.ds(row + lane, rows, stride=stride), :] = ref[
                :, lane * 128 : (lane + 1) * 128
            ]
    for part in range(2):
        for i in range(count):
            start, lead = divmod(i * lengths_now[part], 128)
            rows = outs[part].shape[1]
            outs[part][places[part][i]] = flats[part][start : start + rows, :].astype(
                outs[part].dtype
            )


def cut_grads(places, lengths_now, window_sizes, grads):
    count = len(places[0])
    return pl.pallas_call(
        functools.partial(cut_kernel, places, lengths_now),
        out_shape=[
            jax.ShapeDtypeStruct((count, rows, 128), jnp.bfloat16) for rows in window_sizes
        ],
        in_specs=[pl.BlockSpec(memory_space=pltpu.VMEM)] * 10,
        out_specs=[pl.BlockSpec(memory_space=pltpu.VMEM)] * 2,
        scratch_shapes=[
            pltpu.VMEM((RES_ROWS + 24, 128), jnp.float32),
            pltpu.VMEM((TF_ROWS + 28, 128), jnp.float32),
        ],
        compiler_params=pltpu.CompilerParams(vmem_limit_bytes=40 * 1024 * 1024),
    )(*grads)


def flat_index(mesh_sizes):
    index = 0
    for name, size in mesh_sizes:
        index = index * size + lax.axis_index(name)
    return index


def to_window(master, rows, owner):
    lead = (owner * master.shape[0]) % 128
    window = jnp.zeros((rows * 128,), jnp.bfloat16)
    return lax.dynamic_update_slice(window, master.astype(jnp.bfloat16), (lead,)).reshape(rows, 128)


def from_window(window, length_now, owner):
    lead = (owner * length_now) % 128
    return lax.dynamic_slice(window.reshape(-1), (lead,), (length_now,))


def to_utts(cells):
    return lax.all_to_all(cells, "seq", split_axis=0, concat_axis=1, tiled=True)


def to_frames(cells):
    low = cells.astype(jnp.bfloat16)
    return lax.all_to_all(low, "seq", split_axis=1, concat_axis=0, tiled=True).astype(jnp.float32)


SIN_TERMS = (
    0.9999999956945583,
    -0.1666665793542191,
    0.008333049779226345,
    -0.00019808982984063025,
    2.605019582312477e-06,
)
COS_TERMS = (
    0.9999999997785896,
    -0.4999999935376167,
    0.04166663608814044,
    -0.0013888359276781354,
    2.47600539678114e-05,
    -2.6049608156992194e-07,
)
PI_PARTS = (3.140625, 0.0009670257568359375, 6.27832957178498e-07)
ROUND_SHIFT = 12582912.0
TILE = 256


def mm(left, right):
    return jnp.dot(left, right, preferred_element_type=jnp.float32)


def mm_right(left, right):
    return lax.dot_general(
        left, right, (((1,), (1,)), ((), ())), preferred_element_type=jnp.float32
    )


def mm_left(left, right):
    return lax.dot_general(
        left, right, (((0,), (0,)), ((), ())), preferred_element_type=jnp.float32
    )


def column_sum(cells):
    return jnp.sum(cells, axis=0, keepdims=True)


def sin_cos(angle):
    turns = (angle * (1.0 / math.pi) + ROUND_SHIFT) - ROUND_SHIFT
    rest = angle - turns * PI_PARTS[0]
    rest = rest - turns * PI_PARTS[1]
    rest = rest - turns * PI_PARTS[2]
    square = rest * rest
    sine = SIN_TERMS[-1]
    for term in SIN_TERMS[-2::-1]:
        sine = sine * square + term
    cosine = COS_TERMS[-1]
    for term in COS_TERMS[-2::-1]:
        cosine = cosine * square + term
    return (sine * rest, cosine)


def mish_value(signal):
    expo = jnp.exp(jnp.minimum(signal, 20.0))
    upper = expo * (expo + 2.0)
    return signal * (upper / (upper + 2.0))


def mish_slope(signal):
    expo = jnp.exp(jnp.minimum(signal, 20.0))
    upper = expo * (expo + 2.0)
    inverse = 1.0 / (upper + 2.0)
    return upper * inverse + signal * (4.0 * expo * (1.0 + expo)) * (inverse * inverse)


def row_norm(signal):
    center = signal - jnp.mean(signal, axis=-1, keepdims=True)
    spread = jnp.mean(center * center, axis=-1, keepdims=True)
    inverse = lax.rsqrt(spread + EPSILON)
    return (center * inverse, inverse)


def row_norm_back(grad_out, normed, inverse, gain_row):
    inner_grad = grad_out * gain_row
    first = jnp.mean(inner_grad, axis=-1, keepdims=True)
    second = jnp.mean(inner_grad * normed, axis=-1, keepdims=True)
    return (inner_grad - first - normed * second) * inverse


def step_kernel(
    lengths_ref,
    x_ref,
    g_ref,
    time_ref,
    convs_ref,
    res_ref,
    rows_ref,
    qkv_ref,
    out_ref,
    up_ref,
    down_ref,
    tf_rows_ref,
    wide_ref,
    final_ref,
    gin_ref,
    gtime_ref,
    gconvs_ref,
    gres_ref,
    grows_ref,
    gqkv_ref,
    gout_ref,
    gup_ref,
    gdown_ref,
    gtf_ref,
    gwide_ref,
    pad,
    col_one,
    col_two,
    col_grad,
    z_one,
    z_two,
    block,
    grad_mid,
    grad_norm,
    attn_in,
    heads_q,
    heads_k,
    heads_v,
    heads_g,
    attn_vals,
    probs,
    snake,
    grad_up,
    ff_in,
    grad_attn,
    grad_key,
    grad_value,
    grad_query,
    grad_qkv,
    grad_skip,
):
    frames = z_one.shape[0]
    tiles = frames // TILE
    utt = pl.program_id(0)
    length_now = lengths_ref[utt]
    number = length_now.astype(jnp.float32) * (C // GROUPS)

    @pl.when(utt == 0)
    def clear():
        for ref in (
            gconvs_ref,
            gres_ref,
            grows_ref,
            gqkv_ref,
            gout_ref,
            gup_ref,
            gdown_ref,
            gtf_ref,
            gwide_ref,
        ):
            ref[...] = jnp.zeros_like(ref)

    edge = jnp.zeros((8, C), jnp.float32)
    pad[0:8, :] = edge
    pad[frames + 8 : frames + 16, :] = edge
    gtime_ref[...] = jnp.zeros_like(gtime_ref)
    group_row = lax.broadcasted_iota(jnp.int32, (C, C), 0) // (C // GROUPS)
    group_column = lax.broadcasted_iota(jnp.int32, (C, C), 1) // (C // GROUPS)
    group_ones = (group_row == group_column).astype(jnp.float32)
    lane = lax.broadcasted_iota(jnp.int32, (1, INNER), 1) // HD
    head_masks = [(lane == head).astype(jnp.float32) for head in range(HEADS)]
    key_bias = jnp.where(
        lax.broadcasted_iota(jnp.int32, (1, frames), 1) < length_now, 0.0, MASK_FILL
    )

    def rows_at(index, lead=0):
        return pl.ds(pl.multiple_of(index * TILE + lead, 8), TILE)

    def tile_mask(index):
        ids = lax.broadcasted_iota(jnp.int32, (TILE, 1), 0) + index * TILE
        return (ids < length_now).astype(jnp.float32)

    def group_sum(row):
        wide = jnp.broadcast_to(row, (8, C))
        return jnp.dot(
            wide,
            group_ones,
            precision=lax.Precision.HIGHEST,
            preferred_element_type=jnp.float32,
        )[0:1]

    def build_columns(target):
        for index in range(tiles):
            start = index * TILE
            for tap in range(3):
                piece = pad[start + 7 + tap : start + 7 + tap + TILE, :]
                target[start : start + TILE, tap * C : (tap + 1) * C] = piece.astype(jnp.bfloat16)

    def loop(body):
        def wrapped(index, carry):
            body(index)
            return carry

        lax.fori_loop(0, tiles, wrapped, 0)

    def conv_stage(columns, base, bias_at, target):
        def one(index, carry):
            rows = rows_at(index)
            cells = mm(columns[rows, :], convs_ref[base : base + 3 * C, :])
            cells = cells + rows_ref[bias_at : bias_at + 1, :]
            target[rows, :] = cells
            masked = cells * tile_mask(index)
            return (carry[0] + column_sum(masked), carry[1] + column_sum(masked * masked))

        zero = jnp.zeros((1, C), jnp.float32)
        total, squares = lax.fori_loop(0, tiles, one, (zero, zero))
        mean_row = group_sum(total) / number
        inv_row = lax.rsqrt(group_sum(squares) / number - mean_row * mean_row + EPSILON)
        return (mean_row, inv_row)

    def copy_in(index):
        pad[rows_at(index, 8), :] = x_ref[0, rows_at(index), :].astype(jnp.float32)

    loop(copy_in)
    build_columns(col_one)
    mean_one, inv_one = conv_stage(col_one, 0, 0, z_one)

    def hidden(index):
        normed = (z_one[rows_at(index), :] - mean_one) * inv_one
        act = mish_value(normed * rows_ref[1:2, :] + rows_ref[2:3, :])
        pad[rows_at(index, 8), :] = (act + time_ref[0]) * tile_mask(index)

    loop(hidden)
    build_columns(col_two)
    mean_two, inv_two = conv_stage(col_two, 3 * C, 3, z_two)

    def enter(index):
        rows = rows_at(index)
        normed = (z_two[rows, :] - mean_two) * inv_two
        act = mish_value(normed * rows_ref[4:5, :] + rows_ref[5:6, :]) * tile_mask(index)
        state = act + mm(x_ref[0, rows, :], res_ref[...]) + rows_ref[6:7, :]
        block[rows, :] = state
        normed, _ = row_norm(state)
        low = (normed * tf_rows_ref[0:1, :] + tf_rows_ref[1:2, :]).astype(jnp.bfloat16)
        attn_in[rows, :] = low
        parts = mm(low, qkv_ref[...]).astype(jnp.bfloat16).astype(jnp.float32)
        query = parts[:, :INNER] * SCORE_SCALE
        for head in range(HEADS):
            heads_q[head, rows, :] = (query * head_masks[head]).astype(jnp.bfloat16)
            heads_k[head, rows, :] = (parts[:, INNER : 2 * INNER] * head_masks[head]).astype(
                jnp.bfloat16
            )
            heads_v[head, rows, :] = (parts[:, 2 * INNER :] * head_masks[head]).astype(
                jnp.bfloat16
            )

    loop(enter)

    def attend(index):
        rows = rows_at(index)
        total = jnp.zeros((TILE, INNER), jnp.float32)
        for head in range(HEADS):
            scores = mm_right(heads_q[head, rows, :], heads_k[head]) + key_bias
            expo = jnp.exp(scores - jnp.max(scores, axis=-1, keepdims=True))
            chance = expo * (1.0 / jnp.sum(expo, axis=-1, keepdims=True))
            probs[head, rows, :] = chance
            total = total + mm(chance.astype(jnp.bfloat16), heads_v[head])
        attn_vals[rows, :] = total.astype(jnp.bfloat16)

    loop(attend)

    def feed(index):
        rows = rows_at(index)
        mid = block[rows, :] + mm(attn_vals[rows, :], out_ref[...]) + tf_rows_ref[2:3, :]
        normed, inverse = row_norm(mid)
        low = (normed * tf_rows_ref[3:4, :] + tf_rows_ref[4:5, :]).astype(jnp.bfloat16)
        ff_in[rows, :] = low
        grad_low = g_ref[0, rows, :]
        result = jnp.zeros((TILE, C), jnp.float32)
        grad_in = jnp.zeros((TILE, C), jnp.float32)
        for chunk in range(F // 256):
            lanes = slice(chunk * 256, (chunk + 1) * 256)
            up_out = mm(low, up_ref[:, lanes]) + wide_ref[0:1, lanes]
            grad_snake = mm_right(grad_low, down_ref[lanes, :])
            speed = jnp.exp(wide_ref[1:2, lanes])
            depth = 1.0 / (jnp.exp(wide_ref[2:3, lanes]) + 1e-09)
            angle = up_out * speed
            sine, cosine = sin_cos(angle)
            square = sine * sine
            value = (up_out + square * depth).astype(jnp.bfloat16)
            snake[rows, lanes] = value
            result = result + mm(value, down_ref[lanes, :])
            slope = grad_snake * ((2.0 * sine) * cosine) * depth
            grad_here = (grad_snake + slope * speed).astype(jnp.bfloat16)
            grad_up[rows, lanes] = grad_here
            grad_in = grad_in + mm_right(grad_here, up_ref[:, lanes])
            gwide_ref[0:1, lanes] += column_sum(grad_here.astype(jnp.float32))
            gwide_ref[1:2, lanes] += column_sum(slope * angle)
            gwide_ref[2:3, lanes] += column_sum(grad_snake * square)
        final_ref[0, rows, :] = ((mid + result + tf_rows_ref[5:6, :]) * tile_mask(index)).astype(
            jnp.bfloat16
        )
        grad_wide = grad_low.astype(jnp.float32)
        gtf_ref[5:6, :] += column_sum(grad_wide)
        gtf_ref[3:4, :] += column_sum(grad_in * normed)
        gtf_ref[4:5, :] += column_sum(grad_in)
        grad_state = grad_wide + row_norm_back(grad_in, normed, inverse, tf_rows_ref[3:4, :])
        grad_mid[rows, :] = grad_state
        grad_state = grad_state.astype(jnp.bfloat16)
        grad_attn[rows, :] = grad_state
        gtf_ref[2:3, :] += column_sum(grad_state.astype(jnp.float32))
        grad_vals = mm_right(grad_state, out_ref[...]).astype(jnp.bfloat16).astype(jnp.float32)
        for head in range(HEADS):
            heads_g[head, rows, :] = (grad_vals * head_masks[head]).astype(jnp.bfloat16)

    loop(feed)

    def feed_weights(index, carry):
        lanes = pl.ds(pl.multiple_of(index * 256, 256), 256)
        gdown_ref[lanes, :] += mm_left(snake[:, lanes], g_ref[0])
        gup_ref[:, lanes] += mm_left(ff_in[...], grad_up[:, lanes])
        return carry

    lax.fori_loop(0, F // 256, feed_weights, 0)
    gout_ref[...] += mm_left(attn_vals[...], grad_attn[...])
    grad_key[...] = jnp.zeros_like(grad_key)
    grad_value[...] = jnp.zeros_like(grad_value)

    def attend_back(index):
        rows = rows_at(index)
        total = jnp.zeros((TILE, INNER), jnp.float32)
        for head in range(HEADS):
            grad_out = heads_g[head, rows, :]
            chance = probs[head, rows, :]
            grad_probs = mm_right(grad_out, heads_v[head])
            dot_row = jnp.sum(chance * grad_probs, axis=-1, keepdims=True)
            grad_scores = (chance * (grad_probs - dot_row)).astype(jnp.bfloat16)
            total = total + mm(grad_scores, heads_k[head])
            grad_key[...] += mm_left(grad_scores, heads_q[head, rows, :])
            grad_value[...] += mm_left(chance.astype(jnp.bfloat16), grad_out)
        grad_query[rows, :] = total * SCORE_SCALE

    loop(attend_back)

    def leave(index, carry):
        rows = rows_at(index)
        grad_qkv[rows, 0:INNER] = grad_query[rows, :].astype(jnp.bfloat16)
        grad_qkv[rows, INNER : 2 * INNER] = grad_key[rows, :].astype(jnp.bfloat16)
        grad_qkv[rows, 2 * INNER : 3 * INNER] = grad_value[rows, :].astype(jnp.bfloat16)
        grad_in = mm_right(grad_qkv[rows, :], qkv_ref[...])
        normed, inverse = row_norm(block[rows, :])
        gtf_ref[0:1, :] += column_sum(grad_in * normed)
        gtf_ref[1:2, :] += column_sum(grad_in)
        grad_state = grad_mid[rows, :] + row_norm_back(
            grad_in, normed, inverse, tf_rows_ref[0:1, :]
        )
        low = grad_state.astype(jnp.bfloat16)
        grad_skip[rows, :] = low
        grows_ref[6:7, :] += column_sum(low.astype(jnp.float32))
        normed = (z_two[rows, :] - mean_two) * inv_two
        grad_here = (
            mish_slope(normed * rows_ref[4:5, :] + rows_ref[5:6, :])
            * tile_mask(index)
            * grad_state
        )
        grad_norm[rows, :] = grad_here
        return (carry[0] + column_sum(grad_here), carry[1] + column_sum(grad_here * normed))

    zero = jnp.zeros((1, C), jnp.float32)

    def norm_back(target, mean_row, inv_row, gain_at, bias_at, shift_sum, gain_sum):
        gain_row = rows_ref[gain_at : gain_at + 1, :]
        grows_ref[gain_at : gain_at + 1, :] += gain_sum
        grows_ref[gain_at + 1 : gain_at + 2, :] += shift_sum
        first = group_sum(shift_sum * gain_row) / number
        second = group_sum(gain_sum * gain_row) / number

        def one(index):
            rows = rows_at(index)
            normed = (target[rows, :] - mean_row) * inv_row
            cells = inv_row * (
                grad_norm[rows, :] * gain_row - tile_mask(index) * (first + normed * second)
            )
            cells = cells.astype(jnp.bfloat16).astype(jnp.float32)
            grows_ref[bias_at : bias_at + 1, :] += column_sum(cells)
            pad[rows_at(index, 8), :] = cells

        loop(one)
        build_columns(col_grad)

    def conv_back(rows, base):
        total = mm_right(col_grad[rows, 2 * C : 3 * C], convs_ref[base : base + C, :])
        total = total + mm_right(col_grad[rows, C : 2 * C], convs_ref[base + C : base + 2 * C, :])
        return total + mm_right(col_grad[rows, 0:C], convs_ref[base + 2 * C : base + 3 * C, :])

    def conv_weights(columns, base):
        for tap in range(3):
            gconvs_ref[base + tap * C : base + (tap + 1) * C, :] += mm_left(
                columns[:, tap * C : (tap + 1) * C], col_grad[:, C : 2 * C]
            )

    shift_sum, gain_sum = lax.fori_loop(0, tiles, leave, (zero, zero))
    norm_back(z_two, mean_two, inv_two, 4, 3, shift_sum, gain_sum)
    conv_weights(col_two, 3 * C)

    def hidden_back(index, carry):
        rows = rows_at(index)
        grad_here = conv_back(rows, 3 * C) * tile_mask(index)
        gtime_ref[0] += column_sum(grad_here)
        normed = (z_one[rows, :] - mean_one) * inv_one
        grad_here = mish_slope(normed * rows_ref[1:2, :] + rows_ref[2:3, :]) * grad_here
        grad_norm[rows, :] = grad_here
        return (carry[0] + column_sum(grad_here), carry[1] + column_sum(grad_here * normed))

    shift_sum, gain_sum = lax.fori_loop(0, tiles, hidden_back, (zero, zero))
    grows_ref[7:8, :] += gtime_ref[0]
    norm_back(z_one, mean_one, inv_one, 1, 0, shift_sum, gain_sum)
    conv_weights(col_one, 0)

    def finish(index):
        rows = rows_at(index)
        total = conv_back(rows, 0) + mm_right(grad_skip[rows, :], res_ref[...])
        gin_ref[0, rows, :] = (total * tile_mask(index)).astype(jnp.bfloat16)

    loop(finish)
    gres_ref[...] += mm_left(x_ref[0], grad_skip[...])
    gqkv_ref[...] += mm_left(attn_in[...], grad_qkv[...])

    @pl.when(utt == pl.num_programs(0) - 1)
    def scale_rows():
        low_side = jnp.exp(wide_ref[2:3, :])
        depth = 1.0 / (low_side + 1e-09)
        gwide_ref[2:3, :] = -gwide_ref[2:3, :] * low_side * depth * depth


def whole_step(lengths, cells, grads, time_proj, weights):
    (convs, res_weight, rows, qkv_weight, out_weight, up_weight, down_weight, tf_rows, wide) = weights
    utts, frames, _ = cells.shape
    by_utt = pl.BlockSpec((1, frames, C), lambda u, s: (u, 0, 0))
    row_by_utt = pl.BlockSpec((1, 1, C), lambda u, s: (u, 0, 0))

    def fixed(array):
        return pl.BlockSpec(array.shape, lambda u, s: (0, 0))

    f32, low = jnp.float32, jnp.bfloat16
    scratch = [
        ((frames + 16, C), f32),
        ((frames, 3 * C), low),
        ((frames, 3 * C), low),
        ((frames, 3 * C), low),
        ((frames, C), f32),
        ((frames, C), f32),
        ((frames, C), f32),
        ((frames, C), f32),
        ((frames, C), f32),
        ((frames, C), low),
        ((HEADS, frames, INNER), low),
        ((HEADS, frames, INNER), low),
        ((HEADS, frames, INNER), low),
        ((HEADS, frames, INNER), low),
        ((frames, INNER), low),
        ((HEADS, frames, frames), f32),
        ((frames, F), low),
        ((frames, F), low),
        ((frames, C), low),
        ((frames, C), low),
        ((frames, INNER), f32),
        ((frames, INNER), f32),
        ((frames, INNER), f32),
        ((frames, 3 * INNER), low),
        ((frames, C), low),
    ]
    return pl.pallas_call(
        step_kernel,
        grid_spec=pltpu.PrefetchScalarGridSpec(
            num_scalar_prefetch=1,
            grid=(utts,),
            in_specs=[by_utt, by_utt, row_by_utt] + [fixed(array) for array in weights],
            out_specs=[by_utt, by_utt, row_by_utt] + [fixed(array) for array in weights],
            scratch_shapes=[pltpu.VMEM(shape, kind) for shape, kind in scratch],
        ),
        out_shape=[
            jax.ShapeDtypeStruct(cells.shape, low),
            jax.ShapeDtypeStruct(cells.shape, low),
            jax.ShapeDtypeStruct((utts, 1, C), f32),
        ]
        + [jax.ShapeDtypeStruct(array.shape, f32) for array in weights],
        compiler_params=pltpu.CompilerParams(
            dimension_semantics=("arbitrary",), vmem_limit_bytes=60 * 1024 * 1024
        ),
    )(lengths, cells, grads, time_proj, *weights)


def per_device(
    inputs,
    encoded,
    durations,
    lengths,
    time_embed,
    cotangent,
    res_master,
    res_moment,
    res_average,
    tf_master,
    tf_moment,
    tf_average,
):
    utts_here, local_len, _ = inputs.shape
    seq_size = lax.axis_size("seq")
    key_total = local_len * seq_size
    utt_count = utts_here // seq_size
    inner = HEADS * HD
    seq_index = lax.axis_index("seq")
    frame_ids = seq_index * local_len + jnp.arange(local_len, dtype=jnp.int32)
    local_mask = (frame_ids[None, :] < lengths[:, None]).astype(jnp.float32)[:, :, None]
    boundary = jnp.cumsum(durations, axis=1)
    phone = jnp.sum((boundary[:, None, :] <= frame_ids[None, :, None]).astype(jnp.int32), axis=2)
    phone = jnp.minimum(phone, durations.shape[1] - 1)
    start_state = inputs + jax.vmap(take_rows)(encoded, phone)
    mesh_sizes = [(name, lax.axis_size(name)) for name in ("dp", "seq")]
    orders = part_orders(mesh_sizes)
    places = place_maps(orders, mesh_sizes)
    owner = flat_index(mesh_sizes)
    shard_lengths = (res_master.shape[0], tf_master.shape[0])
    window_sizes = [window_rows(size, len(places[0])) for size in shard_lengths]
    gathered = gather_windows(
        orders,
        to_window(res_master, window_sizes[0], owner),
        to_window(tf_master, window_sizes[1], owner),
    )
    (
        convs,
        res_weight,
        time_weight,
        res_small,
        qkv_weight,
        out_weight,
        up_weight,
        down_weight,
        tf_small,
        wide_small,
    ) = assemble_weights(places, shard_lengths, *gathered)
    masked_in = to_utts((start_state * local_mask).astype(jnp.bfloat16))
    grad_ff = to_utts((cotangent * local_mask).astype(jnp.bfloat16))
    lengths = lax.dynamic_slice_in_dim(lengths, seq_index * utt_count, utt_count)
    time_embed = lax.dynamic_slice_in_dim(time_embed, seq_index * utt_count, utt_count)
    time_act = mish_fn(time_embed).astype(jnp.bfloat16)
    time_proj = jnp.dot(time_act, time_weight, preferred_element_type=jnp.float32) + res_small[7]
    weights = (
        convs,
        res_weight,
        res_small,
        qkv_weight,
        out_weight,
        up_weight,
        down_weight,
        tf_small,
        wide_small,
    )
    (
        final,
        grad_inputs,
        grad_time_proj,
        grad_convs,
        grad_res_w,
        grad_rows,
        *tf_grads,
    ) = whole_step(lengths, masked_in, grad_ff, time_proj[:, None, :], weights)
    grad_time_w = jnp.dot(
        time_act.astype(jnp.float32).T, grad_time_proj[:, 0], precision=lax.Precision.HIGHEST
    )
    grads = (grad_convs, grad_res_w, grad_time_w, grad_rows, *tf_grads)
    summed = reduce_windows(orders, *cut_grads(places, shard_lengths, window_sizes, grads))
    res_share = from_window(summed[0], shard_lengths[0], owner)
    tf_share = from_window(summed[1], shard_lengths[1], owner)
    tokens_total = utts_here * key_total * lax.axis_size("dp")
    rate = LEARN_BASE / math.sqrt(tokens_total)
    res_new, res_moment_new, res_average_new, res_low = update(
        res_master, res_moment, res_average, res_share, rate
    )
    tf_new, tf_moment_new, tf_average_new, tf_low = update(
        tf_master, tf_moment, tf_average, tf_share, rate
    )
    return (
        to_frames(final),
        to_frames(grad_inputs),
        res_share,
        tf_share,
        res_new,
        tf_new,
        res_moment_new,
        tf_moment_new,
        res_average_new,
        tf_average_new,
        res_low,
        tf_low,
    )


def solution(mesh):
    placed = (
        P("dp", "seq", None),
        P("dp", None, None),
        P("dp", None),
        P("dp"),
        P("dp", None),
        P("dp", "seq", None),
        P(("dp", "seq")),
        P(("dp", "seq")),
        P(("dp", "seq")),
        P(("dp", "seq")),
        P(("dp", "seq")),
        P(("dp", "seq")),
    )
    return jax.shard_map(
        per_device,
        mesh=mesh,
        in_specs=placed,
        out_specs=(
            P("dp", "seq", None),
            P("dp", "seq", None),
            P(("dp", "seq")),
            P(("dp", "seq")),
            P(("dp", "seq")),
            P(("dp", "seq")),
            P(("dp", "seq")),
            P(("dp", "seq")),
            P(("dp", "seq")),
            P(("dp", "seq")),
            P(("dp", "seq")),
            P(("dp", "seq")),
        ),
        check_vma=False,
    )
```

```python
import functools
import math

import jax
import jax.numpy as jnp
from jax import lax
from jax.experimental import pallas as pl
from jax.experimental.pallas import tpu as pltpu
from jax.sharding import PartitionSpec as P

C = 256
GROUPS = 8
TE = 1024
HEADS = 2
HD = 64
F = 1024


EPSILON = 1e-05
SCORE_SCALE = 0.125
MOMENTUM = 0.9
AVERAGE_DECAY = 0.99
LEARN_BASE = 0.015
MASK_FILL = -1e30


def soft_plus(signal):
    return jnp.log1p(jnp.exp(-jnp.abs(signal))) + jnp.maximum(signal, 0.0)


def mish_fn(signal):
    return signal * jnp.tanh(soft_plus(signal))


def snake_fn(signal, alpha_row, beta_row):
    return signal + jnp.sin(signal * jnp.exp(alpha_row)) ** 2 / (jnp.exp(beta_row) + 1e-09)


def layer_norm(signal, gain_row, shift_row):
    center = signal - jnp.mean(signal, axis=-1, keepdims=True)
    spread = jnp.mean(center * center, axis=-1, keepdims=True)
    return center * lax.rsqrt(spread + EPSILON) * gain_row + shift_row


def take_rows(phone_table, phone_rows):
    return phone_table[phone_rows]


def rim_pad(signal):
    return jnp.pad(signal, ((0, 0), (1, 1), (0, 0)))


def conv_apply(padded, weight):
    length_here = padded.shape[1] - 2
    result = jnp.dot(padded[:, 0:length_here], weight[0], preferred_element_type=jnp.float32)
    result = result + jnp.dot(
        padded[:, 1 : length_here + 1], weight[1], preferred_element_type=jnp.float32
    )
    return result + jnp.dot(padded[:, 2:], weight[2], preferred_element_type=jnp.float32)


def conv_weight_grad(padded, grad_low):
    length_here = grad_low.shape[1]
    return jnp.stack(
        [
            jnp.einsum(
                "utc,utd->cd",
                padded[:, tap_index : tap_index + length_here],
                grad_low,
                preferred_element_type=jnp.float32,
            )
            for tap_index in range(3)
        ]
    )


def conv_input_grad(grad_low, weight):
    padded = rim_pad(grad_low)
    length_here = grad_low.shape[1]
    result = jnp.einsum("utd,cd->utc", padded[:, 2:], weight[0], preferred_element_type=jnp.float32)
    result = result + jnp.einsum(
        "utd,cd->utc", padded[:, 1 : length_here + 1], weight[1], preferred_element_type=jnp.float32
    )
    return result + jnp.einsum(
        "utd,cd->utc", padded[:, 0:length_here], weight[2], preferred_element_type=jnp.float32
    )


def norm_forward(signal, frame_mask, valid_count, gain_row, shift_row):
    width = C // GROUPS
    shape_now = signal.shape
    grouped = (signal * frame_mask[:, :, None]).reshape(shape_now[0], shape_now[1], GROUPS, width)
    total = jnp.sum(grouped, axis=(1, 3))
    squares = jnp.sum(grouped * grouped, axis=(1, 3))
    number = valid_count[:, None] * width
    mean_now = total / number
    inv_std = lax.rsqrt(squares / number - mean_now * mean_now + EPSILON)
    mean_wide = jnp.repeat(mean_now, width, axis=1)[:, None, :]
    inv_wide = jnp.repeat(inv_std, width, axis=1)[:, None, :]
    normed = (signal - mean_wide) * inv_wide
    return (normed * gain_row + shift_row, normed, inv_wide)


def norm_backward(grad_out, normed, inv_wide, frame_mask, valid_count, gain_row):
    width = C // GROUPS
    shape_now = grad_out.shape
    grad_norm = grad_out * gain_row
    first_sum = jnp.sum(grad_norm.reshape(shape_now[0], shape_now[1], GROUPS, width), axis=(1, 3))
    second_sum = jnp.sum(
        (grad_norm * normed).reshape(shape_now[0], shape_now[1], GROUPS, width), axis=(1, 3)
    )
    number = valid_count[:, None] * width
    first_wide = jnp.repeat(first_sum / number, width, axis=1)[:, None, :]
    second_wide = jnp.repeat(second_sum / number, width, axis=1)[:, None, :]
    grad_signal = inv_wide * (
        grad_norm - frame_mask[:, :, None] * (first_wide + normed * second_wide)
    )
    grad_gain = jnp.sum(grad_out * normed, axis=(0, 1))
    grad_shift = jnp.sum(grad_out, axis=(0, 1))
    return (grad_signal, grad_gain, grad_shift)


def update(master, moment, average, grad, rate):
    moment_new = MOMENTUM * moment + grad
    master_new = master - rate * (grad + MOMENTUM * moment_new)
    average_new = AVERAGE_DECAY * average + (1.0 - AVERAGE_DECAY) * master_new
    return (master_new, moment_new, average_new, master_new.astype(jnp.bfloat16))


def axis_bits(mesh_sizes):
    bits = []
    for name, size in mesh_sizes:
        weight = size // 2
        while weight >= 1:
            bits.append((name, weight))
            weight //= 2
    return bits


def part_orders(mesh_sizes):
    first = axis_bits(mesh_sizes)
    second = list(first)
    if len(second) >= 3:
        second[-3], second[-2] = second[-2], second[-3]
    return (first, second)


def owner_place(order, mesh_sizes, owner):
    strides, stride = {}, 1
    for name, size in reversed(mesh_sizes):
        strides[name] = (stride, size)
        stride *= size
    place = 0
    for step, (name, weight) in enumerate(order):
        base, size = strides[name]
        place += ((owner // base) % size // weight % 2) << step
    return place


def window_rows(length_now, count):
    most = max((i * length_now) % 128 + length_now for i in range(count))
    return -(-most // (128 * 16)) * 16


def bit_of(name, weight):
    return (lax.axis_index(name) // weight) % 2


def partner_of(name, weight):
    return {name: lax.axis_index(name) + (1 - 2 * bit_of(name, weight)) * weight}


def greet(orders):
    barrier = pltpu.get_barrier_semaphore()
    for name, weight in orders[0]:
        pl.semaphore_signal(
            barrier,
            inc=1,
            device_id=partner_of(name, weight),
            device_id_type=pl.DeviceIdType.MESH,
        )
    pl.semaphore_wait(barrier, len(orders[0]))


def gather_kernel(orders, in_a, in_b, out_a, out_b, local_sem, send_sem, recv_sem):
    ins, outs = (in_a, in_b), (out_a, out_b)
    stage_count = len(orders[0])
    offsets = []
    for part in range(2):
        offset = 0
        for step, (name, weight) in enumerate(orders[part]):
            offset = offset + bit_of(name, weight) * (1 << step)
        offsets.append(offset)
    locals_now = [
        pltpu.make_async_copy(ins[part], outs[part].at[offsets[part]], local_sem.at[part])
        for part in range(2)
    ]
    for copy in locals_now:
        copy.start()
    greet(orders)
    for copy in locals_now:
        copy.wait()
    copies = []
    for step in range(stage_count):
        held = 1 << step
        for part in range(2):
            name, weight = orders[part][step]
            start = offsets[part]
            block = outs[part].at[pl.ds(start, held)]
            copy = pltpu.make_async_remote_copy(
                src_ref=block,
                dst_ref=block,
                send_sem=send_sem.at[part, step],
                recv_sem=recv_sem.at[part, step],
                device_id=partner_of(name, weight),
                device_id_type=pl.DeviceIdType.MESH,
            )
            copy.start()
            copies.append(copy)
        for part in range(2):
            copies[2 * step + part].wait_recv()
            name, weight = orders[part][step]
            offsets[part] = offsets[part] - bit_of(name, weight) * held
    for copy in copies:
        copy.wait_send()


def gather_windows(orders, win_a, win_b):
    count = 1 << len(orders[0])
    stages = len(orders[0])
    return pl.pallas_call(
        functools.partial(gather_kernel, orders),
        out_shape=(
            jax.ShapeDtypeStruct((count,) + win_a.shape, win_a.dtype),
            jax.ShapeDtypeStruct((count,) + win_b.shape, win_b.dtype),
        ),
        in_specs=[pl.BlockSpec(memory_space=pltpu.VMEM)] * 2,
        out_specs=[pl.BlockSpec(memory_space=pltpu.VMEM)] * 2,
        scratch_shapes=[
            pltpu.SemaphoreType.DMA((2,)),
            pltpu.SemaphoreType.DMA((2, stages)),
            pltpu.SemaphoreType.DMA((2, stages)),
        ],
        compiler_params=pltpu.CompilerParams(
            collective_id=0, has_side_effects=True, vmem_limit_bytes=32 * 1024 * 1024
        ),
    )(win_a, win_b)


def reduce_kernel(orders, in_a, in_b, out_a, out_b, land_a, land_b, send_sem, recv_sem):
    ins, outs, lands = (in_a, in_b), (out_a, out_b), (land_a, land_b)
    stage_count = len(orders[0])
    greet(orders)
    copies = []

    def source(part, step, keep):
        name, weight = orders[part][stage_count - 1 - step]
        held = 1 << (stage_count - 1 - step)
        side = bit_of(name, weight)
        side = side if keep else 1 - side
        if step == 0:
            return ins[part].at[pl.ds(side * held, held)]
        base = (1 << stage_count) - (1 << (stage_count - step + 1))
        return lands[part].at[pl.ds(base + side * held, held)]

    for step in range(stage_count):
        held = 1 << (stage_count - 1 - step)
        base = (1 << stage_count) - (1 << (stage_count - step))
        for part in range(2):
            name, weight = orders[part][stage_count - 1 - step]
            copy = pltpu.make_async_remote_copy(
                src_ref=source(part, step, False),
                dst_ref=lands[part].at[pl.ds(base, held)],
                send_sem=send_sem.at[part, step],
                recv_sem=recv_sem.at[part, step],
                device_id=partner_of(name, weight),
                device_id_type=pl.DeviceIdType.MESH,
            )
            copy.start()
            copies.append(copy)
        for part in range(2):
            copies[2 * step + part].wait_recv()
            mine = source(part, step, True)
            if step == stage_count - 1:
                outs[part][...] = mine[0].astype(jnp.float32) + lands[part][base].astype(
                    jnp.float32
                )
            else:

                def add_one(index, carry, mine=mine, part=part, base=base):
                    land = lands[part].at[base + index]
                    total = mine[index].astype(jnp.float32) + land[...].astype(jnp.float32)
                    land[...] = total.astype(land.dtype)
                    return carry

                lax.fori_loop(0, held, add_one, 0)
    for copy in copies:
        copy.wait_send()


def reduce_windows(orders, rows_a, rows_b):
    count = 1 << len(orders[0])
    stages = len(orders[0])
    return pl.pallas_call(
        functools.partial(reduce_kernel, orders),
        out_shape=(
            jax.ShapeDtypeStruct(rows_a.shape[1:], jnp.float32),
            jax.ShapeDtypeStruct(rows_b.shape[1:], jnp.float32),
        ),
        in_specs=[pl.BlockSpec(memory_space=pltpu.VMEM)] * 2,
        out_specs=[pl.BlockSpec(memory_space=pltpu.VMEM)] * 2,
        scratch_shapes=[
            pltpu.VMEM((count - 1,) + rows_a.shape[1:], rows_a.dtype),
            pltpu.VMEM((count - 1,) + rows_b.shape[1:], rows_b.dtype),
            pltpu.SemaphoreType.DMA((2, stages)),
            pltpu.SemaphoreType.DMA((2, stages)),
        ],
        compiler_params=pltpu.CompilerParams(
            collective_id=1, has_side_effects=True, vmem_limit_bytes=32 * 1024 * 1024
        ),
    )(rows_a, rows_b)


RES_SQUARES = 7 * C * C
RES_ROWS = (RES_SQUARES + TE * C + 8 * C) // 128
INNER = HEADS * HD
TF_SIZES = (3 * C * INNER, INNER * C, C * F, F * C, 6 * C, 3 * F)
TF_ROWS = sum(TF_SIZES) // 128


def place_maps(orders, mesh_sizes):
    count = 1 << len(orders[0])
    return [[owner_place(orders[part], mesh_sizes, i) for i in range(count)] for part in range(2)]


def matrix_views():
    views = []
    row = 0
    for rows, width in ((6 * C, C), (C, C), (TE, C), (8, C)):
        views.append((0, row, rows, width))
        row += rows * width // 128
    row = 0
    for rows, width in ((C, 3 * INNER), (INNER, C), (C, F), (F, C), (6, C), (3, F)):
        views.append((1, row, rows, width))
        row += rows * width // 128
    return views


def assemble_kernel(places, lengths_now, in_a, in_b, *refs):
    outs, flats = refs[:10], refs[10:12]
    count = len(places[0])
    for part, ref in enumerate((in_a, in_b)):
        flat = flats[part]
        for i in range(count):
            start, lead = divmod(i * lengths_now[part], 128)
            rows = -(-(lead + lengths_now[part]) // 128)
            if lead:
                edge = flat[start : start + 1, :]
            flat[start : start + rows, :] = ref[places[part][i]].astype(jnp.float32)[:rows]
            if lead:
                flat[start : start + 1, :] = flat[start : start + 1, :] + edge
    for out, (part, row, rows, width) in zip(outs, matrix_views()):
        stride = width // 128
        for lane in range(stride):
            piece = flats[part][pl.ds(row + lane, rows, stride=stride), :]
            out[:, lane * 128 : (lane + 1) * 128] = piece.astype(out.dtype)


def assemble_weights(places, lengths_now, win_a, win_b):
    shapes = []
    for index, (part, row, rows, width) in enumerate(matrix_views()):
        kind = jnp.float32 if index in (3, 8, 9) else jnp.bfloat16
        shapes.append(jax.ShapeDtypeStruct((rows, width), kind))
    return pl.pallas_call(
        functools.partial(assemble_kernel, places, lengths_now),
        out_shape=shapes,
        in_specs=[pl.BlockSpec(memory_space=pltpu.VMEM)] * 2,
        out_specs=[pl.BlockSpec(memory_space=pltpu.VMEM)] * 10,
        scratch_shapes=[
            pltpu.VMEM((RES_ROWS + 8, 128), jnp.float32),
            pltpu.VMEM((TF_ROWS + 12, 128), jnp.float32),
        ],
        compiler_params=pltpu.CompilerParams(vmem_limit_bytes=32 * 1024 * 1024),
    )(win_a, win_b)


def cut_kernel(places, lengths_now, *refs):
    ins, outs, flats = refs[:10], refs[10:12], refs[12:14]
    count = len(places[0])
    for ref, (part, row, rows, width) in zip(ins, matrix_views()):
        stride = width // 128
        for lane in range(stride):
            flats[part][pl.ds(row + lane, rows, stride=stride), :] = ref[
                :, lane * 128 : (lane + 1) * 128
            ]
    for part in range(2):
        for i in range(count):
            start, lead = divmod(i * lengths_now[part], 128)
            rows = outs[part].shape[1]
            outs[part][places[part][i]] = flats[part][start : start + rows, :].astype(
                outs[part].dtype
            )


def cut_grads(places, lengths_now, window_sizes, grads):
    count = len(places[0])
    return pl.pallas_call(
        functools.partial(cut_kernel, places, lengths_now),
        out_shape=[
            jax.ShapeDtypeStruct((count, rows, 128), jnp.bfloat16) for rows in window_sizes
        ],
        in_specs=[pl.BlockSpec(memory_space=pltpu.VMEM)] * 10,
        out_specs=[pl.BlockSpec(memory_space=pltpu.VMEM)] * 2,
        scratch_shapes=[
            pltpu.VMEM((RES_ROWS + 24, 128), jnp.float32),
            pltpu.VMEM((TF_ROWS + 28, 128), jnp.float32),
        ],
        compiler_params=pltpu.CompilerParams(vmem_limit_bytes=40 * 1024 * 1024),
    )(*grads)


def flat_index(mesh_sizes):
    index = 0
    for name, size in mesh_sizes:
        index = index * size + lax.axis_index(name)
    return index


def to_window(master, rows, owner):
    lead = (owner * master.shape[0]) % 128
    window = jnp.zeros((rows * 128,), jnp.bfloat16)
    return lax.dynamic_update_slice(window, master.astype(jnp.bfloat16), (lead,)).reshape(rows, 128)


def from_window(window, length_now, owner):
    lead = (owner * length_now) % 128
    return lax.dynamic_slice(window.reshape(-1), (lead,), (length_now,))


def exchange(cells):
    return lax.all_to_all(cells, "seq", split_axis=0, concat_axis=0)


SIN_TERMS = (
    0.9999999956945583,
    -0.1666665793542191,
    0.008333049779226345,
    -0.00019808982984063025,
    2.605019582312477e-06,
)
COS_TERMS = (
    0.9999999997785896,
    -0.4999999935376167,
    0.04166663608814044,
    -0.0013888359276781354,
    2.47600539678114e-05,
    -2.6049608156992194e-07,
)
PI_PARTS = (3.140625, 0.0009670257568359375, 6.27832957178498e-07)
ROUND_SHIFT = 12582912.0


def mm(left, right):
    return jnp.dot(left, right, preferred_element_type=jnp.float32)


def mm_right(left, right):
    return lax.dot_general(
        left, right, (((1,), (1,)), ((), ())), preferred_element_type=jnp.float32
    )


def mm_left(left, right):
    return lax.dot_general(
        left, right, (((0,), (0,)), ((), ())), preferred_element_type=jnp.float32
    )


def column_sum(cells):
    return jnp.sum(cells, axis=0, keepdims=True)


def sin_cos(angle):
    turns = (angle * (1.0 / math.pi) + ROUND_SHIFT) - ROUND_SHIFT
    rest = angle - turns * PI_PARTS[0]
    rest = rest - turns * PI_PARTS[1]
    rest = rest - turns * PI_PARTS[2]
    square = rest * rest
    sine = SIN_TERMS[-1]
    for term in SIN_TERMS[-2::-1]:
        sine = sine * square + term
    cosine = COS_TERMS[-1]
    for term in COS_TERMS[-2::-1]:
        cosine = cosine * square + term
    return (sine * rest, cosine)


def mish_value(signal):
    expo = jnp.exp(jnp.minimum(signal, 20.0))
    upper = expo * (expo + 2.0)
    return signal * (upper / (upper + 2.0))


def mish_slope(signal):
    expo = jnp.exp(jnp.minimum(signal, 20.0))
    upper = expo * (expo + 2.0)
    inverse = 1.0 / (upper + 2.0)
    return upper * inverse + signal * (4.0 * expo * (1.0 + expo)) * (inverse * inverse)


def row_norm(signal):
    center = signal - jnp.mean(signal, axis=-1, keepdims=True)
    spread = jnp.mean(center * center, axis=-1, keepdims=True)
    inverse = lax.rsqrt(spread + EPSILON)
    return (center * inverse, inverse)


def row_norm_back(grad_out, normed, inverse, gain_row):
    inner_grad = grad_out * gain_row
    first = jnp.mean(inner_grad, axis=-1, keepdims=True)
    second = jnp.mean(inner_grad * normed, axis=-1, keepdims=True)
    return (inner_grad - first - normed * second) * inverse


def step_kernel(
    lengths_ref,
    cells_ref,
    time_ref,
    convs_ref,
    res_ref,
    rows_ref,
    qkv_ref,
    out_ref,
    up_ref,
    down_ref,
    tf_rows_ref,
    wide_ref,
    results_ref,
    gtime_ref,
    gconvs_ref,
    gres_ref,
    grows_ref,
    gqkv_ref,
    gout_ref,
    gup_ref,
    gdown_ref,
    gtf_ref,
    gwide_ref,
    pad,
    col_one,
    col_two,
    col_grad,
    z_one,
    z_two,
    block,
    grad_mid,
    grad_norm,
    attn_in,
    heads_q,
    heads_k,
    heads_v,
    heads_g,
    attn_vals,
    probs,
    snake,
    grad_up,
    ff_in,
    grad_attn,
    grad_key,
    grad_value,
    grad_query,
    grad_qkv,
    grad_skip,
):
    frames = z_one.shape[0]
    tiles, _, tile, _ = cells_ref.shape
    utt = pl.program_id(0)
    length_now = lengths_ref[utt]
    number = length_now.astype(jnp.float32) * (C // GROUPS)

    @pl.when(utt == 0)
    def clear():
        for ref in (
            gconvs_ref,
            gres_ref,
            grows_ref,
            gqkv_ref,
            gout_ref,
            gup_ref,
            gdown_ref,
            gtf_ref,
            gwide_ref,
        ):
            ref[...] = jnp.zeros_like(ref)

    edge = jnp.zeros((8, C), jnp.float32)
    pad[0:8, :] = edge
    pad[frames + 8 : frames + 16, :] = edge
    gtime_ref[...] = jnp.zeros_like(gtime_ref)
    group_row = lax.broadcasted_iota(jnp.int32, (C, C), 0) // (C // GROUPS)
    group_column = lax.broadcasted_iota(jnp.int32, (C, C), 1) // (C // GROUPS)
    group_ones = (group_row == group_column).astype(jnp.float32)
    lane = lax.broadcasted_iota(jnp.int32, (1, INNER), 1) // HD
    head_masks = [(lane == head).astype(jnp.float32) for head in range(HEADS)]
    key_bias = jnp.where(
        lax.broadcasted_iota(jnp.int32, (1, frames), 1) < length_now, 0.0, MASK_FILL
    )

    def rows_at(index, lead=0):
        return pl.ds(pl.multiple_of(index * tile + lead, 8), tile)

    def tile_mask(index):
        ids = lax.broadcasted_iota(jnp.int32, (tile, 1), 0) + index * tile
        return (ids < length_now).astype(jnp.float32)

    def group_sum(row):
        wide = jnp.broadcast_to(row, (8, C))
        return jnp.dot(
            wide,
            group_ones,
            precision=lax.Precision.HIGHEST,
            preferred_element_type=jnp.float32,
        )[0:1]

    def build_columns(target):
        for index in range(tiles):
            start = index * tile
            for tap in range(3):
                piece = pad[start + 7 + tap : start + 7 + tap + tile, :]
                target[start : start + tile, tap * C : (tap + 1) * C] = piece.astype(jnp.bfloat16)

    def loop(body):
        def wrapped(index, carry):
            body(index)
            return carry

        lax.fori_loop(0, tiles, wrapped, 0)

    def conv_stage(columns, base, bias_at, target):
        def one(index, carry):
            rows = rows_at(index)
            cells = mm(columns[rows, :], convs_ref[base : base + 3 * C, :])
            cells = cells + rows_ref[bias_at : bias_at + 1, :]
            target[rows, :] = cells
            masked = cells * tile_mask(index)
            return (carry[0] + column_sum(masked), carry[1] + column_sum(masked * masked))

        zero = jnp.zeros((1, C), jnp.float32)
        total, squares = lax.fori_loop(0, tiles, one, (zero, zero))
        mean_row = group_sum(total) / number
        inv_row = lax.rsqrt(group_sum(squares) / number - mean_row * mean_row + EPSILON)
        return (mean_row, inv_row)

    def copy_in(index):
        pad[rows_at(index, 8), :] = cells_ref[index, 0, :, 0:C].astype(jnp.float32)

    loop(copy_in)
    build_columns(col_one)
    mean_one, inv_one = conv_stage(col_one, 0, 0, z_one)

    def hidden(index):
        normed = (z_one[rows_at(index), :] - mean_one) * inv_one
        act = mish_value(normed * rows_ref[1:2, :] + rows_ref[2:3, :])
        pad[rows_at(index, 8), :] = (act + time_ref[0]) * tile_mask(index)

    loop(hidden)
    build_columns(col_two)
    mean_two, inv_two = conv_stage(col_two, 3 * C, 3, z_two)

    def enter(index):
        rows = rows_at(index)
        normed = (z_two[rows, :] - mean_two) * inv_two
        act = mish_value(normed * rows_ref[4:5, :] + rows_ref[5:6, :]) * tile_mask(index)
        state = act + mm(cells_ref[index, 0, :, 0:C], res_ref[...]) + rows_ref[6:7, :]
        block[rows, :] = state
        normed, _ = row_norm(state)
        low = (normed * tf_rows_ref[0:1, :] + tf_rows_ref[1:2, :]).astype(jnp.bfloat16)
        attn_in[rows, :] = low
        parts = mm(low, qkv_ref[...]).astype(jnp.bfloat16).astype(jnp.float32)
        query = parts[:, :INNER] * SCORE_SCALE
        for head in range(HEADS):
            heads_q[head, rows, :] = (query * head_masks[head]).astype(jnp.bfloat16)
            heads_k[head, rows, :] = (parts[:, INNER : 2 * INNER] * head_masks[head]).astype(
                jnp.bfloat16
            )
            heads_v[head, rows, :] = (parts[:, 2 * INNER :] * head_masks[head]).astype(
                jnp.bfloat16
            )

    loop(enter)

    def attend(index):
        rows = rows_at(index)
        total = jnp.zeros((tile, INNER), jnp.float32)
        for head in range(HEADS):
            scores = mm_right(heads_q[head, rows, :], heads_k[head]) + key_bias
            expo = jnp.exp(scores - jnp.max(scores, axis=-1, keepdims=True))
            chance = expo * (1.0 / jnp.sum(expo, axis=-1, keepdims=True))
            probs[head, rows, :] = chance
            total = total + mm(chance.astype(jnp.bfloat16), heads_v[head])
        attn_vals[rows, :] = total.astype(jnp.bfloat16)

    loop(attend)

    def feed(index):
        rows = rows_at(index)
        mid = block[rows, :] + mm(attn_vals[rows, :], out_ref[...]) + tf_rows_ref[2:3, :]
        normed, inverse = row_norm(mid)
        low = (normed * tf_rows_ref[3:4, :] + tf_rows_ref[4:5, :]).astype(jnp.bfloat16)
        ff_in[rows, :] = low
        grad_low = cells_ref[index, 0, :, C : 2 * C]
        result = jnp.zeros((tile, C), jnp.float32)
        grad_in = jnp.zeros((tile, C), jnp.float32)
        for chunk in range(F // 256):
            lanes = slice(chunk * 256, (chunk + 1) * 256)
            up_out = mm(low, up_ref[:, lanes]) + wide_ref[0:1, lanes]
            grad_snake = mm_right(grad_low, down_ref[lanes, :])
            speed = jnp.exp(wide_ref[1:2, lanes])
            depth = 1.0 / (jnp.exp(wide_ref[2:3, lanes]) + 1e-09)
            angle = up_out * speed
            sine, cosine = sin_cos(angle)
            square = sine * sine
            value = (up_out + square * depth).astype(jnp.bfloat16)
            snake[rows, lanes] = value
            result = result + mm(value, down_ref[lanes, :])
            slope = grad_snake * ((2.0 * sine) * cosine) * depth
            grad_here = (grad_snake + slope * speed).astype(jnp.bfloat16)
            grad_up[rows, lanes] = grad_here
            grad_in = grad_in + mm_right(grad_here, up_ref[:, lanes])
            gwide_ref[0:1, lanes] += column_sum(grad_here.astype(jnp.float32))
            gwide_ref[1:2, lanes] += column_sum(slope * angle)
            gwide_ref[2:3, lanes] += column_sum(grad_snake * square)
        results_ref[index, 0, :, 0:C] = ((mid + result + tf_rows_ref[5:6, :]) * tile_mask(index)).astype(
            jnp.bfloat16
        )
        grad_wide = grad_low.astype(jnp.float32)
        gtf_ref[5:6, :] += column_sum(grad_wide)
        gtf_ref[3:4, :] += column_sum(grad_in * normed)
        gtf_ref[4:5, :] += column_sum(grad_in)
        grad_state = grad_wide + row_norm_back(grad_in, normed, inverse, tf_rows_ref[3:4, :])
        grad_mid[rows, :] = grad_state
        grad_state = grad_state.astype(jnp.bfloat16)
        grad_attn[rows, :] = grad_state
        gtf_ref[2:3, :] += column_sum(grad_state.astype(jnp.float32))
        grad_vals = mm_right(grad_state, out_ref[...]).astype(jnp.bfloat16).astype(jnp.float32)
        for head in range(HEADS):
            heads_g[head, rows, :] = (grad_vals * head_masks[head]).astype(jnp.bfloat16)

    loop(feed)

    def feed_weights(index, carry):
        lanes = pl.ds(pl.multiple_of(index * 256, 256), 256)
        grads = cells_ref[:, 0, :, C : 2 * C].reshape(frames, C)
        gdown_ref[lanes, :] += mm_left(snake[:, lanes], grads)
        gup_ref[:, lanes] += mm_left(ff_in[...], grad_up[:, lanes])
        return carry

    lax.fori_loop(0, F // 256, feed_weights, 0)
    gout_ref[...] += mm_left(attn_vals[...], grad_attn[...])
    grad_key[...] = jnp.zeros_like(grad_key)
    grad_value[...] = jnp.zeros_like(grad_value)

    def attend_back(index):
        rows = rows_at(index)
        total = jnp.zeros((tile, INNER), jnp.float32)
        for head in range(HEADS):
            grad_out = heads_g[head, rows, :]
            chance = probs[head, rows, :]
            grad_probs = mm_right(grad_out, heads_v[head])
            dot_row = jnp.sum(chance * grad_probs, axis=-1, keepdims=True)
            grad_scores = (chance * (grad_probs - dot_row)).astype(jnp.bfloat16)
            total = total + mm(grad_scores, heads_k[head])
            grad_key[...] += mm_left(grad_scores, heads_q[head, rows, :])
            grad_value[...] += mm_left(chance.astype(jnp.bfloat16), grad_out)
        grad_query[rows, :] = total * SCORE_SCALE

    loop(attend_back)

    def leave(index, carry):
        rows = rows_at(index)
        grad_qkv[rows, 0:INNER] = grad_query[rows, :].astype(jnp.bfloat16)
        grad_qkv[rows, INNER : 2 * INNER] = grad_key[rows, :].astype(jnp.bfloat16)
        grad_qkv[rows, 2 * INNER : 3 * INNER] = grad_value[rows, :].astype(jnp.bfloat16)
        grad_in = mm_right(grad_qkv[rows, :], qkv_ref[...])
        normed, inverse = row_norm(block[rows, :])
        gtf_ref[0:1, :] += column_sum(grad_in * normed)
        gtf_ref[1:2, :] += column_sum(grad_in)
        grad_state = grad_mid[rows, :] + row_norm_back(
            grad_in, normed, inverse, tf_rows_ref[0:1, :]
        )
        low = grad_state.astype(jnp.bfloat16)
        grad_skip[rows, :] = low
        grows_ref[6:7, :] += column_sum(low.astype(jnp.float32))
        normed = (z_two[rows, :] - mean_two) * inv_two
        grad_here = (
            mish_slope(normed * rows_ref[4:5, :] + rows_ref[5:6, :])
            * tile_mask(index)
            * grad_state
        )
        grad_norm[rows, :] = grad_here
        return (carry[0] + column_sum(grad_here), carry[1] + column_sum(grad_here * normed))

    zero = jnp.zeros((1, C), jnp.float32)

    def norm_back(target, mean_row, inv_row, gain_at, bias_at, shift_sum, gain_sum):
        gain_row = rows_ref[gain_at : gain_at + 1, :]
        grows_ref[gain_at : gain_at + 1, :] += gain_sum
        grows_ref[gain_at + 1 : gain_at + 2, :] += shift_sum
        first = group_sum(shift_sum * gain_row) / number
        second = group_sum(gain_sum * gain_row) / number

        def one(index):
            rows = rows_at(index)
            normed = (target[rows, :] - mean_row) * inv_row
            cells = inv_row * (
                grad_norm[rows, :] * gain_row - tile_mask(index) * (first + normed * second)
            )
            cells = cells.astype(jnp.bfloat16).astype(jnp.float32)
            grows_ref[bias_at : bias_at + 1, :] += column_sum(cells)
            pad[rows_at(index, 8), :] = cells

        loop(one)
        build_columns(col_grad)

    def conv_back(rows, base):
        total = mm_right(col_grad[rows, 2 * C : 3 * C], convs_ref[base : base + C, :])
        total = total + mm_right(col_grad[rows, C : 2 * C], convs_ref[base + C : base + 2 * C, :])
        return total + mm_right(col_grad[rows, 0:C], convs_ref[base + 2 * C : base + 3 * C, :])

    def conv_weights(columns, base):
        for tap in range(3):
            gconvs_ref[base + tap * C : base + (tap + 1) * C, :] += mm_left(
                columns[:, tap * C : (tap + 1) * C], col_grad[:, C : 2 * C]
            )

    shift_sum, gain_sum = lax.fori_loop(0, tiles, leave, (zero, zero))
    norm_back(z_two, mean_two, inv_two, 4, 3, shift_sum, gain_sum)
    conv_weights(col_two, 3 * C)

    def hidden_back(index, carry):
        rows = rows_at(index)
        grad_here = conv_back(rows, 3 * C) * tile_mask(index)
        gtime_ref[0] += column_sum(grad_here)
        normed = (z_one[rows, :] - mean_one) * inv_one
        grad_here = mish_slope(normed * rows_ref[1:2, :] + rows_ref[2:3, :]) * grad_here
        grad_norm[rows, :] = grad_here
        return (carry[0] + column_sum(grad_here), carry[1] + column_sum(grad_here * normed))

    shift_sum, gain_sum = lax.fori_loop(0, tiles, hidden_back, (zero, zero))
    grows_ref[7:8, :] += gtime_ref[0]
    norm_back(z_one, mean_one, inv_one, 1, 0, shift_sum, gain_sum)
    conv_weights(col_one, 0)

    def finish(index):
        rows = rows_at(index)
        total = conv_back(rows, 0) + mm_right(grad_skip[rows, :], res_ref[...])
        results_ref[index, 0, :, C : 2 * C] = (total * tile_mask(index)).astype(jnp.bfloat16)

    loop(finish)
    gres_ref[...] += mm_left(cells_ref[:, 0, :, 0:C].reshape(frames, C), grad_skip[...])
    gqkv_ref[...] += mm_left(attn_in[...], grad_qkv[...])

    @pl.when(utt == pl.num_programs(0) - 1)
    def scale_rows():
        low_side = jnp.exp(wide_ref[2:3, :])
        depth = 1.0 / (low_side + 1e-09)
        gwide_ref[2:3, :] = -gwide_ref[2:3, :] * low_side * depth * depth


def whole_step(lengths, cells, time_proj, weights):
    (convs, res_weight, rows, qkv_weight, out_weight, up_weight, down_weight, tf_rows, wide) = weights
    tiles, utts, tile, _ = cells.shape
    frames = tiles * tile
    by_utt = pl.BlockSpec((tiles, 1, tile, 2 * C), lambda u, s: (0, u, 0, 0))
    row_by_utt = pl.BlockSpec((1, 1, C), lambda u, s: (u, 0, 0))

    def fixed(array):
        return pl.BlockSpec(array.shape, lambda u, s: (0, 0))

    f32, low = jnp.float32, jnp.bfloat16
    scratch = [
        ((frames + 16, C), f32),
        ((frames, 3 * C), low),
        ((frames, 3 * C), low),
        ((frames, 3 * C), low),
        ((frames, C), f32),
        ((frames, C), f32),
        ((frames, C), f32),
        ((frames, C), f32),
        ((frames, C), f32),
        ((frames, C), low),
        ((HEADS, frames, INNER), low),
        ((HEADS, frames, INNER), low),
        ((HEADS, frames, INNER), low),
        ((HEADS, frames, INNER), low),
        ((frames, INNER), low),
        ((HEADS, frames, frames), f32),
        ((frames, F), low),
        ((frames, F), low),
        ((frames, C), low),
        ((frames, C), low),
        ((frames, INNER), f32),
        ((frames, INNER), f32),
        ((frames, INNER), f32),
        ((frames, 3 * INNER), low),
        ((frames, C), low),
    ]
    return pl.pallas_call(
        step_kernel,
        grid_spec=pltpu.PrefetchScalarGridSpec(
            num_scalar_prefetch=1,
            grid=(utts,),
            in_specs=[by_utt, row_by_utt] + [fixed(array) for array in weights],
            out_specs=[by_utt, row_by_utt] + [fixed(array) for array in weights],
            scratch_shapes=[pltpu.VMEM(shape, kind) for shape, kind in scratch],
        ),
        out_shape=[
            jax.ShapeDtypeStruct(cells.shape, low),
            jax.ShapeDtypeStruct((utts, 1, C), f32),
        ]
        + [jax.ShapeDtypeStruct(array.shape, f32) for array in weights],
        compiler_params=pltpu.CompilerParams(
            dimension_semantics=("arbitrary",), vmem_limit_bytes=60 * 1024 * 1024
        ),
    )(lengths, cells, time_proj, *weights)


def prepare_kernel(
    lengths_ref, place_ref, inputs_ref, encoded_ref, durations_ref, cotangent_ref, out_ref
):
    frames, phones = inputs_ref.shape[1], durations_ref.shape[2]
    first = place_ref[0] * frames
    durations = durations_ref[0].astype(jnp.float32)
    before = lax.broadcasted_iota(jnp.int32, (phones, phones), 0)
    after = lax.broadcasted_iota(jnp.int32, (phones, phones), 1)
    upper = (before <= after).astype(jnp.bfloat16)
    wide = jnp.broadcast_to(durations, (16, phones)).astype(jnp.bfloat16)
    ends = mm(wide, upper)[0:1]
    starts = ends - durations
    last = lax.broadcasted_iota(jnp.int32, (1, phones), 1) == phones - 1
    ends = jnp.where(last, 1e9, ends)
    ids = lax.broadcasted_iota(jnp.int32, (frames, 1), 0) + first
    times = ids.astype(jnp.float32)
    picked = jnp.where((times >= starts) & (times < ends), 1.0, 0.0).astype(jnp.bfloat16)
    table = encoded_ref[0]
    high = table.astype(jnp.bfloat16)
    rest = table - high.astype(jnp.float32)
    middle = rest.astype(jnp.bfloat16)
    low = (rest - middle.astype(jnp.float32)).astype(jnp.bfloat16)
    rows = (mm(picked, high) + mm(picked, middle)) + mm(picked, low)
    mask = (ids < lengths_ref[pl.program_id(0)]).astype(jnp.float32)
    out_ref[0, 0, :, 0:C] = ((inputs_ref[0] + rows) * mask).astype(jnp.bfloat16)
    out_ref[0, 0, :, C : 2 * C] = (cotangent_ref[0] * mask).astype(jnp.bfloat16)


def prepare(inputs, encoded, durations, lengths, cotangent):
    utts, frames, _ = inputs.shape
    phones = durations.shape[1]
    seq_size = lax.axis_size("seq")
    group = utts // seq_size
    place = jnp.full((1,), lax.axis_index("seq"), jnp.int32)
    by_utt = lambda u, n, p: (u, 0, 0)
    return pl.pallas_call(
        prepare_kernel,
        grid_spec=pltpu.PrefetchScalarGridSpec(
            num_scalar_prefetch=2,
            grid=(utts,),
            in_specs=[
                pl.BlockSpec((1, frames, C), by_utt),
                pl.BlockSpec((1, phones, C), by_utt),
                pl.BlockSpec((1, 1, phones), by_utt),
                pl.BlockSpec((1, frames, C), by_utt),
            ],
            out_specs=pl.BlockSpec(
                (1, 1, frames, 2 * C), lambda u, n, p: (u // group, u % group, 0, 0)
            ),
        ),
        out_shape=jax.ShapeDtypeStruct((seq_size, group, frames, 2 * C), jnp.bfloat16),
        compiler_params=pltpu.CompilerParams(dimension_semantics=("arbitrary",)),
    )(lengths, place, inputs, encoded, durations[:, None, :], cotangent)


def per_device(
    inputs,
    encoded,
    durations,
    lengths,
    time_embed,
    cotangent,
    res_master,
    res_moment,
    res_average,
    tf_master,
    tf_moment,
    tf_average,
):
    utts_here, local_len, _ = inputs.shape
    seq_size = lax.axis_size("seq")
    key_total = local_len * seq_size
    utt_count = utts_here // seq_size
    seq_index = lax.axis_index("seq")
    cells = exchange(prepare(inputs, encoded, durations, lengths, cotangent))
    mesh_sizes = [(name, lax.axis_size(name)) for name in ("dp", "seq")]
    orders = part_orders(mesh_sizes)
    places = place_maps(orders, mesh_sizes)
    owner = flat_index(mesh_sizes)
    shard_lengths = (res_master.shape[0], tf_master.shape[0])
    window_sizes = [window_rows(size, len(places[0])) for size in shard_lengths]
    gathered = gather_windows(
        orders,
        to_window(res_master, window_sizes[0], owner),
        to_window(tf_master, window_sizes[1], owner),
    )
    (
        convs,
        res_weight,
        time_weight,
        res_small,
        qkv_weight,
        out_weight,
        up_weight,
        down_weight,
        tf_small,
        wide_small,
    ) = assemble_weights(places, shard_lengths, *gathered)
    lengths = lax.dynamic_slice_in_dim(lengths, seq_index * utt_count, utt_count)
    time_embed = lax.dynamic_slice_in_dim(time_embed, seq_index * utt_count, utt_count)
    time_act = mish_fn(time_embed).astype(jnp.bfloat16)
    time_proj = jnp.dot(time_act, time_weight, preferred_element_type=jnp.float32) + res_small[7]
    weights = (
        convs,
        res_weight,
        res_small,
        qkv_weight,
        out_weight,
        up_weight,
        down_weight,
        tf_small,
        wide_small,
    )
    (
        results,
        grad_time_proj,
        grad_convs,
        grad_res_w,
        grad_rows,
        *tf_grads,
    ) = whole_step(lengths, cells, time_proj[:, None, :], weights)
    grad_time_w = jnp.dot(
        time_act.astype(jnp.float32).T, grad_time_proj[:, 0], precision=lax.Precision.HIGHEST
    )
    results = exchange(results).reshape(utts_here, local_len, 2 * C)
    grads = (grad_convs, grad_res_w, grad_time_w, grad_rows, *tf_grads)
    summed = reduce_windows(orders, *cut_grads(places, shard_lengths, window_sizes, grads))
    res_share = from_window(summed[0], shard_lengths[0], owner)
    tf_share = from_window(summed[1], shard_lengths[1], owner)
    tokens_total = utts_here * key_total * lax.axis_size("dp")
    rate = LEARN_BASE / math.sqrt(tokens_total)
    res_new, res_moment_new, res_average_new, res_low = update(
        res_master, res_moment, res_average, res_share, rate
    )
    tf_new, tf_moment_new, tf_average_new, tf_low = update(
        tf_master, tf_moment, tf_average, tf_share, rate
    )
    return (
        results[:, :, :C].astype(jnp.float32),
        results[:, :, C:].astype(jnp.float32),
        res_share,
        tf_share,
        res_new,
        tf_new,
        res_moment_new,
        tf_moment_new,
        res_average_new,
        tf_average_new,
        res_low,
        tf_low,
    )


def solution(mesh):
    placed = (
        P("dp", "seq", None),
        P("dp", None, None),
        P("dp", None),
        P("dp"),
        P("dp", None),
        P("dp", "seq", None),
        P(("dp", "seq")),
        P(("dp", "seq")),
        P(("dp", "seq")),
        P(("dp", "seq")),
        P(("dp", "seq")),
        P(("dp", "seq")),
    )
    return jax.shard_map(
        per_device,
        mesh=mesh,
        in_specs=placed,
        out_specs=(
            P("dp", "seq", None),
            P("dp", "seq", None),
            P(("dp", "seq")),
            P(("dp", "seq")),
            P(("dp", "seq")),
            P(("dp", "seq")),
            P(("dp", "seq")),
            P(("dp", "seq")),
            P(("dp", "seq")),
            P(("dp", "seq")),
            P(("dp", "seq")),
            P(("dp", "seq")),
        ),
        check_vma=False,
    )
```

```python
import functools
import math

import jax
import jax.numpy as jnp
from jax import lax
from jax.experimental import pallas as pl
from jax.experimental.pallas import tpu as pltpu
from jax.sharding import PartitionSpec as P

C = 256
GROUPS = 8
TE = 1024
HEADS = 2
HD = 64
F = 1024


EPSILON = 1e-05
SCORE_SCALE = 0.125
MOMENTUM = 0.9
AVERAGE_DECAY = 0.99
LEARN_BASE = 0.015
MASK_FILL = -1e30


def soft_plus(signal):
    return jnp.log1p(jnp.exp(-jnp.abs(signal))) + jnp.maximum(signal, 0.0)


def mish_fn(signal):
    return signal * jnp.tanh(soft_plus(signal))


def snake_fn(signal, alpha_row, beta_row):
    return signal + jnp.sin(signal * jnp.exp(alpha_row)) ** 2 / (jnp.exp(beta_row) + 1e-09)


def layer_norm(signal, gain_row, shift_row):
    center = signal - jnp.mean(signal, axis=-1, keepdims=True)
    spread = jnp.mean(center * center, axis=-1, keepdims=True)
    return center * lax.rsqrt(spread + EPSILON) * gain_row + shift_row


def take_rows(phone_table, phone_rows):
    return phone_table[phone_rows]


def rim_pad(signal):
    return jnp.pad(signal, ((0, 0), (1, 1), (0, 0)))


def conv_apply(padded, weight):
    length_here = padded.shape[1] - 2
    result = jnp.dot(padded[:, 0:length_here], weight[0], preferred_element_type=jnp.float32)
    result = result + jnp.dot(
        padded[:, 1 : length_here + 1], weight[1], preferred_element_type=jnp.float32
    )
    return result + jnp.dot(padded[:, 2:], weight[2], preferred_element_type=jnp.float32)


def conv_weight_grad(padded, grad_low):
    length_here = grad_low.shape[1]
    return jnp.stack(
        [
            jnp.einsum(
                "utc,utd->cd",
                padded[:, tap_index : tap_index + length_here],
                grad_low,
                preferred_element_type=jnp.float32,
            )
            for tap_index in range(3)
        ]
    )


def conv_input_grad(grad_low, weight):
    padded = rim_pad(grad_low)
    length_here = grad_low.shape[1]
    result = jnp.einsum("utd,cd->utc", padded[:, 2:], weight[0], preferred_element_type=jnp.float32)
    result = result + jnp.einsum(
        "utd,cd->utc", padded[:, 1 : length_here + 1], weight[1], preferred_element_type=jnp.float32
    )
    return result + jnp.einsum(
        "utd,cd->utc", padded[:, 0:length_here], weight[2], preferred_element_type=jnp.float32
    )


def norm_forward(signal, frame_mask, valid_count, gain_row, shift_row):
    width = C // GROUPS
    shape_now = signal.shape
    grouped = (signal * frame_mask[:, :, None]).reshape(shape_now[0], shape_now[1], GROUPS, width)
    total = jnp.sum(grouped, axis=(1, 3))
    squares = jnp.sum(grouped * grouped, axis=(1, 3))
    number = valid_count[:, None] * width
    mean_now = total / number
    inv_std = lax.rsqrt(squares / number - mean_now * mean_now + EPSILON)
    mean_wide = jnp.repeat(mean_now, width, axis=1)[:, None, :]
    inv_wide = jnp.repeat(inv_std, width, axis=1)[:, None, :]
    normed = (signal - mean_wide) * inv_wide
    return (normed * gain_row + shift_row, normed, inv_wide)


def norm_backward(grad_out, normed, inv_wide, frame_mask, valid_count, gain_row):
    width = C // GROUPS
    shape_now = grad_out.shape
    grad_norm = grad_out * gain_row
    first_sum = jnp.sum(grad_norm.reshape(shape_now[0], shape_now[1], GROUPS, width), axis=(1, 3))
    second_sum = jnp.sum(
        (grad_norm * normed).reshape(shape_now[0], shape_now[1], GROUPS, width), axis=(1, 3)
    )
    number = valid_count[:, None] * width
    first_wide = jnp.repeat(first_sum / number, width, axis=1)[:, None, :]
    second_wide = jnp.repeat(second_sum / number, width, axis=1)[:, None, :]
    grad_signal = inv_wide * (
        grad_norm - frame_mask[:, :, None] * (first_wide + normed * second_wide)
    )
    grad_gain = jnp.sum(grad_out * normed, axis=(0, 1))
    grad_shift = jnp.sum(grad_out, axis=(0, 1))
    return (grad_signal, grad_gain, grad_shift)


def update(master, moment, average, grad, rate):
    moment_new = MOMENTUM * moment + grad
    master_new = master - rate * (grad + MOMENTUM * moment_new)
    average_new = AVERAGE_DECAY * average + (1.0 - AVERAGE_DECAY) * master_new
    return (master_new, moment_new, average_new, master_new.astype(jnp.bfloat16))


def axis_bits(mesh_sizes):
    bits = []
    for name, size in mesh_sizes:
        weight = size // 2
        while weight >= 1:
            bits.append((name, weight))
            weight //= 2
    return bits


def part_orders(mesh_sizes):
    wide = axis_bits(mesh_sizes[:1])
    near = axis_bits(mesh_sizes[1:])
    first = near[:-1] + wide + near[-1:]
    second = near[:-1] + wide[-1:] + wide[:-1] + near[-1:]
    return (first, second)


def owner_place(order, mesh_sizes, owner):
    strides, stride = {}, 1
    for name, size in reversed(mesh_sizes):
        strides[name] = (stride, size)
        stride *= size
    place = 0
    for step, (name, weight) in enumerate(order):
        base, size = strides[name]
        place += ((owner // base) % size // weight % 2) << step
    return place


def window_rows(length_now, count):
    most = max((i * length_now) % 128 + length_now for i in range(count))
    return -(-most // (128 * 16)) * 16


def bit_of(name, weight):
    return (lax.axis_index(name) // weight) % 2


def partner_of(name, weight):
    return {name: lax.axis_index(name) + (1 - 2 * bit_of(name, weight)) * weight}


def seq_neighbour(step):
    return lax.rem(lax.axis_index("seq") + step, lax.axis_size("seq"))


def greet(orders):
    barrier = pltpu.get_barrier_semaphore()
    others = [partner_of(name, weight) for name, weight in orders[0] if name != "seq"]
    others += [{"seq": seq_neighbour(step)} for step in range(1, lax.axis_size("seq"))]
    for other in others:
        pl.semaphore_signal(
            barrier, inc=1, device_id=other, device_id_type=pl.DeviceIdType.MESH
        )
    pl.semaphore_wait(barrier, len(others))


def exchange_copies(cells, cells_out, swap_send, swap_recv):
    copies = []
    for step in range(1, lax.axis_size("seq")):
        target = seq_neighbour(step)
        copies.append(
            pltpu.make_async_remote_copy(
                src_ref=cells.at[target],
                dst_ref=cells_out.at[lax.axis_index("seq")],
                send_sem=swap_send.at[step - 1],
                recv_sem=swap_recv.at[step - 1],
                device_id={"seq": target},
                device_id_type=pl.DeviceIdType.MESH,
            )
        )
    return copies


def gather_kernel(
    orders,
    in_a,
    in_b,
    cells,
    out_a,
    out_b,
    cells_out,
    local_sem,
    send_sem,
    recv_sem,
    swap_send,
    swap_recv,
):
    ins, outs = (in_a, in_b), (out_a, out_b)
    stage_count = len(orders[0])
    offsets = []
    for part in range(2):
        offset = 0
        for step, (name, weight) in enumerate(orders[part]):
            offset = offset + bit_of(name, weight) * (1 << step)
        offsets.append(offset)
    locals_now = [
        pltpu.make_async_copy(ins[part], outs[part].at[offsets[part]], local_sem.at[part])
        for part in range(2)
    ]
    place = lax.axis_index("seq")
    locals_now.append(pltpu.make_async_copy(cells.at[place], cells_out.at[place], local_sem.at[2]))
    for copy in locals_now:
        copy.start()
    greet(orders)
    swaps = exchange_copies(cells, cells_out, swap_send, swap_recv)
    for copy in locals_now:
        copy.wait()
    copies = []
    for step in range(stage_count):
        held = 1 << step
        for part in range(2):
            name, weight = orders[part][step]
            start = offsets[part]
            block = outs[part].at[pl.ds(start, held)]
            copy = pltpu.make_async_remote_copy(
                src_ref=block,
                dst_ref=block,
                send_sem=send_sem.at[part, step],
                recv_sem=recv_sem.at[part, step],
                device_id=partner_of(name, weight),
                device_id_type=pl.DeviceIdType.MESH,
            )
            copy.start()
            copies.append(copy)
        if step == 0:
            for copy in swaps:
                copy.start()
        for part in range(2):
            copies[2 * step + part].wait_recv()
            name, weight = orders[part][step]
            offsets[part] = offsets[part] - bit_of(name, weight) * held
    for copy in copies:
        copy.wait_send()
    for copy in swaps:
        copy.wait()


def gather_windows(orders, win_a, win_b, cells):
    count = 1 << len(orders[0])
    stages = len(orders[0])
    return pl.pallas_call(
        functools.partial(gather_kernel, orders),
        out_shape=(
            jax.ShapeDtypeStruct((count,) + win_a.shape, win_a.dtype),
            jax.ShapeDtypeStruct((count,) + win_b.shape, win_b.dtype),
            jax.ShapeDtypeStruct(cells.shape, cells.dtype),
        ),
        in_specs=[pl.BlockSpec(memory_space=pltpu.VMEM)] * 3,
        out_specs=[pl.BlockSpec(memory_space=pltpu.VMEM)] * 3,
        scratch_shapes=[
            pltpu.SemaphoreType.DMA((3,)),
            pltpu.SemaphoreType.DMA((2, stages)),
            pltpu.SemaphoreType.DMA((2, stages)),
            pltpu.SemaphoreType.DMA((cells.shape[0] - 1,)),
            pltpu.SemaphoreType.DMA((cells.shape[0] - 1,)),
        ],
        compiler_params=pltpu.CompilerParams(
            collective_id=0, has_side_effects=True, vmem_limit_bytes=32 * 1024 * 1024
        ),
    )(win_a, win_b, cells)


def reduce_kernel(
    orders,
    in_a,
    in_b,
    cells,
    out_a,
    out_b,
    cells_out,
    land_a,
    land_b,
    local_sem,
    send_sem,
    recv_sem,
    swap_send,
    swap_recv,
):
    ins, outs, lands = (in_a, in_b), (out_a, out_b), (land_a, land_b)
    stage_count = len(orders[0])
    place = lax.axis_index("seq")
    local = pltpu.make_async_copy(cells.at[place], cells_out.at[place], local_sem.at[0])
    local.start()
    greet(orders)
    swaps = exchange_copies(cells, cells_out, swap_send, swap_recv)
    copies = []

    def source(part, step, keep):
        name, weight = orders[part][stage_count - 1 - step]
        held = 1 << (stage_count - 1 - step)
        side = bit_of(name, weight)
        side = side if keep else 1 - side
        if step == 0:
            return ins[part].at[pl.ds(side * held, held)]
        base = (1 << stage_count) - (1 << (stage_count - step + 1))
        return lands[part].at[pl.ds(base + side * held, held)]

    for step in range(stage_count):
        held = 1 << (stage_count - 1 - step)
        base = (1 << stage_count) - (1 << (stage_count - step))
        for part in range(2):
            name, weight = orders[part][stage_count - 1 - step]
            copy = pltpu.make_async_remote_copy(
                src_ref=source(part, step, False),
                dst_ref=lands[part].at[pl.ds(base, held)],
                send_sem=send_sem.at[part, step],
                recv_sem=recv_sem.at[part, step],
                device_id=partner_of(name, weight),
                device_id_type=pl.DeviceIdType.MESH,
            )
            copy.start()
            copies.append(copy)
        if step == 0:
            for copy in swaps:
                copy.start()
        for part in range(2):
            copies[2 * step + part].wait_recv()
            mine = source(part, step, True)
            if step == stage_count - 1:
                outs[part][...] = mine[0].astype(jnp.float32) + lands[part][base].astype(
                    jnp.float32
                )
            else:

                def add_one(index, carry, mine=mine, part=part, base=base):
                    land = lands[part].at[base + index]
                    total = mine[index].astype(jnp.float32) + land[...].astype(jnp.float32)
                    land[...] = total.astype(land.dtype)
                    return carry

                lax.fori_loop(0, held, add_one, 0)
    for copy in copies:
        copy.wait_send()
    for copy in swaps:
        copy.wait()
    local.wait()


def reduce_windows(orders, rows_a, rows_b, cells):
    count = 1 << len(orders[0])
    stages = len(orders[0])
    return pl.pallas_call(
        functools.partial(reduce_kernel, orders),
        out_shape=(
            jax.ShapeDtypeStruct(rows_a.shape[1:], jnp.float32),
            jax.ShapeDtypeStruct(rows_b.shape[1:], jnp.float32),
            jax.ShapeDtypeStruct(cells.shape, cells.dtype),
        ),
        in_specs=[pl.BlockSpec(memory_space=pltpu.VMEM)] * 3,
        out_specs=[pl.BlockSpec(memory_space=pltpu.VMEM)] * 3,
        scratch_shapes=[
            pltpu.VMEM((count - 1,) + rows_a.shape[1:], rows_a.dtype),
            pltpu.VMEM((count - 1,) + rows_b.shape[1:], rows_b.dtype),
            pltpu.SemaphoreType.DMA((1,)),
            pltpu.SemaphoreType.DMA((2, stages)),
            pltpu.SemaphoreType.DMA((2, stages)),
            pltpu.SemaphoreType.DMA((cells.shape[0] - 1,)),
            pltpu.SemaphoreType.DMA((cells.shape[0] - 1,)),
        ],
        compiler_params=pltpu.CompilerParams(
            collective_id=1, has_side_effects=True, vmem_limit_bytes=32 * 1024 * 1024
        ),
    )(rows_a, rows_b, cells)


RES_SQUARES = 7 * C * C
RES_ROWS = (RES_SQUARES + TE * C + 8 * C) // 128
INNER = HEADS * HD
TF_SIZES = (3 * C * INNER, INNER * C, C * F, F * C, 6 * C, 3 * F)
TF_ROWS = sum(TF_SIZES) // 128


def place_maps(orders, mesh_sizes):
    count = 1 << len(orders[0])
    return [[owner_place(orders[part], mesh_sizes, i) for i in range(count)] for part in range(2)]


def matrix_views():
    views = []
    row = 0
    for rows, width in ((6 * C, C), (C, C), (TE, C), (8, C)):
        views.append((0, row, rows, width))
        row += rows * width // 128
    row = 0
    for rows, width in ((C, 3 * INNER), (INNER, C), (C, F), (F, C), (6, C), (3, F)):
        views.append((1, row, rows, width))
        row += rows * width // 128
    return views


def assemble_kernel(places, lengths_now, in_a, in_b, *refs):
    outs, flats = refs[:10], refs[10:12]
    count = len(places[0])
    for part, ref in enumerate((in_a, in_b)):
        flat = flats[part]
        for i in range(count):
            start, lead = divmod(i * lengths_now[part], 128)
            rows = -(-(lead + lengths_now[part]) // 128)
            if lead:
                edge = flat[start : start + 1, :]
            flat[start : start + rows, :] = ref[places[part][i]].astype(jnp.float32)[:rows]
            if lead:
                flat[start : start + 1, :] = flat[start : start + 1, :] + edge
    for out, (part, row, rows, width) in zip(outs, matrix_views()):
        stride = width // 128
        for lane in range(stride):
            piece = flats[part][pl.ds(row + lane, rows, stride=stride), :]
            out[:, lane * 128 : (lane + 1) * 128] = piece.astype(out.dtype)


def assemble_weights(places, lengths_now, win_a, win_b):
    shapes = []
    for index, (part, row, rows, width) in enumerate(matrix_views()):
        kind = jnp.float32 if index in (3, 8, 9) else jnp.bfloat16
        shapes.append(jax.ShapeDtypeStruct((rows, width), kind))
    return pl.pallas_call(
        functools.partial(assemble_kernel, places, lengths_now),
        out_shape=shapes,
        in_specs=[pl.BlockSpec(memory_space=pltpu.VMEM)] * 2,
        out_specs=[pl.BlockSpec(memory_space=pltpu.VMEM)] * 10,
        scratch_shapes=[
            pltpu.VMEM((RES_ROWS + 8, 128), jnp.float32),
            pltpu.VMEM((TF_ROWS + 12, 128), jnp.float32),
        ],
        compiler_params=pltpu.CompilerParams(vmem_limit_bytes=32 * 1024 * 1024),
    )(win_a, win_b)


def cut_kernel(places, lengths_now, *refs):
    ins, outs, flats = refs[:10], refs[10:12], refs[12:14]
    count = len(places[0])
    for ref, (part, row, rows, width) in zip(ins, matrix_views()):
        stride = width // 128
        for lane in range(stride):
            flats[part][pl.ds(row + lane, rows, stride=stride), :] = ref[
                :, lane * 128 : (lane + 1) * 128
            ]
    for part in range(2):
        for i in range(count):
            start, lead = divmod(i * lengths_now[part], 128)
            rows = outs[part].shape[1]
            outs[part][places[part][i]] = flats[part][start : start + rows, :].astype(
                outs[part].dtype
            )


def cut_grads(places, lengths_now, window_sizes, grads):
    count = len(places[0])
    return pl.pallas_call(
        functools.partial(cut_kernel, places, lengths_now),
        out_shape=[
            jax.ShapeDtypeStruct((count, rows, 128), jnp.bfloat16) for rows in window_sizes
        ],
        in_specs=[pl.BlockSpec(memory_space=pltpu.VMEM)] * 10,
        out_specs=[pl.BlockSpec(memory_space=pltpu.VMEM)] * 2,
        scratch_shapes=[
            pltpu.VMEM((RES_ROWS + 24, 128), jnp.float32),
            pltpu.VMEM((TF_ROWS + 28, 128), jnp.float32),
        ],
        compiler_params=pltpu.CompilerParams(vmem_limit_bytes=40 * 1024 * 1024),
    )(*grads)


def flat_index(mesh_sizes):
    index = 0
    for name, size in mesh_sizes:
        index = index * size + lax.axis_index(name)
    return index


def to_window(master, rows, owner):
    lead = (owner * master.shape[0]) % 128
    window = jnp.zeros((rows * 128,), jnp.bfloat16)
    return lax.dynamic_update_slice(window, master.astype(jnp.bfloat16), (lead,)).reshape(rows, 128)


def from_window(window, length_now, owner):
    lead = (owner * length_now) % 128
    return lax.dynamic_slice(window.reshape(-1), (lead,), (length_now,))


SIN_TERMS = (
    3.141592640063848,
    -5.167710072816043,
    2.5500772667383647,
    -0.5982893715546711,
    0.07765328748430061,
)
COS_TERMS = (
    0.9999999530157438,
    -4.934792793539851,
    4.058410463392346,
    -1.3318699300230954,
    0.21967444597863747,
)
ROUND_SHIFT = 12582912.0


def mm(left, right):
    return jnp.dot(left, right, preferred_element_type=jnp.float32)


def mm_right(left, right):
    return lax.dot_general(
        left, right, (((1,), (1,)), ((), ())), preferred_element_type=jnp.float32
    )


def mm_left(left, right):
    return lax.dot_general(
        left, right, (((0,), (0,)), ((), ())), preferred_element_type=jnp.float32
    )


def column_sum(cells):
    return jnp.sum(cells, axis=0, keepdims=True)


def sin_cos(half_turns):
    rest = half_turns - ((half_turns + ROUND_SHIFT) - ROUND_SHIFT)
    square = rest * rest
    sine = SIN_TERMS[-1]
    for term in SIN_TERMS[-2::-1]:
        sine = sine * square + term
    cosine = COS_TERMS[-1]
    for term in COS_TERMS[-2::-1]:
        cosine = cosine * square + term
    return (sine * rest, cosine)


def mish_value(signal):
    expo = jnp.exp(jnp.minimum(signal, 20.0))
    upper = expo * (expo + 2.0)
    return signal * (upper / (upper + 2.0))


def mish_slope(signal):
    expo = jnp.exp(jnp.minimum(signal, 20.0))
    upper = expo * (expo + 2.0)
    inverse = 1.0 / (upper + 2.0)
    return upper * inverse + signal * (4.0 * expo * (1.0 + expo)) * (inverse * inverse)


def row_norm(signal):
    center = signal - jnp.mean(signal, axis=-1, keepdims=True)
    spread = jnp.mean(center * center, axis=-1, keepdims=True)
    inverse = lax.rsqrt(spread + EPSILON)
    return (center * inverse, inverse)


def row_norm_back(grad_out, normed, inverse, gain_row):
    inner_grad = grad_out * gain_row
    first = jnp.mean(inner_grad, axis=-1, keepdims=True)
    second = jnp.mean(inner_grad * normed, axis=-1, keepdims=True)
    return (inner_grad - first - normed * second) * inverse


def step_kernel(
    lengths_ref,
    cells_ref,
    time_ref,
    convs_ref,
    res_ref,
    rows_ref,
    qkv_ref,
    out_ref,
    up_ref,
    down_ref,
    tf_rows_ref,
    wide_ref,
    results_ref,
    gtime_ref,
    gconvs_ref,
    gres_ref,
    grows_ref,
    gqkv_ref,
    gout_ref,
    gup_ref,
    gdown_ref,
    gtf_ref,
    gwide_ref,
    pad,
    col_one,
    col_two,
    col_grad,
    z_one,
    z_two,
    block,
    grad_mid,
    grad_norm,
    attn_in,
    heads_q,
    heads_k,
    heads_v,
    heads_g,
    attn_vals,
    probs,
    snake,
    grad_up,
    ff_in,
    grad_attn,
    grad_key,
    grad_value,
    grad_query,
    grad_qkv,
    grad_skip,
):
    frames = z_one.shape[0]
    tiles, _, tile, _ = cells_ref.shape
    utt = pl.program_id(0)
    length_now = lengths_ref[utt]
    number = length_now.astype(jnp.float32) * (C // GROUPS)

    @pl.when(utt == 0)
    def clear():
        for ref in (
            gconvs_ref,
            gres_ref,
            grows_ref,
            gqkv_ref,
            gout_ref,
            gup_ref,
            gdown_ref,
            gtf_ref,
            gwide_ref,
        ):
            ref[...] = jnp.zeros_like(ref)

    edge = jnp.zeros((8, C), jnp.float32)
    pad[0:8, :] = edge
    pad[frames + 8 : frames + 16, :] = edge
    gtime_ref[...] = jnp.zeros_like(gtime_ref)
    group_row = lax.broadcasted_iota(jnp.int32, (C, C), 0) // (C // GROUPS)
    group_column = lax.broadcasted_iota(jnp.int32, (C, C), 1) // (C // GROUPS)
    group_ones = (group_row == group_column).astype(jnp.float32)
    lane = lax.broadcasted_iota(jnp.int32, (1, INNER), 1) // HD
    head_masks = [(lane == head).astype(jnp.float32) for head in range(HEADS)]
    key_bias = jnp.where(
        lax.broadcasted_iota(jnp.int32, (1, frames), 1) < length_now, 0.0, MASK_FILL
    )

    def rows_at(index, lead=0):
        return pl.ds(pl.multiple_of(index * tile + lead, 8), tile)

    def tile_mask(index):
        ids = lax.broadcasted_iota(jnp.int32, (tile, 1), 0) + index * tile
        return (ids < length_now).astype(jnp.float32)

    def group_sum(row):
        wide = jnp.broadcast_to(row, (8, C))
        return jnp.dot(
            wide,
            group_ones,
            precision=lax.Precision.HIGHEST,
            preferred_element_type=jnp.float32,
        )[0:1]

    def build_columns(target):
        for index in range(tiles):
            start = index * tile
            for tap in range(3):
                piece = pad[start + 7 + tap : start + 7 + tap + tile, :]
                target[start : start + tile, tap * C : (tap + 1) * C] = piece.astype(jnp.bfloat16)

    def loop(body):
        def wrapped(index, carry):
            body(index)
            return carry

        lax.fori_loop(0, tiles, wrapped, 0)

    def conv_stage(columns, base, bias_at, target):
        def one(index, carry):
            rows = rows_at(index)
            cells = mm(columns[rows, :], convs_ref[base : base + 3 * C, :])
            cells = cells + rows_ref[bias_at : bias_at + 1, :]
            target[rows, :] = cells
            masked = cells * tile_mask(index)
            return (carry[0] + column_sum(masked), carry[1] + column_sum(masked * masked))

        zero = jnp.zeros((1, C), jnp.float32)
        total, squares = lax.fori_loop(0, tiles, one, (zero, zero))
        mean_row = group_sum(total) / number
        inv_row = lax.rsqrt(group_sum(squares) / number - mean_row * mean_row + EPSILON)
        return (mean_row, inv_row)

    def copy_in(index):
        pad[rows_at(index, 8), :] = cells_ref[index, 0, :, 0:C].astype(jnp.float32)

    loop(copy_in)
    build_columns(col_one)
    mean_one, inv_one = conv_stage(col_one, 0, 0, z_one)

    def hidden(index):
        normed = (z_one[rows_at(index), :] - mean_one) * inv_one
        act = mish_value(normed * rows_ref[1:2, :] + rows_ref[2:3, :])
        pad[rows_at(index, 8), :] = (act + time_ref[0]) * tile_mask(index)

    loop(hidden)
    build_columns(col_two)
    mean_two, inv_two = conv_stage(col_two, 3 * C, 3, z_two)

    def enter(index):
        rows = rows_at(index)
        normed = (z_two[rows, :] - mean_two) * inv_two
        act = mish_value(normed * rows_ref[4:5, :] + rows_ref[5:6, :]) * tile_mask(index)
        state = act + mm(cells_ref[index, 0, :, 0:C], res_ref[...]) + rows_ref[6:7, :]
        block[rows, :] = state
        normed, _ = row_norm(state)
        low = (normed * tf_rows_ref[0:1, :] + tf_rows_ref[1:2, :]).astype(jnp.bfloat16)
        attn_in[rows, :] = low
        parts = mm(low, qkv_ref[...]).astype(jnp.bfloat16).astype(jnp.float32)
        query = parts[:, :INNER] * SCORE_SCALE
        for head in range(HEADS):
            heads_q[head, rows, :] = (query * head_masks[head]).astype(jnp.bfloat16)
            heads_k[head, rows, :] = (parts[:, INNER : 2 * INNER] * head_masks[head]).astype(
                jnp.bfloat16
            )
            heads_v[head, rows, :] = (parts[:, 2 * INNER :] * head_masks[head]).astype(
                jnp.bfloat16
            )

    loop(enter)

    def attend(index):
        rows = rows_at(index)
        total = jnp.zeros((tile, INNER), jnp.float32)
        for head in range(HEADS):
            scores = mm_right(heads_q[head, rows, :], heads_k[head]) + key_bias
            expo = jnp.exp(scores - jnp.max(scores, axis=-1, keepdims=True))
            chance = expo * (1.0 / jnp.sum(expo, axis=-1, keepdims=True))
            probs[head, rows, :] = chance
            total = total + mm(chance.astype(jnp.bfloat16), heads_v[head])
        attn_vals[rows, :] = total.astype(jnp.bfloat16)

    loop(attend)

    def feed(index):
        rows = rows_at(index)
        mid = block[rows, :] + mm(attn_vals[rows, :], out_ref[...]) + tf_rows_ref[2:3, :]
        normed, inverse = row_norm(mid)
        low = (normed * tf_rows_ref[3:4, :] + tf_rows_ref[4:5, :]).astype(jnp.bfloat16)
        ff_in[rows, :] = low
        grad_low = cells_ref[index, 0, :, C : 2 * C]
        result = jnp.zeros((tile, C), jnp.float32)
        grad_in = jnp.zeros((tile, C), jnp.float32)
        for chunk in range(F // 256):
            lanes = slice(chunk * 256, (chunk + 1) * 256)
            up_out = mm(low, up_ref[:, lanes]) + wide_ref[0:1, lanes]
            grad_snake = mm_right(grad_low, down_ref[lanes, :])
            speed = jnp.exp(wide_ref[1:2, lanes])
            depth = 1.0 / (jnp.exp(wide_ref[2:3, lanes]) + 1e-09)
            half_turns = up_out * (speed * (1.0 / math.pi))
            sine, cosine = sin_cos(half_turns)
            square = sine * sine
            value = (up_out + square * depth).astype(jnp.bfloat16)
            snake[rows, lanes] = value
            result = result + mm(value, down_ref[lanes, :])
            slope = (grad_snake * (2.0 * depth)) * (sine * cosine)
            grad_here = (grad_snake + slope * speed).astype(jnp.bfloat16)
            grad_up[rows, lanes] = grad_here
            grad_in = grad_in + mm_right(grad_here, up_ref[:, lanes])
            gwide_ref[0:1, lanes] += column_sum(grad_here.astype(jnp.float32))
            gwide_ref[1:2, lanes] += column_sum(slope * half_turns)
            gwide_ref[2:3, lanes] += column_sum(grad_snake * square)
        results_ref[index, 0, :, 0:C] = ((mid + result + tf_rows_ref[5:6, :]) * tile_mask(index)).astype(
            jnp.bfloat16
        )
        grad_wide = grad_low.astype(jnp.float32)
        gtf_ref[5:6, :] += column_sum(grad_wide)
        gtf_ref[3:4, :] += column_sum(grad_in * normed)
        gtf_ref[4:5, :] += column_sum(grad_in)
        grad_state = grad_wide + row_norm_back(grad_in, normed, inverse, tf_rows_ref[3:4, :])
        grad_mid[rows, :] = grad_state
        grad_state = grad_state.astype(jnp.bfloat16)
        grad_attn[rows, :] = grad_state
        gtf_ref[2:3, :] += column_sum(grad_state.astype(jnp.float32))
        grad_vals = mm_right(grad_state, out_ref[...]).astype(jnp.bfloat16).astype(jnp.float32)
        for head in range(HEADS):
            heads_g[head, rows, :] = (grad_vals * head_masks[head]).astype(jnp.bfloat16)

    loop(feed)

    def feed_weights(index, carry):
        lanes = pl.ds(pl.multiple_of(index * 256, 256), 256)
        grads = cells_ref[:, 0, :, C : 2 * C].reshape(frames, C)
        gdown_ref[lanes, :] += mm_left(snake[:, lanes], grads)
        gup_ref[:, lanes] += mm_left(ff_in[...], grad_up[:, lanes])
        return carry

    lax.fori_loop(0, F // 256, feed_weights, 0)
    gout_ref[...] += mm_left(attn_vals[...], grad_attn[...])
    grad_key[...] = jnp.zeros_like(grad_key)
    grad_value[...] = jnp.zeros_like(grad_value)

    def attend_back(index):
        rows = rows_at(index)
        total = jnp.zeros((tile, INNER), jnp.float32)
        scores_low, chances_low = [], []
        for head in range(HEADS):
            grad_out = heads_g[head, rows, :]
            chance = probs[head, rows, :]
            grad_probs = mm_right(grad_out, heads_v[head])
            dot_row = jnp.sum(chance * grad_probs, axis=-1, keepdims=True)
            grad_scores = (chance * (grad_probs - dot_row)).astype(jnp.bfloat16)
            total = total + mm(grad_scores, heads_k[head])
            scores_low.append(grad_scores)
            chances_low.append(chance.astype(jnp.bfloat16))
        both = (HEADS * tile, INNER)
        grad_key[...] += mm_left(
            jnp.concatenate(scores_low, axis=0), heads_q[:, rows, :].reshape(both)
        )
        grad_value[...] += mm_left(
            jnp.concatenate(chances_low, axis=0), heads_g[:, rows, :].reshape(both)
        )
        grad_query[rows, :] = total * SCORE_SCALE

    loop(attend_back)

    def leave(index, carry):
        rows = rows_at(index)
        grad_qkv[rows, 0:INNER] = grad_query[rows, :].astype(jnp.bfloat16)
        grad_qkv[rows, INNER : 2 * INNER] = grad_key[rows, :].astype(jnp.bfloat16)
        grad_qkv[rows, 2 * INNER : 3 * INNER] = grad_value[rows, :].astype(jnp.bfloat16)
        grad_in = mm_right(grad_qkv[rows, :], qkv_ref[...])
        normed, inverse = row_norm(block[rows, :])
        gtf_ref[0:1, :] += column_sum(grad_in * normed)
        gtf_ref[1:2, :] += column_sum(grad_in)
        grad_state = grad_mid[rows, :] + row_norm_back(
            grad_in, normed, inverse, tf_rows_ref[0:1, :]
        )
        low = grad_state.astype(jnp.bfloat16)
        grad_skip[rows, :] = low
        grows_ref[6:7, :] += column_sum(low.astype(jnp.float32))
        normed = (z_two[rows, :] - mean_two) * inv_two
        grad_here = (
            mish_slope(normed * rows_ref[4:5, :] + rows_ref[5:6, :])
            * tile_mask(index)
            * grad_state
        )
        grad_norm[rows, :] = grad_here
        return (carry[0] + column_sum(grad_here), carry[1] + column_sum(grad_here * normed))

    zero = jnp.zeros((1, C), jnp.float32)

    def norm_back(target, mean_row, inv_row, gain_at, bias_at, shift_sum, gain_sum):
        gain_row = rows_ref[gain_at : gain_at + 1, :]
        grows_ref[gain_at : gain_at + 1, :] += gain_sum
        grows_ref[gain_at + 1 : gain_at + 2, :] += shift_sum
        first = group_sum(shift_sum * gain_row) / number
        second = group_sum(gain_sum * gain_row) / number

        def one(index):
            rows = rows_at(index)
            normed = (target[rows, :] - mean_row) * inv_row
            cells = inv_row * (
                grad_norm[rows, :] * gain_row - tile_mask(index) * (first + normed * second)
            )
            cells = cells.astype(jnp.bfloat16).astype(jnp.float32)
            grows_ref[bias_at : bias_at + 1, :] += column_sum(cells)
            pad[rows_at(index, 8), :] = cells

        loop(one)
        build_columns(col_grad)

    def conv_back(rows, base):
        total = mm_right(col_grad[rows, 2 * C : 3 * C], convs_ref[base : base + C, :])
        total = total + mm_right(col_grad[rows, C : 2 * C], convs_ref[base + C : base + 2 * C, :])
        return total + mm_right(col_grad[rows, 0:C], convs_ref[base + 2 * C : base + 3 * C, :])

    def conv_weights(columns, base):
        for tap in range(3):
            gconvs_ref[base + tap * C : base + (tap + 1) * C, :] += mm_left(
                columns[:, tap * C : (tap + 1) * C], col_grad[:, C : 2 * C]
            )

    shift_sum, gain_sum = lax.fori_loop(0, tiles, leave, (zero, zero))
    norm_back(z_two, mean_two, inv_two, 4, 3, shift_sum, gain_sum)
    conv_weights(col_two, 3 * C)

    def hidden_back(index, carry):
        rows = rows_at(index)
        grad_here = conv_back(rows, 3 * C) * tile_mask(index)
        gtime_ref[0] += column_sum(grad_here)
        normed = (z_one[rows, :] - mean_one) * inv_one
        grad_here = mish_slope(normed * rows_ref[1:2, :] + rows_ref[2:3, :]) * grad_here
        grad_norm[rows, :] = grad_here
        return (carry[0] + column_sum(grad_here), carry[1] + column_sum(grad_here * normed))

    shift_sum, gain_sum = lax.fori_loop(0, tiles, hidden_back, (zero, zero))
    grows_ref[7:8, :] += gtime_ref[0]
    norm_back(z_one, mean_one, inv_one, 1, 0, shift_sum, gain_sum)
    conv_weights(col_one, 0)

    def finish(index):
        rows = rows_at(index)
        total = conv_back(rows, 0) + mm_right(grad_skip[rows, :], res_ref[...])
        results_ref[index, 0, :, C : 2 * C] = (total * tile_mask(index)).astype(jnp.bfloat16)

    loop(finish)
    gres_ref[...] += mm_left(cells_ref[:, 0, :, 0:C].reshape(frames, C), grad_skip[...])
    gqkv_ref[...] += mm_left(attn_in[...], grad_qkv[...])

    @pl.when(utt == pl.num_programs(0) - 1)
    def scale_rows():
        low_side = jnp.exp(wide_ref[2:3, :])
        depth = 1.0 / (low_side + 1e-09)
        gwide_ref[1:2, :] = gwide_ref[1:2, :] * math.pi
        gwide_ref[2:3, :] = -gwide_ref[2:3, :] * low_side * depth * depth


def whole_step(lengths, cells, time_proj, weights):
    (convs, res_weight, rows, qkv_weight, out_weight, up_weight, down_weight, tf_rows, wide) = weights
    tiles, utts, tile, _ = cells.shape
    frames = tiles * tile
    by_utt = pl.BlockSpec((tiles, 1, tile, 2 * C), lambda u, s: (0, u, 0, 0))
    row_by_utt = pl.BlockSpec((1, 1, C), lambda u, s: (u, 0, 0))

    def fixed(array):
        return pl.BlockSpec(array.shape, lambda u, s: (0, 0))

    f32, low = jnp.float32, jnp.bfloat16
    scratch = [
        ((frames + 16, C), f32),
        ((frames, 3 * C), low),
        ((frames, 3 * C), low),
        ((frames, 3 * C), low),
        ((frames, C), f32),
        ((frames, C), f32),
        ((frames, C), f32),
        ((frames, C), f32),
        ((frames, C), f32),
        ((frames, C), low),
        ((HEADS, frames, INNER), low),
        ((HEADS, frames, INNER), low),
        ((HEADS, frames, INNER), low),
        ((HEADS, frames, INNER), low),
        ((frames, INNER), low),
        ((HEADS, frames, frames), f32),
        ((frames, F), low),
        ((frames, F), low),
        ((frames, C), low),
        ((frames, C), low),
        ((frames, INNER), f32),
        ((frames, INNER), f32),
        ((frames, INNER), f32),
        ((frames, 3 * INNER), low),
        ((frames, C), low),
    ]
    return pl.pallas_call(
        step_kernel,
        grid_spec=pltpu.PrefetchScalarGridSpec(
            num_scalar_prefetch=1,
            grid=(utts,),
            in_specs=[by_utt, row_by_utt] + [fixed(array) for array in weights],
            out_specs=[by_utt, row_by_utt] + [fixed(array) for array in weights],
            scratch_shapes=[pltpu.VMEM(shape, kind) for shape, kind in scratch],
        ),
        out_shape=[
            jax.ShapeDtypeStruct(cells.shape, low),
            jax.ShapeDtypeStruct((utts, 1, C), f32),
        ]
        + [jax.ShapeDtypeStruct(array.shape, f32) for array in weights],
        compiler_params=pltpu.CompilerParams(
            dimension_semantics=("arbitrary",), vmem_limit_bytes=60 * 1024 * 1024
        ),
    )(lengths, cells, time_proj, *weights)


def prepare_kernel(
    lengths_ref, place_ref, inputs_ref, encoded_ref, durations_ref, cotangent_ref, out_ref
):
    frames, phones = inputs_ref.shape[1], durations_ref.shape[2]
    first = place_ref[0] * frames
    durations = durations_ref[0].astype(jnp.float32)
    before = lax.broadcasted_iota(jnp.int32, (phones, phones), 0)
    after = lax.broadcasted_iota(jnp.int32, (phones, phones), 1)
    upper = (before <= after).astype(jnp.bfloat16)
    wide = jnp.broadcast_to(durations, (16, phones)).astype(jnp.bfloat16)
    ends = mm(wide, upper)[0:1]
    starts = ends - durations
    last = lax.broadcasted_iota(jnp.int32, (1, phones), 1) == phones - 1
    ends = jnp.where(last, 1e9, ends)
    ids = lax.broadcasted_iota(jnp.int32, (frames, 1), 0) + first
    times = ids.astype(jnp.float32)
    picked = jnp.where((times >= starts) & (times < ends), 1.0, 0.0).astype(jnp.bfloat16)
    table = encoded_ref[0]
    high = table.astype(jnp.bfloat16)
    rest = table - high.astype(jnp.float32)
    middle = rest.astype(jnp.bfloat16)
    low = (rest - middle.astype(jnp.float32)).astype(jnp.bfloat16)
    rows = (mm(picked, high) + mm(picked, middle)) + mm(picked, low)
    mask = (ids < lengths_ref[pl.program_id(0)]).astype(jnp.float32)
    out_ref[0, 0, :, 0:C] = ((inputs_ref[0] + rows) * mask).astype(jnp.bfloat16)
    out_ref[0, 0, :, C : 2 * C] = (cotangent_ref[0] * mask).astype(jnp.bfloat16)


def prepare(inputs, encoded, durations, lengths, cotangent):
    utts, frames, _ = inputs.shape
    phones = durations.shape[1]
    seq_size = lax.axis_size("seq")
    group = utts // seq_size
    place = jnp.full((1,), lax.axis_index("seq"), jnp.int32)
    by_utt = lambda u, n, p: (u, 0, 0)
    return pl.pallas_call(
        prepare_kernel,
        grid_spec=pltpu.PrefetchScalarGridSpec(
            num_scalar_prefetch=2,
            grid=(utts,),
            in_specs=[
                pl.BlockSpec((1, frames, C), by_utt),
                pl.BlockSpec((1, phones, C), by_utt),
                pl.BlockSpec((1, 1, phones), by_utt),
                pl.BlockSpec((1, frames, C), by_utt),
            ],
            out_specs=pl.BlockSpec(
                (1, 1, frames, 2 * C), lambda u, n, p: (u // group, u % group, 0, 0)
            ),
        ),
        out_shape=jax.ShapeDtypeStruct((seq_size, group, frames, 2 * C), jnp.bfloat16),
        compiler_params=pltpu.CompilerParams(dimension_semantics=("arbitrary",)),
    )(lengths, place, inputs, encoded, durations[:, None, :], cotangent)


def per_device(
    inputs,
    encoded,
    durations,
    lengths,
    time_embed,
    cotangent,
    res_master,
    res_moment,
    res_average,
    tf_master,
    tf_moment,
    tf_average,
):
    utts_here, local_len, _ = inputs.shape
    seq_size = lax.axis_size("seq")
    key_total = local_len * seq_size
    utt_count = utts_here // seq_size
    seq_index = lax.axis_index("seq")
    cells = prepare(inputs, encoded, durations, lengths, cotangent)
    mesh_sizes = [(name, lax.axis_size(name)) for name in ("dp", "seq")]
    orders = part_orders(mesh_sizes)
    places = place_maps(orders, mesh_sizes)
    owner = flat_index(mesh_sizes)
    shard_lengths = (res_master.shape[0], tf_master.shape[0])
    window_sizes = [window_rows(size, len(places[0])) for size in shard_lengths]
    *gathered, cells = gather_windows(
        orders,
        to_window(res_master, window_sizes[0], owner),
        to_window(tf_master, window_sizes[1], owner),
        cells,
    )
    (
        convs,
        res_weight,
        time_weight,
        res_small,
        qkv_weight,
        out_weight,
        up_weight,
        down_weight,
        tf_small,
        wide_small,
    ) = assemble_weights(places, shard_lengths, *gathered)
    lengths = lax.dynamic_slice_in_dim(lengths, seq_index * utt_count, utt_count)
    time_embed = lax.dynamic_slice_in_dim(time_embed, seq_index * utt_count, utt_count)
    time_act = mish_fn(time_embed).astype(jnp.bfloat16)
    time_proj = jnp.dot(time_act, time_weight, preferred_element_type=jnp.float32) + res_small[7]
    weights = (
        convs,
        res_weight,
        res_small,
        qkv_weight,
        out_weight,
        up_weight,
        down_weight,
        tf_small,
        wide_small,
    )
    (
        results,
        grad_time_proj,
        grad_convs,
        grad_res_w,
        grad_rows,
        *tf_grads,
    ) = whole_step(lengths, cells, time_proj[:, None, :], weights)
    grad_time_w = jnp.dot(
        time_act.astype(jnp.float32).T, grad_time_proj[:, 0], precision=lax.Precision.HIGHEST
    )
    grads = (grad_convs, grad_res_w, grad_time_w, grad_rows, *tf_grads)
    *summed, results = reduce_windows(
        orders, *cut_grads(places, shard_lengths, window_sizes, grads), results
    )
    results = results.reshape(utts_here, local_len, 2 * C)
    res_share = from_window(summed[0], shard_lengths[0], owner)
    tf_share = from_window(summed[1], shard_lengths[1], owner)
    tokens_total = utts_here * key_total * lax.axis_size("dp")
    rate = LEARN_BASE / math.sqrt(tokens_total)
    res_new, res_moment_new, res_average_new, res_low = update(
        res_master, res_moment, res_average, res_share, rate
    )
    tf_new, tf_moment_new, tf_average_new, tf_low = update(
        tf_master, tf_moment, tf_average, tf_share, rate
    )
    return (
        results[:, :, :C].astype(jnp.float32),
        results[:, :, C:].astype(jnp.float32),
        res_share,
        tf_share,
        res_new,
        tf_new,
        res_moment_new,
        tf_moment_new,
        res_average_new,
        tf_average_new,
        res_low,
        tf_low,
    )


def solution(mesh):
    placed = (
        P("dp", "seq", None),
        P("dp", None, None),
        P("dp", None),
        P("dp"),
        P("dp", None),
        P("dp", "seq", None),
        P(("dp", "seq")),
        P(("dp", "seq")),
        P(("dp", "seq")),
        P(("dp", "seq")),
        P(("dp", "seq")),
        P(("dp", "seq")),
    )
    return jax.shard_map(
        per_device,
        mesh=mesh,
        in_specs=placed,
        out_specs=(
            P("dp", "seq", None),
            P("dp", "seq", None),
            P(("dp", "seq")),
            P(("dp", "seq")),
            P(("dp", "seq")),
            P(("dp", "seq")),
            P(("dp", "seq")),
            P(("dp", "seq")),
            P(("dp", "seq")),
            P(("dp", "seq")),
            P(("dp", "seq")),
            P(("dp", "seq")),
        ),
        check_vma=False,
    )
```

```python
import functools
import math

import jax
import jax.numpy as jnp
from jax import lax
from jax.experimental import pallas as pl
from jax.experimental.pallas import tpu as pltpu
from jax.sharding import PartitionSpec as P

C = 256
GROUPS = 8
TE = 1024
HEADS = 2
HD = 64
F = 1024


EPSILON = 1e-05
SCORE_SCALE = 0.125
MOMENTUM = 0.9
AVERAGE_DECAY = 0.99
LEARN_BASE = 0.015
MASK_FILL = -1e30


def update(master, moment, average, grad, rate):
    moment_new = MOMENTUM * moment + grad
    master_new = master - rate * (grad + MOMENTUM * moment_new)
    average_new = AVERAGE_DECAY * average + (1.0 - AVERAGE_DECAY) * master_new
    return (master_new, moment_new, average_new, master_new.astype(jnp.bfloat16))


def axis_bits(mesh_sizes):
    bits = []
    for name, size in mesh_sizes:
        weight = size // 2
        while weight >= 1:
            bits.append((name, weight))
            weight //= 2
    return bits


def part_orders(mesh_sizes):
    wide = axis_bits(mesh_sizes[:1])
    near = axis_bits(mesh_sizes[1:])
    first = near[:-1] + wide + near[-1:]
    second = near[:-1] + wide[-1:] + wide[:-1] + near[-1:]
    return (first, second)


def owner_place(order, mesh_sizes, owner):
    strides, stride = {}, 1
    for name, size in reversed(mesh_sizes):
        strides[name] = (stride, size)
        stride *= size
    place = 0
    for step, (name, weight) in enumerate(order):
        base, size = strides[name]
        place += ((owner // base) % size // weight % 2) << step
    return place


def window_rows(length_now, count):
    most = max((i * length_now) % 128 + length_now for i in range(count))
    return -(-most // (128 * 16)) * 16


def bit_of(name, weight):
    return (lax.axis_index(name) // weight) % 2


def partner_of(name, weight):
    return {name: lax.axis_index(name) + (1 - 2 * bit_of(name, weight)) * weight}


def seq_neighbour(step):
    return lax.rem(lax.axis_index("seq") + step, lax.axis_size("seq"))


def greet(orders):
    barrier = pltpu.get_barrier_semaphore()
    others = [partner_of(name, weight) for name, weight in orders[0] if name != "seq"]
    others += [{"seq": seq_neighbour(step)} for step in range(1, lax.axis_size("seq"))]
    for other in others:
        pl.semaphore_signal(
            barrier, inc=1, device_id=other, device_id_type=pl.DeviceIdType.MESH
        )
    pl.semaphore_wait(barrier, len(others))


def exchange_copies(cells, cells_out, swap_send, swap_recv):
    copies = []
    for step in range(1, lax.axis_size("seq")):
        target = seq_neighbour(step)
        copies.append(
            pltpu.make_async_remote_copy(
                src_ref=cells.at[target],
                dst_ref=cells_out.at[lax.axis_index("seq")],
                send_sem=swap_send.at[step - 1],
                recv_sem=swap_recv.at[step - 1],
                device_id={"seq": target},
                device_id_type=pl.DeviceIdType.MESH,
            )
        )
    return copies


def gather_kernel(
    orders,
    in_a,
    in_b,
    cells,
    out_a,
    out_b,
    cells_out,
    local_sem,
    send_sem,
    recv_sem,
    swap_send,
    swap_recv,
):
    ins, outs = (in_a, in_b), (out_a, out_b)
    stage_count = len(orders[0])
    offsets = []
    for part in range(2):
        offset = 0
        for step, (name, weight) in enumerate(orders[part]):
            offset = offset + bit_of(name, weight) * (1 << step)
        offsets.append(offset)
    locals_now = [
        pltpu.make_async_copy(ins[part], outs[part].at[offsets[part]], local_sem.at[part])
        for part in range(2)
    ]
    place = lax.axis_index("seq")
    locals_now.append(pltpu.make_async_copy(cells.at[place], cells_out.at[place], local_sem.at[2]))
    for copy in locals_now:
        copy.start()
    greet(orders)
    swaps = exchange_copies(cells, cells_out, swap_send, swap_recv)
    for copy in locals_now:
        copy.wait()
    copies = []
    for step in range(stage_count):
        held = 1 << step
        for part in range(2):
            name, weight = orders[part][step]
            start = offsets[part]
            block = outs[part].at[pl.ds(start, held)]
            copy = pltpu.make_async_remote_copy(
                src_ref=block,
                dst_ref=block,
                send_sem=send_sem.at[part, step],
                recv_sem=recv_sem.at[part, step],
                device_id=partner_of(name, weight),
                device_id_type=pl.DeviceIdType.MESH,
            )
            copy.start()
            copies.append(copy)
        if step == 0:
            for copy in swaps:
                copy.start()
        for part in range(2):
            copies[2 * step + part].wait_recv()
            name, weight = orders[part][step]
            offsets[part] = offsets[part] - bit_of(name, weight) * held
    for copy in copies:
        copy.wait_send()
    for copy in swaps:
        copy.wait()


def gather_windows(orders, win_a, win_b, cells):
    count = 1 << len(orders[0])
    stages = len(orders[0])
    return pl.pallas_call(
        functools.partial(gather_kernel, orders),
        out_shape=(
            jax.ShapeDtypeStruct((count,) + win_a.shape, win_a.dtype),
            jax.ShapeDtypeStruct((count,) + win_b.shape, win_b.dtype),
            jax.ShapeDtypeStruct(cells.shape, cells.dtype),
        ),
        in_specs=[pl.BlockSpec(memory_space=pltpu.VMEM)] * 2
        + [pl.BlockSpec(memory_space=pltpu.HBM)],
        out_specs=[pl.BlockSpec(memory_space=pltpu.HBM)] * 3,
        scratch_shapes=[
            pltpu.SemaphoreType.DMA((3,)),
            pltpu.SemaphoreType.DMA((2, stages)),
            pltpu.SemaphoreType.DMA((2, stages)),
            pltpu.SemaphoreType.DMA((cells.shape[0] - 1,)),
            pltpu.SemaphoreType.DMA((cells.shape[0] - 1,)),
        ],
        compiler_params=pltpu.CompilerParams(
            collective_id=0, has_side_effects=True, vmem_limit_bytes=62 * 1024 * 1024
        ),
    )(win_a, win_b, cells)


def reduce_kernel(
    orders,
    in_a,
    in_b,
    cells,
    out_a,
    out_b,
    cells_out,
    land_a,
    land_b,
    local_sem,
    send_sem,
    recv_sem,
    swap_send,
    swap_recv,
):
    ins, outs, lands = (in_a, in_b), (out_a, out_b), (land_a, land_b)
    stage_count = len(orders[0])
    place = lax.axis_index("seq")
    local = pltpu.make_async_copy(cells.at[place], cells_out.at[place], local_sem.at[0])
    local.start()
    greet(orders)
    swaps = exchange_copies(cells, cells_out, swap_send, swap_recv)
    copies = []

    def source(part, step, keep):
        name, weight = orders[part][stage_count - 1 - step]
        held = 1 << (stage_count - 1 - step)
        side = bit_of(name, weight)
        side = side if keep else 1 - side
        if step == 0:
            return ins[part].at[pl.ds(side * held, held)]
        base = (1 << stage_count) - (1 << (stage_count - step + 1))
        return lands[part].at[pl.ds(base + side * held, held)]

    for step in range(stage_count):
        held = 1 << (stage_count - 1 - step)
        base = (1 << stage_count) - (1 << (stage_count - step))
        for part in range(2):
            name, weight = orders[part][stage_count - 1 - step]
            copy = pltpu.make_async_remote_copy(
                src_ref=source(part, step, False),
                dst_ref=lands[part].at[pl.ds(base, held)],
                send_sem=send_sem.at[part, step],
                recv_sem=recv_sem.at[part, step],
                device_id=partner_of(name, weight),
                device_id_type=pl.DeviceIdType.MESH,
            )
            copy.start()
            copies.append(copy)
        if step == 0:
            for copy in swaps:
                copy.start()
        for part in range(2):
            copies[2 * step + part].wait_recv()
            mine = source(part, step, True)
            if step == stage_count - 1:
                outs[part][...] = mine[0].astype(jnp.float32) + lands[part][base].astype(
                    jnp.float32
                )
            else:

                def add_one(index, carry, mine=mine, part=part, base=base):
                    land = lands[part].at[base + index]
                    total = mine[index].astype(jnp.float32) + land[...].astype(jnp.float32)
                    land[...] = total.astype(land.dtype)
                    return carry

                lax.fori_loop(0, held, add_one, 0)
    for copy in copies:
        copy.wait_send()
    for copy in swaps:
        copy.wait()
    local.wait()


def reduce_windows(orders, rows_a, rows_b, cells):
    count = 1 << len(orders[0])
    stages = len(orders[0])
    return pl.pallas_call(
        functools.partial(reduce_kernel, orders),
        out_shape=(
            jax.ShapeDtypeStruct(rows_a.shape[1:], jnp.float32),
            jax.ShapeDtypeStruct(rows_b.shape[1:], jnp.float32),
            jax.ShapeDtypeStruct(cells.shape, cells.dtype),
        ),
        in_specs=[pl.BlockSpec(memory_space=pltpu.VMEM)] * 2
        + [pl.BlockSpec(memory_space=pltpu.HBM)],
        out_specs=[pl.BlockSpec(memory_space=pltpu.VMEM)] * 2
        + [pl.BlockSpec(memory_space=pltpu.HBM)],
        scratch_shapes=[
            pltpu.VMEM((count - 1,) + rows_a.shape[1:], rows_a.dtype),
            pltpu.VMEM((count - 1,) + rows_b.shape[1:], rows_b.dtype),
            pltpu.SemaphoreType.DMA((1,)),
            pltpu.SemaphoreType.DMA((2, stages)),
            pltpu.SemaphoreType.DMA((2, stages)),
            pltpu.SemaphoreType.DMA((cells.shape[0] - 1,)),
            pltpu.SemaphoreType.DMA((cells.shape[0] - 1,)),
        ],
        compiler_params=pltpu.CompilerParams(
            collective_id=1, has_side_effects=True, vmem_limit_bytes=62 * 1024 * 1024
        ),
    )(rows_a, rows_b, cells)


RES_SQUARES = 7 * C * C
RES_ROWS = (RES_SQUARES + TE * C + 8 * C) // 128
INNER = HEADS * HD
TF_SIZES = (3 * C * INNER, INNER * C, C * F, F * C, 6 * C, 3 * F)
TF_ROWS = sum(TF_SIZES) // 128


def place_maps(orders, mesh_sizes):
    count = 1 << len(orders[0])
    return [[owner_place(orders[part], mesh_sizes, i) for i in range(count)] for part in range(2)]


def matrix_views():
    views = []
    row = 0
    for rows, width in ((6 * C, C), (C, C), (TE, C), (8, C)):
        views.append((0, row, rows, width))
        row += rows * width // 128
    row = 0
    for rows, width in ((C, 3 * INNER), (INNER, C), (C, F), (F, C), (6, C), (3, F)):
        views.append((1, row, rows, width))
        row += rows * width // 128
    return views


def assemble(places, lengths_now, in_a, in_b, *refs):
    outs, flats = refs[:10], refs[10:12]
    count = len(places[0])
    for part, ref in enumerate((in_a, in_b)):
        flat = flats[part]
        for i in range(count):
            start, lead = divmod(i * lengths_now[part], 128)
            rows = -(-(lead + lengths_now[part]) // 128)
            if lead:
                edge = flat[start : start + 1, :]
            flat[start : start + rows, :] = ref[places[part][i]].astype(jnp.float32)[:rows]
            if lead:
                flat[start : start + 1, :] = flat[start : start + 1, :] + edge
    for out, (part, row, rows, width) in zip(outs, matrix_views()):
        stride = width // 128
        for lane in range(stride):
            piece = flats[part][pl.ds(row + lane, rows, stride=stride), :]
            out[:, lane * 128 : (lane + 1) * 128] = piece.astype(out.dtype)


def cut(places, lengths_now, *refs):
    ins, outs, flats = refs[:10], refs[10:12], refs[12:14]
    count = len(places[0])
    for ref, (part, row, rows, width) in zip(ins, matrix_views()):
        stride = width // 128
        for lane in range(stride):
            flats[part][pl.ds(row + lane, rows, stride=stride), :] = ref[
                :, lane * 128 : (lane + 1) * 128
            ]
    for part in range(2):
        for i in range(count):
            start, lead = divmod(i * lengths_now[part], 128)
            rows = outs[part].shape[1]
            outs[part][places[part][i]] = flats[part][start : start + rows, :].astype(
                outs[part].dtype
            )


def flat_index(mesh_sizes):
    index = 0
    for name, size in mesh_sizes:
        index = index * size + lax.axis_index(name)
    return index


def to_window(master, rows, owner):
    lead = (owner * master.shape[0]) % 128
    window = jnp.zeros((rows * 128,), jnp.bfloat16)
    return lax.dynamic_update_slice(window, master.astype(jnp.bfloat16), (lead,)).reshape(rows, 128)


def from_window(window, length_now, owner):
    lead = (owner * length_now) % 128
    return lax.dynamic_slice(window.reshape(-1), (lead,), (length_now,))


SIN_TERMS = (
    3.141592640063848,
    -5.167710072816043,
    2.5500772667383647,
    -0.5982893715546711,
    0.07765328748430061,
)
COS_TERMS = (
    0.9999999530157438,
    -4.934792793539851,
    4.058410463392346,
    -1.3318699300230954,
    0.21967444597863747,
)
ROUND_SHIFT = 12582912.0


def mm(left, right):
    return jnp.dot(left, right, preferred_element_type=jnp.float32)


def mm_right(left, right):
    return lax.dot_general(
        left, right, (((1,), (1,)), ((), ())), preferred_element_type=jnp.float32
    )


def mm_left(left, right):
    return lax.dot_general(
        left, right, (((0,), (0,)), ((), ())), preferred_element_type=jnp.float32
    )


def column_sum(cells):
    return jnp.sum(cells, axis=0, keepdims=True)


def sin_cos(half_turns):
    rest = half_turns - ((half_turns + ROUND_SHIFT) - ROUND_SHIFT)
    square = rest * rest
    sine = SIN_TERMS[-1]
    for term in SIN_TERMS[-2::-1]:
        sine = sine * square + term
    cosine = COS_TERMS[-1]
    for term in COS_TERMS[-2::-1]:
        cosine = cosine * square + term
    return (sine * rest, cosine)


def mish_value(signal):
    expo = jnp.exp(jnp.minimum(signal, 20.0))
    upper = expo * (expo + 2.0)
    return signal * (upper / (upper + 2.0))


def mish_slope(signal):
    expo = jnp.exp(jnp.minimum(signal, 20.0))
    upper = expo * (expo + 2.0)
    inverse = 1.0 / (upper + 2.0)
    return upper * inverse + signal * (4.0 * expo * (1.0 + expo)) * (inverse * inverse)


def row_norm(signal):
    center = signal - jnp.mean(signal, axis=-1, keepdims=True)
    spread = jnp.mean(center * center, axis=-1, keepdims=True)
    inverse = lax.rsqrt(spread + EPSILON)
    return (center * inverse, inverse)


def row_norm_back(grad_out, normed, inverse, gain_row):
    inner_grad = grad_out * gain_row
    first = jnp.mean(inner_grad, axis=-1, keepdims=True)
    second = jnp.mean(inner_grad * normed, axis=-1, keepdims=True)
    return (inner_grad - first - normed * second) * inverse


def step_kernel(
    places,
    shard_lengths,
    lengths_ref,
    place_ref,
    cells_ref,
    time_ref,
    win_a,
    win_b,
    results_ref,
    cut_a,
    cut_b,
    convs_ref,
    res_ref,
    timew_ref,
    rows_ref,
    qkv_ref,
    out_ref,
    up_ref,
    down_ref,
    tf_rows_ref,
    wide_ref,
    gconvs_ref,
    gres_ref,
    gtimew_ref,
    grows_ref,
    gqkv_ref,
    gout_ref,
    gup_ref,
    gdown_ref,
    gtf_ref,
    gwide_ref,
    flat_a,
    flat_b,
    time_rows,
    gtime_rows,
    pad,
    col_one,
    col_two,
    col_grad,
    z_one,
    z_two,
    block,
    grad_mid,
    grad_norm,
    attn_in,
    heads_q,
    heads_k,
    heads_v,
    heads_g,
    attn_vals,
    probs,
    snake,
    grad_up,
    ff_in,
    grad_attn,
    grad_key,
    grad_value,
    grad_query,
    grad_qkv,
    grad_skip,
):
    frames = z_one.shape[0]
    tiles, _, tile, _ = cells_ref.shape
    utt = pl.program_id(0)
    row_at = place_ref[0] * pl.num_programs(0) + utt
    length_now = lengths_ref[row_at]
    number = length_now.astype(jnp.float32) * (C // GROUPS)
    weight_refs = (
        convs_ref,
        res_ref,
        timew_ref,
        rows_ref,
        qkv_ref,
        out_ref,
        up_ref,
        down_ref,
        tf_rows_ref,
        wide_ref,
    )
    grad_refs = (
        gconvs_ref,
        gres_ref,
        gtimew_ref,
        grows_ref,
        gqkv_ref,
        gout_ref,
        gup_ref,
        gdown_ref,
        gtf_ref,
        gwide_ref,
    )

    @pl.when(utt == 0)
    def begin():
        assemble(places, shard_lengths, win_a, win_b, *weight_refs, flat_a, flat_b)
        for ref in grad_refs:
            ref[...] = jnp.zeros_like(ref)
        gtime_rows[...] = jnp.zeros_like(gtime_rows)
        low = mish_value(time_ref[...]).astype(jnp.bfloat16)
        time_rows[...] = mm(low, timew_ref[...]) + rows_ref[7:8, :]

    time_row = time_rows[pl.ds(row_at, 1), :]
    edge = jnp.zeros((8, C), jnp.float32)
    pad[0:8, :] = edge
    pad[frames + 8 : frames + 16, :] = edge
    group_row = lax.broadcasted_iota(jnp.int32, (C, C), 0) // (C // GROUPS)
    group_column = lax.broadcasted_iota(jnp.int32, (C, C), 1) // (C // GROUPS)
    group_ones = (group_row == group_column).astype(jnp.float32)
    lane = lax.broadcasted_iota(jnp.int32, (1, INNER), 1) // HD
    head_masks = [(lane == head).astype(jnp.float32) for head in range(HEADS)]
    key_bias = jnp.where(
        lax.broadcasted_iota(jnp.int32, (1, frames), 1) < length_now, 0.0, MASK_FILL
    )

    def rows_at(index, lead=0):
        return pl.ds(pl.multiple_of(index * tile + lead, 8), tile)

    def tile_mask(index):
        ids = lax.broadcasted_iota(jnp.int32, (tile, 1), 0) + index * tile
        return (ids < length_now).astype(jnp.float32)

    def group_sum(row):
        wide = jnp.broadcast_to(row, (8, C))
        return jnp.dot(
            wide,
            group_ones,
            precision=lax.Precision.HIGHEST,
            preferred_element_type=jnp.float32,
        )[0:1]

    def build_columns(target):
        for index in range(tiles):
            start = index * tile
            for tap in range(3):
                piece = pad[start + 7 + tap : start + 7 + tap + tile, :]
                target[start : start + tile, tap * C : (tap + 1) * C] = piece.astype(jnp.bfloat16)

    def loop(body):
        def wrapped(index, carry):
            body(index)
            return carry

        lax.fori_loop(0, tiles, wrapped, 0)

    def conv_stage(columns, base, bias_at, target):
        def one(index, carry):
            rows = rows_at(index)
            cells = mm(columns[rows, :], convs_ref[base : base + 3 * C, :])
            cells = cells + rows_ref[bias_at : bias_at + 1, :]
            target[rows, :] = cells
            masked = cells * tile_mask(index)
            return (carry[0] + column_sum(masked), carry[1] + column_sum(masked * masked))

        zero = jnp.zeros((1, C), jnp.float32)
        total, squares = lax.fori_loop(0, tiles, one, (zero, zero))
        mean_row = group_sum(total) / number
        inv_row = lax.rsqrt(group_sum(squares) / number - mean_row * mean_row + EPSILON)
        return (mean_row, inv_row)

    def copy_in(index):
        pad[rows_at(index, 8), :] = cells_ref[index, 0, :, 0:C].astype(jnp.float32)

    loop(copy_in)
    build_columns(col_one)
    mean_one, inv_one = conv_stage(col_one, 0, 0, z_one)

    def hidden(index):
        normed = (z_one[rows_at(index), :] - mean_one) * inv_one
        act = mish_value(normed * rows_ref[1:2, :] + rows_ref[2:3, :])
        pad[rows_at(index, 8), :] = (act + time_row) * tile_mask(index)

    loop(hidden)
    build_columns(col_two)
    mean_two, inv_two = conv_stage(col_two, 3 * C, 3, z_two)

    def enter(index):
        rows = rows_at(index)
        normed = (z_two[rows, :] - mean_two) * inv_two
        act = mish_value(normed * rows_ref[4:5, :] + rows_ref[5:6, :]) * tile_mask(index)
        state = act + mm(cells_ref[index, 0, :, 0:C], res_ref[...]) + rows_ref[6:7, :]
        block[rows, :] = state
        normed, _ = row_norm(state)
        low = (normed * tf_rows_ref[0:1, :] + tf_rows_ref[1:2, :]).astype(jnp.bfloat16)
        attn_in[rows, :] = low
        parts = mm(low, qkv_ref[...]).astype(jnp.bfloat16).astype(jnp.float32)
        query = parts[:, :INNER] * SCORE_SCALE
        for head in range(HEADS):
            heads_q[head, rows, :] = (query * head_masks[head]).astype(jnp.bfloat16)
            heads_k[head, rows, :] = (parts[:, INNER : 2 * INNER] * head_masks[head]).astype(
                jnp.bfloat16
            )
            heads_v[head, rows, :] = (parts[:, 2 * INNER :] * head_masks[head]).astype(
                jnp.bfloat16
            )

    loop(enter)

    def attend(index):
        rows = rows_at(index)
        total = jnp.zeros((tile, INNER), jnp.float32)
        for head in range(HEADS):
            scores = mm_right(heads_q[head, rows, :], heads_k[head]) + key_bias
            expo = jnp.exp(scores - jnp.max(scores, axis=-1, keepdims=True))
            chance = expo * (1.0 / jnp.sum(expo, axis=-1, keepdims=True))
            probs[head, rows, :] = chance
            total = total + mm(chance.astype(jnp.bfloat16), heads_v[head])
        attn_vals[rows, :] = total.astype(jnp.bfloat16)

    loop(attend)

    def feed(index):
        rows = rows_at(index)
        mid = block[rows, :] + mm(attn_vals[rows, :], out_ref[...]) + tf_rows_ref[2:3, :]
        normed, inverse = row_norm(mid)
        low = (normed * tf_rows_ref[3:4, :] + tf_rows_ref[4:5, :]).astype(jnp.bfloat16)
        ff_in[rows, :] = low
        grad_low = cells_ref[index, 0, :, C : 2 * C]
        result = jnp.zeros((tile, C), jnp.float32)
        grad_in = jnp.zeros((tile, C), jnp.float32)
        for chunk in range(F // 256):
            lanes = slice(chunk * 256, (chunk + 1) * 256)
            up_out = mm(low, up_ref[:, lanes]) + wide_ref[0:1, lanes]
            grad_snake = mm_right(grad_low, down_ref[lanes, :])
            speed = jnp.exp(wide_ref[1:2, lanes])
            depth = 1.0 / (jnp.exp(wide_ref[2:3, lanes]) + 1e-09)
            half_turns = up_out * (speed * (1.0 / math.pi))
            sine, cosine = sin_cos(half_turns)
            square = sine * sine
            value = (up_out + square * depth).astype(jnp.bfloat16)
            snake[rows, lanes] = value
            result = result + mm(value, down_ref[lanes, :])
            slope = (grad_snake * (2.0 * depth)) * (sine * cosine)
            grad_here = (grad_snake + slope * speed).astype(jnp.bfloat16)
            grad_up[rows, lanes] = grad_here
            grad_in = grad_in + mm_right(grad_here, up_ref[:, lanes])
            gwide_ref[0:1, lanes] += column_sum(grad_here.astype(jnp.float32))
            gwide_ref[1:2, lanes] += column_sum(slope * half_turns)
            gwide_ref[2:3, lanes] += column_sum(grad_snake * square)
        results_ref[index, 0, :, 0:C] = ((mid + result + tf_rows_ref[5:6, :]) * tile_mask(index)).astype(
            jnp.bfloat16
        )
        grad_wide = grad_low.astype(jnp.float32)
        gtf_ref[5:6, :] += column_sum(grad_wide)
        gtf_ref[3:4, :] += column_sum(grad_in * normed)
        gtf_ref[4:5, :] += column_sum(grad_in)
        grad_state = grad_wide + row_norm_back(grad_in, normed, inverse, tf_rows_ref[3:4, :])
        grad_mid[rows, :] = grad_state
        grad_state = grad_state.astype(jnp.bfloat16)
        grad_attn[rows, :] = grad_state
        gtf_ref[2:3, :] += column_sum(grad_state.astype(jnp.float32))
        grad_vals = mm_right(grad_state, out_ref[...]).astype(jnp.bfloat16).astype(jnp.float32)
        for head in range(HEADS):
            heads_g[head, rows, :] = (grad_vals * head_masks[head]).astype(jnp.bfloat16)

    loop(feed)

    def feed_weights(index, carry):
        lanes = pl.ds(pl.multiple_of(index * 256, 256), 256)
        grads = cells_ref[:, 0, :, C : 2 * C].reshape(frames, C)
        gdown_ref[lanes, :] += mm_left(snake[:, lanes], grads)
        gup_ref[:, lanes] += mm_left(ff_in[...], grad_up[:, lanes])
        return carry

    lax.fori_loop(0, F // 256, feed_weights, 0)
    gout_ref[...] += mm_left(attn_vals[...], grad_attn[...])
    grad_key[...] = jnp.zeros_like(grad_key)
    grad_value[...] = jnp.zeros_like(grad_value)

    def attend_back(index):
        rows = rows_at(index)
        total = jnp.zeros((tile, INNER), jnp.float32)
        scores_low, chances_low = [], []
        for head in range(HEADS):
            grad_out = heads_g[head, rows, :]
            chance = probs[head, rows, :]
            grad_probs = mm_right(grad_out, heads_v[head])
            dot_row = jnp.sum(chance * grad_probs, axis=-1, keepdims=True)
            grad_scores = (chance * (grad_probs - dot_row)).astype(jnp.bfloat16)
            total = total + mm(grad_scores, heads_k[head])
            scores_low.append(grad_scores)
            chances_low.append(chance.astype(jnp.bfloat16))
        both = (HEADS * tile, INNER)
        grad_key[...] += mm_left(
            jnp.concatenate(scores_low, axis=0), heads_q[:, rows, :].reshape(both)
        )
        grad_value[...] += mm_left(
            jnp.concatenate(chances_low, axis=0), heads_g[:, rows, :].reshape(both)
        )
        grad_query[rows, :] = total * SCORE_SCALE

    loop(attend_back)

    def leave(index, carry):
        rows = rows_at(index)
        grad_qkv[rows, 0:INNER] = grad_query[rows, :].astype(jnp.bfloat16)
        grad_qkv[rows, INNER : 2 * INNER] = grad_key[rows, :].astype(jnp.bfloat16)
        grad_qkv[rows, 2 * INNER : 3 * INNER] = grad_value[rows, :].astype(jnp.bfloat16)
        grad_in = mm_right(grad_qkv[rows, :], qkv_ref[...])
        normed, inverse = row_norm(block[rows, :])
        gtf_ref[0:1, :] += column_sum(grad_in * normed)
        gtf_ref[1:2, :] += column_sum(grad_in)
        grad_state = grad_mid[rows, :] + row_norm_back(
            grad_in, normed, inverse, tf_rows_ref[0:1, :]
        )
        low = grad_state.astype(jnp.bfloat16)
        grad_skip[rows, :] = low
        grows_ref[6:7, :] += column_sum(low.astype(jnp.float32))
        normed = (z_two[rows, :] - mean_two) * inv_two
        grad_here = (
            mish_slope(normed * rows_ref[4:5, :] + rows_ref[5:6, :])
            * tile_mask(index)
            * grad_state
        )
        grad_norm[rows, :] = grad_here
        return (carry[0] + column_sum(grad_here), carry[1] + column_sum(grad_here * normed))

    zero = jnp.zeros((1, C), jnp.float32)

    def norm_back(target, mean_row, inv_row, gain_at, bias_at, shift_sum, gain_sum):
        gain_row = rows_ref[gain_at : gain_at + 1, :]
        grows_ref[gain_at : gain_at + 1, :] += gain_sum
        grows_ref[gain_at + 1 : gain_at + 2, :] += shift_sum
        first = group_sum(shift_sum * gain_row) / number
        second = group_sum(gain_sum * gain_row) / number

        def one(index):
            rows = rows_at(index)
            normed = (target[rows, :] - mean_row) * inv_row
            cells = inv_row * (
                grad_norm[rows, :] * gain_row - tile_mask(index) * (first + normed * second)
            )
            cells = cells.astype(jnp.bfloat16).astype(jnp.float32)
            grows_ref[bias_at : bias_at + 1, :] += column_sum(cells)
            pad[rows_at(index, 8), :] = cells

        loop(one)
        build_columns(col_grad)

    def conv_back(rows, base):
        total = mm_right(col_grad[rows, 2 * C : 3 * C], convs_ref[base : base + C, :])
        total = total + mm_right(col_grad[rows, C : 2 * C], convs_ref[base + C : base + 2 * C, :])
        return total + mm_right(col_grad[rows, 0:C], convs_ref[base + 2 * C : base + 3 * C, :])

    def conv_weights(columns, base):
        for tap in range(3):
            gconvs_ref[base + tap * C : base + (tap + 1) * C, :] += mm_left(
                columns[:, tap * C : (tap + 1) * C], col_grad[:, C : 2 * C]
            )

    shift_sum, gain_sum = lax.fori_loop(0, tiles, leave, (zero, zero))
    norm_back(z_two, mean_two, inv_two, 4, 3, shift_sum, gain_sum)
    conv_weights(col_two, 3 * C)

    def hidden_back(index, carry):
        rows = rows_at(index)
        grad_here = conv_back(rows, 3 * C) * tile_mask(index)
        time_sum = column_sum(grad_here)
        normed = (z_one[rows, :] - mean_one) * inv_one
        grad_here = mish_slope(normed * rows_ref[1:2, :] + rows_ref[2:3, :]) * grad_here
        grad_norm[rows, :] = grad_here
        return (
            carry[0] + column_sum(grad_here),
            carry[1] + column_sum(grad_here * normed),
            carry[2] + time_sum,
        )

    shift_sum, gain_sum, time_sum = lax.fori_loop(0, tiles, hidden_back, (zero, zero, zero))
    grows_ref[7:8, :] += time_sum
    gtime_rows[pl.ds(row_at, 1), :] = time_sum
    norm_back(z_one, mean_one, inv_one, 1, 0, shift_sum, gain_sum)
    conv_weights(col_one, 0)

    def finish(index):
        rows = rows_at(index)
        total = conv_back(rows, 0) + mm_right(grad_skip[rows, :], res_ref[...])
        results_ref[index, 0, :, C : 2 * C] = (total * tile_mask(index)).astype(jnp.bfloat16)

    loop(finish)
    gres_ref[...] += mm_left(cells_ref[:, 0, :, 0:C].reshape(frames, C), grad_skip[...])
    gqkv_ref[...] += mm_left(attn_in[...], grad_qkv[...])

    @pl.when(utt == pl.num_programs(0) - 1)
    def end():
        low_side = jnp.exp(wide_ref[2:3, :])
        depth = 1.0 / (low_side + 1e-09)
        gwide_ref[1:2, :] = gwide_ref[1:2, :] * math.pi
        gwide_ref[2:3, :] = -gwide_ref[2:3, :] * low_side * depth * depth
        time_low = mish_value(time_ref[...]).astype(jnp.bfloat16).astype(jnp.float32)
        gtimew_ref[...] = lax.dot_general(
            time_low,
            gtime_rows[...],
            (((0,), (0,)), ((), ())),
            precision=lax.Precision.HIGHEST,
            preferred_element_type=jnp.float32,
        )
        cut(places, shard_lengths, *grad_refs, cut_a, cut_b, flat_a, flat_b)


def whole_step(places, shard_lengths, lengths, place, cells, time_embed, windows):
    tiles, utts, tile, _ = cells.shape
    frames = tiles * tile
    by_utt = pl.BlockSpec((tiles, 1, tile, 2 * C), lambda u, n, p: (0, u, 0, 0))

    def fixed(array):
        return pl.BlockSpec(
            array.shape, lambda u, n, p: (0,) * array.ndim, pipeline_mode=pl.Buffered(1)
        )

    f32, low = jnp.float32, jnp.bfloat16
    weight_kinds = [
        ((rows, width), f32 if index in (3, 8, 9) else low)
        for index, (part, row, rows, width) in enumerate(matrix_views())
    ]
    scratch = weight_kinds + [(shape, f32) for shape, kind in weight_kinds]
    scratch += [
        ((RES_ROWS + 24, 128), f32),
        ((TF_ROWS + 28, 128), f32),
        (time_embed.shape[:1] + (C,), f32),
        (time_embed.shape[:1] + (C,), f32),
        ((frames + 16, C), f32),
        ((frames, 3 * C), low),
        ((frames, 3 * C), low),
        ((frames, 3 * C), low),
        ((frames, C), f32),
        ((frames, C), f32),
        ((frames, C), f32),
        ((frames, C), f32),
        ((frames, C), f32),
        ((frames, C), low),
        ((HEADS, frames, INNER), low),
        ((HEADS, frames, INNER), low),
        ((HEADS, frames, INNER), low),
        ((HEADS, frames, INNER), low),
        ((frames, INNER), low),
        ((HEADS, frames, frames), f32),
        ((frames, F), low),
        ((frames, F), low),
        ((frames, C), low),
        ((frames, C), low),
        ((frames, INNER), f32),
        ((frames, INNER), f32),
        ((frames, INNER), f32),
        ((frames, 3 * INNER), low),
        ((frames, C), low),
    ]
    return pl.pallas_call(
        functools.partial(step_kernel, places, shard_lengths),
        grid_spec=pltpu.PrefetchScalarGridSpec(
            num_scalar_prefetch=2,
            grid=(utts,),
            in_specs=[by_utt] + [fixed(array) for array in (time_embed, *windows)],
            out_specs=[by_utt] + [fixed(array) for array in windows],
            scratch_shapes=[pltpu.VMEM(shape, kind) for shape, kind in scratch],
        ),
        out_shape=[jax.ShapeDtypeStruct(array.shape, low) for array in (cells, *windows)],
        compiler_params=pltpu.CompilerParams(
            dimension_semantics=("arbitrary",), vmem_limit_bytes=61 * 1024 * 1024
        ),
    )(lengths, place, cells, time_embed, *windows)


def prepare_kernel(
    lengths_ref, place_ref, inputs_ref, encoded_ref, durations_ref, cotangent_ref, out_ref
):
    group, frames, _ = inputs_ref.shape
    phones = durations_ref.shape[2]
    first = place_ref[0] * frames
    before = lax.broadcasted_iota(jnp.int32, (phones, phones), 0)
    after = lax.broadcasted_iota(jnp.int32, (phones, phones), 1)
    upper = (before <= after).astype(jnp.bfloat16)
    last = lax.broadcasted_iota(jnp.int32, (1, phones), 1) == phones - 1
    ids = lax.broadcasted_iota(jnp.int32, (frames, 1), 0) + first
    times = ids.astype(jnp.float32)
    for utt in range(group):
        durations = durations_ref[utt].astype(jnp.float32)
        wide = jnp.broadcast_to(durations, (16, phones)).astype(jnp.bfloat16)
        ends = mm(wide, upper)[0:1]
        starts = ends - durations
        ends = jnp.where(last, 1e9, ends)
        picked = jnp.where((times >= starts) & (times < ends), 1.0, 0.0).astype(jnp.bfloat16)
        table = encoded_ref[utt]
        high = table.astype(jnp.bfloat16)
        rest = table - high.astype(jnp.float32)
        middle = rest.astype(jnp.bfloat16)
        low = (rest - middle.astype(jnp.float32)).astype(jnp.bfloat16)
        rows = (mm(picked, high) + mm(picked, middle)) + mm(picked, low)
        mask = (ids < lengths_ref[pl.program_id(0) * group + utt]).astype(jnp.float32)
        out_ref[0, utt, :, 0:C] = ((inputs_ref[utt] + rows) * mask).astype(jnp.bfloat16)
        out_ref[0, utt, :, C : 2 * C] = (cotangent_ref[utt] * mask).astype(jnp.bfloat16)


def prepare(inputs, encoded, durations, lengths, place, cotangent):
    utts, frames, _ = inputs.shape
    phones = durations.shape[1]
    seq_size = lax.axis_size("seq")
    group = utts // seq_size
    by_group = lambda s, n, p: (s, 0, 0)
    return pl.pallas_call(
        prepare_kernel,
        grid_spec=pltpu.PrefetchScalarGridSpec(
            num_scalar_prefetch=2,
            grid=(seq_size,),
            in_specs=[
                pl.BlockSpec((group, frames, C), by_group),
                pl.BlockSpec((group, phones, C), by_group),
                pl.BlockSpec((group, 1, phones), by_group),
                pl.BlockSpec((group, frames, C), by_group),
            ],
            out_specs=pl.BlockSpec((1, group, frames, 2 * C), lambda s, n, p: (s, 0, 0, 0)),
        ),
        out_shape=jax.ShapeDtypeStruct((seq_size, group, frames, 2 * C), jnp.bfloat16),
        compiler_params=pltpu.CompilerParams(dimension_semantics=("arbitrary",)),
    )(lengths, place, inputs, encoded, durations[:, None, :], cotangent)


def per_device(
    inputs,
    encoded,
    durations,
    lengths,
    time_embed,
    cotangent,
    res_master,
    res_moment,
    res_average,
    tf_master,
    tf_moment,
    tf_average,
):
    utts_here, local_len, _ = inputs.shape
    key_total = local_len * lax.axis_size("seq")
    place = jnp.full((1,), lax.axis_index("seq"), jnp.int32)
    cells = prepare(inputs, encoded, durations, lengths, place, cotangent)
    mesh_sizes = [(name, lax.axis_size(name)) for name in ("dp", "seq")]
    orders = part_orders(mesh_sizes)
    places = place_maps(orders, mesh_sizes)
    owner = flat_index(mesh_sizes)
    shard_lengths = (res_master.shape[0], tf_master.shape[0])
    window_sizes = [window_rows(size, len(places[0])) for size in shard_lengths]
    *gathered, cells = gather_windows(
        orders,
        to_window(res_master, window_sizes[0], owner),
        to_window(tf_master, window_sizes[1], owner),
        cells,
    )
    results, *cuts = whole_step(
        places, shard_lengths, lengths, place, cells, time_embed, gathered
    )
    *summed, results = reduce_windows(orders, *cuts, results)
    results = results.reshape(utts_here, local_len, 2 * C)
    res_share = from_window(summed[0], shard_lengths[0], owner)
    tf_share = from_window(summed[1], shard_lengths[1], owner)
    tokens_total = utts_here * key_total * lax.axis_size("dp")
    rate = LEARN_BASE / math.sqrt(tokens_total)
    res_new, res_moment_new, res_average_new, res_low = update(
        res_master, res_moment, res_average, res_share, rate
    )
    tf_new, tf_moment_new, tf_average_new, tf_low = update(
        tf_master, tf_moment, tf_average, tf_share, rate
    )
    return (
        results[:, :, :C].astype(jnp.float32),
        results[:, :, C:].astype(jnp.float32),
        res_share,
        tf_share,
        res_new,
        tf_new,
        res_moment_new,
        tf_moment_new,
        res_average_new,
        tf_average_new,
        res_low,
        tf_low,
    )


def solution(mesh):
    placed = (
        P("dp", "seq", None),
        P("dp", None, None),
        P("dp", None),
        P("dp"),
        P("dp", None),
        P("dp", "seq", None),
        P(("dp", "seq")),
        P(("dp", "seq")),
        P(("dp", "seq")),
        P(("dp", "seq")),
        P(("dp", "seq")),
        P(("dp", "seq")),
    )
    return jax.shard_map(
        per_device,
        mesh=mesh,
        in_specs=placed,
        out_specs=(
            P("dp", "seq", None),
            P("dp", "seq", None),
            P(("dp", "seq")),
            P(("dp", "seq")),
            P(("dp", "seq")),
            P(("dp", "seq")),
            P(("dp", "seq")),
            P(("dp", "seq")),
            P(("dp", "seq")),
            P(("dp", "seq")),
            P(("dp", "seq")),
            P(("dp", "seq")),
        ),
        check_vma=False,
    )
```

```python
import functools
import math

import jax
import jax.numpy as jnp
from jax import lax
from jax.experimental import pallas as pl
from jax.experimental.pallas import tpu as pltpu
from jax.sharding import PartitionSpec as P

C = 256
GROUPS = 8
TE = 1024
HEADS = 2
HD = 64
F = 1024


EPSILON = 1e-05
SCORE_SCALE = 0.125
MOMENTUM = 0.9
AVERAGE_DECAY = 0.99
LEARN_BASE = 0.015
MASK_FILL = -1e30


def update(master, moment, average, grad, rate):
    moment_new = MOMENTUM * moment + grad
    master_new = master - rate * (grad + MOMENTUM * moment_new)
    average_new = AVERAGE_DECAY * average + (1.0 - AVERAGE_DECAY) * master_new
    return (master_new, moment_new, average_new, master_new.astype(jnp.bfloat16))


def axis_bits(mesh_sizes):
    bits = []
    for name, size in mesh_sizes:
        weight = size // 2
        while weight >= 1:
            bits.append((name, weight))
            weight //= 2
    return bits


def part_orders(mesh_sizes):
    wide = axis_bits(mesh_sizes[:1])
    near = axis_bits(mesh_sizes[1:])
    first = near[:-1] + wide + near[-1:]
    second = near[:-1] + wide[-1:] + wide[:-1] + near[-1:]
    return (first, second)


def owner_place(order, mesh_sizes, owner):
    strides, stride = {}, 1
    for name, size in reversed(mesh_sizes):
        strides[name] = (stride, size)
        stride *= size
    place = 0
    for step, (name, weight) in enumerate(order):
        base, size = strides[name]
        place += ((owner // base) % size // weight % 2) << step
    return place


def window_rows(length_now, count):
    most = max((i * length_now) % 128 + length_now for i in range(count))
    return -(-most // (128 * 16)) * 16


def bit_of(name, weight):
    return (lax.axis_index(name) // weight) % 2


def partner_of(name, weight):
    return {name: lax.axis_index(name) + (1 - 2 * bit_of(name, weight)) * weight}


def seq_neighbour(step):
    return lax.rem(lax.axis_index("seq") + step, lax.axis_size("seq"))


def greet(orders):
    barrier = pltpu.get_barrier_semaphore()
    others = [partner_of(name, weight) for name, weight in orders[0] if name != "seq"]
    others += [{"seq": seq_neighbour(step)} for step in range(1, lax.axis_size("seq"))]
    for other in others:
        pl.semaphore_signal(
            barrier, inc=1, device_id=other, device_id_type=pl.DeviceIdType.MESH
        )
    pl.semaphore_wait(barrier, len(others))


def exchange_copies(cells, cells_out, swap_send, swap_recv):
    copies = []
    for step in range(1, lax.axis_size("seq")):
        target = seq_neighbour(step)
        copies.append(
            pltpu.make_async_remote_copy(
                src_ref=cells.at[target],
                dst_ref=cells_out.at[lax.axis_index("seq")],
                send_sem=swap_send.at[step - 1],
                recv_sem=swap_recv.at[step - 1],
                device_id={"seq": target},
                device_id_type=pl.DeviceIdType.MESH,
            )
        )
    return copies


def gather_kernel(
    orders,
    in_a,
    in_b,
    cells,
    out_a,
    out_b,
    cells_out,
    bounce,
    local_sem,
    send_sem,
    recv_sem,
    swap_send,
    swap_recv,
):
    ins, outs = (in_a, in_b), (out_a, out_b)
    stage_count = len(orders[0])
    offsets = []
    for part in range(2):
        offset = 0
        for step, (name, weight) in enumerate(orders[part]):
            offset = offset + bit_of(name, weight) * (1 << step)
        offsets.append(offset)
    locals_now = [
        pltpu.make_async_copy(ins[part], outs[part].at[offsets[part]], local_sem.at[part])
        for part in range(2)
    ]
    place = lax.axis_index("seq")
    own_in = pltpu.make_async_copy(cells.at[place], bounce, local_sem.at[2])
    own_out = pltpu.make_async_copy(bounce, cells_out.at[place], local_sem.at[3])
    own_in.start()
    for copy in locals_now:
        copy.start()
    greet(orders)
    swaps = exchange_copies(cells, cells_out, swap_send, swap_recv)
    for copy in locals_now:
        copy.wait()
    copies = {}

    def send(part, step):
        block = outs[part].at[pl.ds(offsets[part], 1 << step)]
        copy = pltpu.make_async_remote_copy(
            src_ref=block,
            dst_ref=block,
            send_sem=send_sem.at[part, step],
            recv_sem=recv_sem.at[part, step],
            device_id=partner_of(*orders[part][step]),
            device_id_type=pl.DeviceIdType.MESH,
        )
        copy.start()
        copies[part, step] = copy

    for part in range(2):
        send(part, 0)
    for copy in swaps:
        copy.start()
    own_in.wait()
    own_out.start()
    for step in range(stage_count):
        for part in range(2):
            copies[part, step].wait_recv()
            offsets[part] = offsets[part] - bit_of(*orders[part][step]) * (1 << step)
            if step + 1 < stage_count:
                send(part, step + 1)
    for copy in copies.values():
        copy.wait_send()
    for copy in swaps:
        copy.wait()
    own_out.wait()


def gather_windows(orders, win_a, win_b, cells):
    count = 1 << len(orders[0])
    stages = len(orders[0])
    return pl.pallas_call(
        functools.partial(gather_kernel, orders),
        out_shape=(
            jax.ShapeDtypeStruct((count,) + win_a.shape, win_a.dtype),
            jax.ShapeDtypeStruct((count,) + win_b.shape, win_b.dtype),
            jax.ShapeDtypeStruct(cells.shape, cells.dtype),
        ),
        in_specs=[pl.BlockSpec(memory_space=pltpu.VMEM)] * 2
        + [pl.BlockSpec(memory_space=pltpu.HBM)],
        out_specs=[pl.BlockSpec(memory_space=pltpu.VMEM)] * 2
        + [pl.BlockSpec(memory_space=pltpu.HBM)],
        scratch_shapes=[
            pltpu.VMEM(cells.shape[1:], cells.dtype),
            pltpu.SemaphoreType.DMA((4,)),
            pltpu.SemaphoreType.DMA((2, stages)),
            pltpu.SemaphoreType.DMA((2, stages)),
            pltpu.SemaphoreType.DMA((cells.shape[0] - 1,)),
            pltpu.SemaphoreType.DMA((cells.shape[0] - 1,)),
        ],
        compiler_params=pltpu.CompilerParams(
            collective_id=0, has_side_effects=True, vmem_limit_bytes=62 * 1024 * 1024
        ),
    )(win_a, win_b, cells)


def reduce_kernel(
    orders,
    in_a,
    in_b,
    cells,
    out_a,
    out_b,
    cells_out,
    land_a,
    land_b,
    bounce,
    local_sem,
    send_sem,
    recv_sem,
    swap_send,
    swap_recv,
):
    ins, outs, lands = (in_a, in_b), (out_a, out_b), (land_a, land_b)
    stage_count = len(orders[0])
    place = lax.axis_index("seq")
    own_in = pltpu.make_async_copy(cells.at[place], bounce, local_sem.at[0])
    own_out = pltpu.make_async_copy(bounce, cells_out.at[place], local_sem.at[1])
    own_in.start()
    greet(orders)
    swaps = exchange_copies(cells, cells_out, swap_send, swap_recv)
    copies = {}

    def source(part, step, keep):
        name, weight = orders[part][stage_count - 1 - step]
        held = 1 << (stage_count - 1 - step)
        side = bit_of(name, weight)
        side = side if keep else 1 - side
        if step == 0:
            return ins[part].at[pl.ds(side * held, held)]
        base = (1 << stage_count) - (1 << (stage_count - step + 1))
        return lands[part].at[pl.ds(base + side * held, held)]

    def base_of(step):
        return (1 << stage_count) - (1 << (stage_count - step))

    def send(part, step):
        copy = pltpu.make_async_remote_copy(
            src_ref=source(part, step, False),
            dst_ref=lands[part].at[pl.ds(base_of(step), 1 << (stage_count - 1 - step))],
            send_sem=send_sem.at[part, step],
            recv_sem=recv_sem.at[part, step],
            device_id=partner_of(*orders[part][stage_count - 1 - step]),
            device_id_type=pl.DeviceIdType.MESH,
        )
        copy.start()
        copies[part, step] = copy

    for part in range(2):
        send(part, 0)
    for copy in swaps:
        copy.start()
    own_in.wait()
    own_out.start()
    for step in range(stage_count):
        for part in range(2):
            copies[part, step].wait_recv()
            mine = source(part, step, True)
            base = base_of(step)
            if step == stage_count - 1:
                outs[part][...] = mine[0].astype(jnp.float32) + lands[part][base].astype(
                    jnp.float32
                )
                continue

            def add_one(index, carry, mine=mine, part=part, base=base):
                land = lands[part].at[base + index]
                total = mine[index].astype(jnp.float32) + land[...].astype(jnp.float32)
                land[...] = total.astype(land.dtype)
                return carry

            lax.fori_loop(0, 1 << (stage_count - 1 - step), add_one, 0)
            send(part, step + 1)
    for copy in copies.values():
        copy.wait_send()
    for copy in swaps:
        copy.wait()
    own_out.wait()


def reduce_windows(orders, rows_a, rows_b, cells):
    count = 1 << len(orders[0])
    stages = len(orders[0])
    return pl.pallas_call(
        functools.partial(reduce_kernel, orders),
        out_shape=(
            jax.ShapeDtypeStruct(rows_a.shape[1:], jnp.float32),
            jax.ShapeDtypeStruct(rows_b.shape[1:], jnp.float32),
            jax.ShapeDtypeStruct(cells.shape, cells.dtype),
        ),
        in_specs=[pl.BlockSpec(memory_space=pltpu.VMEM)] * 2
        + [pl.BlockSpec(memory_space=pltpu.HBM)],
        out_specs=[pl.BlockSpec(memory_space=pltpu.VMEM)] * 2
        + [pl.BlockSpec(memory_space=pltpu.HBM)],
        scratch_shapes=[
            pltpu.VMEM((count - 1,) + rows_a.shape[1:], rows_a.dtype),
            pltpu.VMEM((count - 1,) + rows_b.shape[1:], rows_b.dtype),
            pltpu.VMEM(cells.shape[1:], cells.dtype),
            pltpu.SemaphoreType.DMA((2,)),
            pltpu.SemaphoreType.DMA((2, stages)),
            pltpu.SemaphoreType.DMA((2, stages)),
            pltpu.SemaphoreType.DMA((cells.shape[0] - 1,)),
            pltpu.SemaphoreType.DMA((cells.shape[0] - 1,)),
        ],
        compiler_params=pltpu.CompilerParams(
            collective_id=1, has_side_effects=True, vmem_limit_bytes=62 * 1024 * 1024
        ),
    )(rows_a, rows_b, cells)


RES_SQUARES = 7 * C * C
RES_ROWS = (RES_SQUARES + TE * C + 8 * C) // 128
INNER = HEADS * HD
TF_SIZES = (3 * C * INNER, INNER * C, C * F, F * C, 6 * C, 3 * F)
TF_ROWS = sum(TF_SIZES) // 128


def place_maps(orders, mesh_sizes):
    count = 1 << len(orders[0])
    return [[owner_place(orders[part], mesh_sizes, i) for i in range(count)] for part in range(2)]


def matrix_views():
    views = []
    row = 0
    for rows, width in ((6 * C, C), (C, C), (TE, C), (8, C)):
        views.append((0, row, rows, width))
        row += rows * width // 128
    row = 0
    for rows, width in ((C, 3 * INNER), (INNER, C), (C, F), (F, C), (6, C), (3, F)):
        views.append((1, row, rows, width))
        row += rows * width // 128
    return views


def assemble(places, lengths_now, in_a, in_b, *refs):
    outs, flats = refs[:10], refs[10:12]
    count = len(places[0])
    for part, ref in enumerate((in_a, in_b)):
        flat = flats[part]
        for i in range(count):
            start, lead = divmod(i * lengths_now[part], 128)
            rows = -(-(lead + lengths_now[part]) // 128)
            if lead:
                edge = flat[start : start + 1, :]
            flat[start : start + rows, :] = ref[places[part][i]].astype(jnp.float32)[:rows]
            if lead:
                flat[start : start + 1, :] = flat[start : start + 1, :] + edge
    for out, (part, row, rows, width) in zip(outs, matrix_views()):
        stride = width // 128
        for lane in range(stride):
            piece = flats[part][pl.ds(row + lane, rows, stride=stride), :]
            out[:, lane * 128 : (lane + 1) * 128] = piece.astype(out.dtype)


def cut(places, lengths_now, *refs):
    ins, outs, flats = refs[:10], refs[10:12], refs[12:14]
    count = len(places[0])
    for ref, (part, row, rows, width) in zip(ins, matrix_views()):
        stride = width // 128
        for lane in range(stride):
            flats[part][pl.ds(row + lane, rows, stride=stride), :] = ref[
                :, lane * 128 : (lane + 1) * 128
            ]
    for part in range(2):
        for i in range(count):
            start, lead = divmod(i * lengths_now[part], 128)
            rows = outs[part].shape[1]
            outs[part][places[part][i]] = flats[part][start : start + rows, :].astype(
                outs[part].dtype
            )


def flat_index(mesh_sizes):
    index = 0
    for name, size in mesh_sizes:
        index = index * size + lax.axis_index(name)
    return index


def to_window(master, rows, owner):
    lead = (owner * master.shape[0]) % 128
    window = jnp.zeros((rows * 128,), jnp.bfloat16)
    return lax.dynamic_update_slice(window, master.astype(jnp.bfloat16), (lead,)).reshape(rows, 128)


def from_window(window, length_now, owner):
    lead = (owner * length_now) % 128
    return lax.dynamic_slice(window.reshape(-1), (lead,), (length_now,))


SIN_TERMS = (
    3.141592640063848,
    -5.167710072816043,
    2.5500772667383647,
    -0.5982893715546711,
    0.07765328748430061,
)
COS_TERMS = (
    0.9999999530157438,
    -4.934792793539851,
    4.058410463392346,
    -1.3318699300230954,
    0.21967444597863747,
)
ROUND_SHIFT = 12582912.0


def mm(left, right):
    return jnp.dot(left, right, preferred_element_type=jnp.float32)


def mm_right(left, right):
    return lax.dot_general(
        left, right, (((1,), (1,)), ((), ())), preferred_element_type=jnp.float32
    )


def mm_left(left, right):
    return lax.dot_general(
        left, right, (((0,), (0,)), ((), ())), preferred_element_type=jnp.float32
    )


def column_sum(cells):
    return jnp.sum(cells, axis=0, keepdims=True)


def sin_cos(half_turns):
    rest = half_turns - ((half_turns + ROUND_SHIFT) - ROUND_SHIFT)
    square = rest * rest
    sine = SIN_TERMS[-1]
    for term in SIN_TERMS[-2::-1]:
        sine = sine * square + term
    cosine = COS_TERMS[-1]
    for term in COS_TERMS[-2::-1]:
        cosine = cosine * square + term
    return (sine * rest, cosine)


def mish_value(signal):
    expo = jnp.exp(jnp.minimum(signal, 20.0))
    upper = expo * (expo + 2.0)
    return signal * (upper / (upper + 2.0))


def mish_slope(signal):
    expo = jnp.exp(jnp.minimum(signal, 20.0))
    upper = expo * (expo + 2.0)
    inverse = 1.0 / (upper + 2.0)
    return upper * inverse + signal * (4.0 * expo * (1.0 + expo)) * (inverse * inverse)


def row_norm(signal):
    center = signal - jnp.mean(signal, axis=-1, keepdims=True)
    spread = jnp.mean(center * center, axis=-1, keepdims=True)
    inverse = lax.rsqrt(spread + EPSILON)
    return (center * inverse, inverse)


def row_norm_back(grad_out, normed, inverse, gain_row):
    inner_grad = grad_out * gain_row
    first = jnp.mean(inner_grad, axis=-1, keepdims=True)
    second = jnp.mean(inner_grad * normed, axis=-1, keepdims=True)
    return (inner_grad - first - normed * second) * inverse


def step_kernel(
    places,
    shard_lengths,
    lengths_ref,
    place_ref,
    cells_ref,
    time_ref,
    win_a,
    win_b,
    results_ref,
    cut_a,
    cut_b,
    convs_ref,
    res_ref,
    timew_ref,
    rows_ref,
    qkv_ref,
    out_ref,
    up_ref,
    down_ref,
    tf_rows_ref,
    wide_ref,
    gconvs_ref,
    gres_ref,
    gtimew_ref,
    grows_ref,
    gqkv_ref,
    gout_ref,
    gup_ref,
    gdown_ref,
    gtf_ref,
    gwide_ref,
    flat_a,
    flat_b,
    time_rows,
    gtime_rows,
    pad,
    col_one,
    col_two,
    col_grad,
    z_one,
    z_two,
    block,
    grad_mid,
    grad_norm,
    attn_in,
    heads_q,
    heads_k,
    heads_v,
    heads_g,
    attn_vals,
    probs,
    snake,
    grad_up,
    ff_in,
    grad_attn,
    grad_key,
    grad_value,
    grad_query,
    grad_qkv,
    grad_skip,
):
    frames = z_one.shape[0]
    tiles, _, tile, _ = cells_ref.shape
    utt = pl.program_id(0)
    row_at = place_ref[0] * pl.num_programs(0) + utt
    length_now = lengths_ref[row_at]
    number = length_now.astype(jnp.float32) * (C // GROUPS)
    weight_refs = (
        convs_ref,
        res_ref,
        timew_ref,
        rows_ref,
        qkv_ref,
        out_ref,
        up_ref,
        down_ref,
        tf_rows_ref,
        wide_ref,
    )
    grad_refs = (
        gconvs_ref,
        gres_ref,
        gtimew_ref,
        grows_ref,
        gqkv_ref,
        gout_ref,
        gup_ref,
        gdown_ref,
        gtf_ref,
        gwide_ref,
    )

    @pl.when(utt == 0)
    def begin():
        assemble(places, shard_lengths, win_a, win_b, *weight_refs, flat_a, flat_b)
        for ref in grad_refs:
            ref[...] = jnp.zeros_like(ref)
        gtime_rows[...] = jnp.zeros_like(gtime_rows)
        low = mish_value(time_ref[...]).astype(jnp.bfloat16)
        time_rows[...] = mm(low, timew_ref[...]) + rows_ref[7:8, :]

    time_row = time_rows[pl.ds(row_at, 1), :]
    edge = jnp.zeros((8, C), jnp.float32)
    pad[0:8, :] = edge
    pad[frames + 8 : frames + 16, :] = edge
    group_row = lax.broadcasted_iota(jnp.int32, (C, C), 0) // (C // GROUPS)
    group_column = lax.broadcasted_iota(jnp.int32, (C, C), 1) // (C // GROUPS)
    group_ones = (group_row == group_column).astype(jnp.float32)
    lane = lax.broadcasted_iota(jnp.int32, (1, INNER), 1) // HD
    head_masks = [(lane == head).astype(jnp.float32) for head in range(HEADS)]
    key_bias = jnp.where(
        lax.broadcasted_iota(jnp.int32, (1, frames), 1) < length_now, 0.0, MASK_FILL
    )

    def rows_at(index, lead=0):
        return pl.ds(pl.multiple_of(index * tile + lead, 8), tile)

    def tile_mask(index):
        ids = lax.broadcasted_iota(jnp.int32, (tile, 1), 0) + index * tile
        return (ids < length_now).astype(jnp.float32)

    def group_sum(row):
        wide = jnp.broadcast_to(row, (8, C))
        return jnp.dot(
            wide,
            group_ones,
            precision=lax.Precision.HIGHEST,
            preferred_element_type=jnp.float32,
        )[0:1]

    def build_columns(target):
        for index in range(tiles):
            start = index * tile
            for tap in range(3):
                piece = pad[start + 7 + tap : start + 7 + tap + tile, :]
                target[start : start + tile, tap * C : (tap + 1) * C] = piece.astype(jnp.bfloat16)

    def loop(body):
        def wrapped(index, carry):
            body(index)
            return carry

        lax.fori_loop(0, tiles, wrapped, 0)

    def conv_stage(columns, base, bias_at, target):
        def one(index, carry):
            rows = rows_at(index)
            cells = mm(columns[rows, :], convs_ref[base : base + 3 * C, :])
            cells = cells + rows_ref[bias_at : bias_at + 1, :]
            target[rows, :] = cells
            masked = cells * tile_mask(index)
            return (carry[0] + column_sum(masked), carry[1] + column_sum(masked * masked))

        zero = jnp.zeros((1, C), jnp.float32)
        total, squares = lax.fori_loop(0, tiles, one, (zero, zero))
        mean_row = group_sum(total) / number
        inv_row = lax.rsqrt(group_sum(squares) / number - mean_row * mean_row + EPSILON)
        return (mean_row, inv_row)

    def copy_in(index):
        pad[rows_at(index, 8), :] = cells_ref[index, 0, :, 0:C].astype(jnp.float32)

    loop(copy_in)
    build_columns(col_one)
    mean_one, inv_one = conv_stage(col_one, 0, 0, z_one)

    def hidden(index):
        normed = (z_one[rows_at(index), :] - mean_one) * inv_one
        act = mish_value(normed * rows_ref[1:2, :] + rows_ref[2:3, :])
        pad[rows_at(index, 8), :] = (act + time_row) * tile_mask(index)

    loop(hidden)
    build_columns(col_two)
    mean_two, inv_two = conv_stage(col_two, 3 * C, 3, z_two)

    def enter(index):
        rows = rows_at(index)
        normed = (z_two[rows, :] - mean_two) * inv_two
        act = mish_value(normed * rows_ref[4:5, :] + rows_ref[5:6, :]) * tile_mask(index)
        state = act + mm(cells_ref[index, 0, :, 0:C], res_ref[...]) + rows_ref[6:7, :]
        block[rows, :] = state
        normed, _ = row_norm(state)
        low = (normed * tf_rows_ref[0:1, :] + tf_rows_ref[1:2, :]).astype(jnp.bfloat16)
        attn_in[rows, :] = low
        parts = mm(low, qkv_ref[...]).astype(jnp.bfloat16).astype(jnp.float32)
        query = parts[:, :INNER] * SCORE_SCALE
        for head in range(HEADS):
            heads_q[head, rows, :] = (query * head_masks[head]).astype(jnp.bfloat16)
            heads_k[head, rows, :] = (parts[:, INNER : 2 * INNER] * head_masks[head]).astype(
                jnp.bfloat16
            )
            heads_v[head, rows, :] = (parts[:, 2 * INNER :] * head_masks[head]).astype(
                jnp.bfloat16
            )

    loop(enter)

    def attend(index):
        rows = rows_at(index)
        total = jnp.zeros((tile, INNER), jnp.float32)
        for head in range(HEADS):
            scores = mm_right(heads_q[head, rows, :], heads_k[head]) + key_bias
            expo = jnp.exp(scores - jnp.max(scores, axis=-1, keepdims=True))
            chance = expo * (1.0 / jnp.sum(expo, axis=-1, keepdims=True))
            probs[head, rows, :] = chance
            total = total + mm(chance.astype(jnp.bfloat16), heads_v[head])
        attn_vals[rows, :] = total.astype(jnp.bfloat16)

    loop(attend)

    def feed(index):
        rows = rows_at(index)
        mid = block[rows, :] + mm(attn_vals[rows, :], out_ref[...]) + tf_rows_ref[2:3, :]
        normed, inverse = row_norm(mid)
        low = (normed * tf_rows_ref[3:4, :] + tf_rows_ref[4:5, :]).astype(jnp.bfloat16)
        ff_in[rows, :] = low
        grad_low = cells_ref[index, 0, :, C : 2 * C]
        result = jnp.zeros((tile, C), jnp.float32)
        grad_in = jnp.zeros((tile, C), jnp.float32)
        for chunk in range(F // 256):
            lanes = slice(chunk * 256, (chunk + 1) * 256)
            up_out = mm(low, up_ref[:, lanes]) + wide_ref[0:1, lanes]
            grad_snake = mm_right(grad_low, down_ref[lanes, :])
            speed = jnp.exp(wide_ref[1:2, lanes])
            depth = 1.0 / (jnp.exp(wide_ref[2:3, lanes]) + 1e-09)
            half_turns = up_out * (speed * (1.0 / math.pi))
            sine, cosine = sin_cos(half_turns)
            square = sine * sine
            value = (up_out + square * depth).astype(jnp.bfloat16)
            snake[rows, lanes] = value
            result = result + mm(value, down_ref[lanes, :])
            slope = (grad_snake * (2.0 * depth)) * (sine * cosine)
            grad_here = (grad_snake + slope * speed).astype(jnp.bfloat16)
            grad_up[rows, lanes] = grad_here
            grad_in = grad_in + mm_right(grad_here, up_ref[:, lanes])
            gwide_ref[0:1, lanes] += column_sum(grad_here.astype(jnp.float32))
            gwide_ref[1:2, lanes] += column_sum(slope * half_turns)
            gwide_ref[2:3, lanes] += column_sum(grad_snake * square)
        results_ref[index, 0, :, 0:C] = ((mid + result + tf_rows_ref[5:6, :]) * tile_mask(index)).astype(
            jnp.bfloat16
        )
        grad_wide = grad_low.astype(jnp.float32)
        gtf_ref[5:6, :] += column_sum(grad_wide)
        gtf_ref[3:4, :] += column_sum(grad_in * normed)
        gtf_ref[4:5, :] += column_sum(grad_in)
        grad_state = grad_wide + row_norm_back(grad_in, normed, inverse, tf_rows_ref[3:4, :])
        grad_mid[rows, :] = grad_state
        grad_state = grad_state.astype(jnp.bfloat16)
        grad_attn[rows, :] = grad_state
        gtf_ref[2:3, :] += column_sum(grad_state.astype(jnp.float32))
        grad_vals = mm_right(grad_state, out_ref[...]).astype(jnp.bfloat16).astype(jnp.float32)
        for head in range(HEADS):
            heads_g[head, rows, :] = (grad_vals * head_masks[head]).astype(jnp.bfloat16)

    loop(feed)

    def feed_weights(index, carry):
        lanes = pl.ds(pl.multiple_of(index * 256, 256), 256)
        grads = cells_ref[:, 0, :, C : 2 * C].reshape(frames, C)
        gdown_ref[lanes, :] += mm_left(snake[:, lanes], grads)
        gup_ref[:, lanes] += mm_left(ff_in[...], grad_up[:, lanes])
        return carry

    lax.fori_loop(0, F // 256, feed_weights, 0)
    gout_ref[...] += mm_left(attn_vals[...], grad_attn[...])
    grad_key[...] = jnp.zeros_like(grad_key)
    grad_value[...] = jnp.zeros_like(grad_value)

    def attend_back(index):
        rows = rows_at(index)
        total = jnp.zeros((tile, INNER), jnp.float32)
        scores_low, chances_low = [], []
        for head in range(HEADS):
            grad_out = heads_g[head, rows, :]
            chance = probs[head, rows, :]
            grad_probs = mm_right(grad_out, heads_v[head])
            dot_row = jnp.sum(chance * grad_probs, axis=-1, keepdims=True)
            grad_scores = (chance * (grad_probs - dot_row)).astype(jnp.bfloat16)
            total = total + mm(grad_scores, heads_k[head])
            scores_low.append(grad_scores)
            chances_low.append(chance.astype(jnp.bfloat16))
        both = (HEADS * tile, INNER)
        grad_key[...] += mm_left(
            jnp.concatenate(scores_low, axis=0), heads_q[:, rows, :].reshape(both)
        )
        grad_value[...] += mm_left(
            jnp.concatenate(chances_low, axis=0), heads_g[:, rows, :].reshape(both)
        )
        grad_query[rows, :] = total * SCORE_SCALE

    loop(attend_back)

    def leave(index, carry):
        rows = rows_at(index)
        grad_qkv[rows, 0:INNER] = grad_query[rows, :].astype(jnp.bfloat16)
        grad_qkv[rows, INNER : 2 * INNER] = grad_key[rows, :].astype(jnp.bfloat16)
        grad_qkv[rows, 2 * INNER : 3 * INNER] = grad_value[rows, :].astype(jnp.bfloat16)
        grad_in = mm_right(grad_qkv[rows, :], qkv_ref[...])
        normed, inverse = row_norm(block[rows, :])
        gtf_ref[0:1, :] += column_sum(grad_in * normed)
        gtf_ref[1:2, :] += column_sum(grad_in)
        grad_state = grad_mid[rows, :] + row_norm_back(
            grad_in, normed, inverse, tf_rows_ref[0:1, :]
        )
        low = grad_state.astype(jnp.bfloat16)
        grad_skip[rows, :] = low
        grows_ref[6:7, :] += column_sum(low.astype(jnp.float32))
        normed = (z_two[rows, :] - mean_two) * inv_two
        grad_here = (
            mish_slope(normed * rows_ref[4:5, :] + rows_ref[5:6, :])
            * tile_mask(index)
            * grad_state
        )
        grad_norm[rows, :] = grad_here
        return (carry[0] + column_sum(grad_here), carry[1] + column_sum(grad_here * normed))

    zero = jnp.zeros((1, C), jnp.float32)

    def norm_back(target, mean_row, inv_row, gain_at, bias_at, shift_sum, gain_sum):
        gain_row = rows_ref[gain_at : gain_at + 1, :]
        grows_ref[gain_at : gain_at + 1, :] += gain_sum
        grows_ref[gain_at + 1 : gain_at + 2, :] += shift_sum
        first = group_sum(shift_sum * gain_row) / number
        second = group_sum(gain_sum * gain_row) / number

        def one(index):
            rows = rows_at(index)
            normed = (target[rows, :] - mean_row) * inv_row
            cells = inv_row * (
                grad_norm[rows, :] * gain_row - tile_mask(index) * (first + normed * second)
            )
            cells = cells.astype(jnp.bfloat16).astype(jnp.float32)
            grows_ref[bias_at : bias_at + 1, :] += column_sum(cells)
            pad[rows_at(index, 8), :] = cells

        loop(one)
        build_columns(col_grad)

    def conv_back(rows, base):
        total = mm_right(col_grad[rows, 2 * C : 3 * C], convs_ref[base : base + C, :])
        total = total + mm_right(col_grad[rows, C : 2 * C], convs_ref[base + C : base + 2 * C, :])
        return total + mm_right(col_grad[rows, 0:C], convs_ref[base + 2 * C : base + 3 * C, :])

    def conv_weights(columns, base):
        for tap in range(3):
            gconvs_ref[base + tap * C : base + (tap + 1) * C, :] += mm_left(
                columns[:, tap * C : (tap + 1) * C], col_grad[:, C : 2 * C]
            )

    shift_sum, gain_sum = lax.fori_loop(0, tiles, leave, (zero, zero))
    norm_back(z_two, mean_two, inv_two, 4, 3, shift_sum, gain_sum)
    conv_weights(col_two, 3 * C)

    def hidden_back(index, carry):
        rows = rows_at(index)
        grad_here = conv_back(rows, 3 * C) * tile_mask(index)
        time_sum = column_sum(grad_here)
        normed = (z_one[rows, :] - mean_one) * inv_one
        grad_here = mish_slope(normed * rows_ref[1:2, :] + rows_ref[2:3, :]) * grad_here
        grad_norm[rows, :] = grad_here
        return (
            carry[0] + column_sum(grad_here),
            carry[1] + column_sum(grad_here * normed),
            carry[2] + time_sum,
        )

    shift_sum, gain_sum, time_sum = lax.fori_loop(0, tiles, hidden_back, (zero, zero, zero))
    grows_ref[7:8, :] += time_sum
    gtime_rows[pl.ds(row_at, 1), :] = time_sum
    norm_back(z_one, mean_one, inv_one, 1, 0, shift_sum, gain_sum)
    conv_weights(col_one, 0)

    def finish(index):
        rows = rows_at(index)
        total = conv_back(rows, 0) + mm_right(grad_skip[rows, :], res_ref[...])
        results_ref[index, 0, :, C : 2 * C] = (total * tile_mask(index)).astype(jnp.bfloat16)

    loop(finish)
    gres_ref[...] += mm_left(cells_ref[:, 0, :, 0:C].reshape(frames, C), grad_skip[...])
    gqkv_ref[...] += mm_left(attn_in[...], grad_qkv[...])

    @pl.when(utt == pl.num_programs(0) - 1)
    def end():
        low_side = jnp.exp(wide_ref[2:3, :])
        depth = 1.0 / (low_side + 1e-09)
        gwide_ref[1:2, :] = gwide_ref[1:2, :] * math.pi
        gwide_ref[2:3, :] = -gwide_ref[2:3, :] * low_side * depth * depth
        time_low = mish_value(time_ref[...]).astype(jnp.bfloat16).astype(jnp.float32)
        gtimew_ref[...] = lax.dot_general(
            time_low,
            gtime_rows[...],
            (((0,), (0,)), ((), ())),
            precision=lax.Precision.HIGHEST,
            preferred_element_type=jnp.float32,
        )
        cut(places, shard_lengths, *grad_refs, cut_a, cut_b, flat_a, flat_b)


def whole_step(places, shard_lengths, lengths, place, cells, time_embed, windows):
    tiles, utts, tile, _ = cells.shape
    frames = tiles * tile
    by_utt = pl.BlockSpec((tiles, 1, tile, 2 * C), lambda u, n, p: (0, u, 0, 0))

    def fixed(array):
        return pl.BlockSpec(
            array.shape, lambda u, n, p: (0,) * array.ndim, pipeline_mode=pl.Buffered(1)
        )

    f32, low = jnp.float32, jnp.bfloat16
    weight_kinds = [
        ((rows, width), f32 if index in (3, 8, 9) else low)
        for index, (part, row, rows, width) in enumerate(matrix_views())
    ]
    scratch = weight_kinds + [(shape, f32) for shape, kind in weight_kinds]
    scratch += [
        ((RES_ROWS + 24, 128), f32),
        ((TF_ROWS + 28, 128), f32),
        (time_embed.shape[:1] + (C,), f32),
        (time_embed.shape[:1] + (C,), f32),
        ((frames + 16, C), f32),
        ((frames, 3 * C), low),
        ((frames, 3 * C), low),
        ((frames, 3 * C), low),
        ((frames, C), f32),
        ((frames, C), f32),
        ((frames, C), f32),
        ((frames, C), f32),
        ((frames, C), f32),
        ((frames, C), low),
        ((HEADS, frames, INNER), low),
        ((HEADS, frames, INNER), low),
        ((HEADS, frames, INNER), low),
        ((HEADS, frames, INNER), low),
        ((frames, INNER), low),
        ((HEADS, frames, frames), f32),
        ((frames, F), low),
        ((frames, F), low),
        ((frames, C), low),
        ((frames, C), low),
        ((frames, INNER), f32),
        ((frames, INNER), f32),
        ((frames, INNER), f32),
        ((frames, 3 * INNER), low),
        ((frames, C), low),
    ]
    return pl.pallas_call(
        functools.partial(step_kernel, places, shard_lengths),
        grid_spec=pltpu.PrefetchScalarGridSpec(
            num_scalar_prefetch=2,
            grid=(utts,),
            in_specs=[by_utt] + [fixed(array) for array in (time_embed, *windows)],
            out_specs=[by_utt] + [fixed(array) for array in windows],
            scratch_shapes=[pltpu.VMEM(shape, kind) for shape, kind in scratch],
        ),
        out_shape=[jax.ShapeDtypeStruct(array.shape, low) for array in (cells, *windows)],
        compiler_params=pltpu.CompilerParams(
            dimension_semantics=("arbitrary",), vmem_limit_bytes=61 * 1024 * 1024
        ),
    )(lengths, place, cells, time_embed, *windows)


def prepare_kernel(
    lengths_ref, place_ref, inputs_ref, encoded_ref, durations_ref, cotangent_ref, out_ref
):
    group, frames, _ = inputs_ref.shape
    phones = durations_ref.shape[2]
    first = place_ref[0] * frames
    before = lax.broadcasted_iota(jnp.int32, (phones, phones), 0)
    after = lax.broadcasted_iota(jnp.int32, (phones, phones), 1)
    upper = (before <= after).astype(jnp.bfloat16)
    last = lax.broadcasted_iota(jnp.int32, (1, phones), 1) == phones - 1
    ids = lax.broadcasted_iota(jnp.int32, (frames, 1), 0) + first
    times = ids.astype(jnp.float32)
    for utt in range(group):
        durations = durations_ref[utt].astype(jnp.float32)
        wide = jnp.broadcast_to(durations, (16, phones)).astype(jnp.bfloat16)
        ends = mm(wide, upper)[0:1]
        starts = ends - durations
        ends = jnp.where(last, 1e9, ends)
        picked = jnp.where((times >= starts) & (times < ends), 1.0, 0.0).astype(jnp.bfloat16)
        table = encoded_ref[utt]
        high = table.astype(jnp.bfloat16)
        rest = table - high.astype(jnp.float32)
        middle = rest.astype(jnp.bfloat16)
        low = (rest - middle.astype(jnp.float32)).astype(jnp.bfloat16)
        rows = (mm(picked, high) + mm(picked, middle)) + mm(picked, low)
        mask = (ids < lengths_ref[pl.program_id(0) * group + utt]).astype(jnp.float32)
        out_ref[0, utt, :, 0:C] = ((inputs_ref[utt] + rows) * mask).astype(jnp.bfloat16)
        out_ref[0, utt, :, C : 2 * C] = (cotangent_ref[utt] * mask).astype(jnp.bfloat16)


def prepare(inputs, encoded, durations, lengths, place, cotangent):
    utts, frames, _ = inputs.shape
    phones = durations.shape[1]
    seq_size = lax.axis_size("seq")
    group = utts // seq_size
    by_group = lambda s, n, p: (s, 0, 0)
    return pl.pallas_call(
        prepare_kernel,
        grid_spec=pltpu.PrefetchScalarGridSpec(
            num_scalar_prefetch=2,
            grid=(seq_size,),
            in_specs=[
                pl.BlockSpec((group, frames, C), by_group),
                pl.BlockSpec((group, phones, C), by_group),
                pl.BlockSpec((group, 1, phones), by_group),
                pl.BlockSpec((group, frames, C), by_group),
            ],
            out_specs=pl.BlockSpec((1, group, frames, 2 * C), lambda s, n, p: (s, 0, 0, 0)),
        ),
        out_shape=jax.ShapeDtypeStruct((seq_size, group, frames, 2 * C), jnp.bfloat16),
        compiler_params=pltpu.CompilerParams(dimension_semantics=("arbitrary",)),
    )(lengths, place, inputs, encoded, durations[:, None, :], cotangent)


def per_device(
    inputs,
    encoded,
    durations,
    lengths,
    time_embed,
    cotangent,
    res_master,
    res_moment,
    res_average,
    tf_master,
    tf_moment,
    tf_average,
):
    utts_here, local_len, _ = inputs.shape
    key_total = local_len * lax.axis_size("seq")
    place = jnp.full((1,), lax.axis_index("seq"), jnp.int32)
    cells = prepare(inputs, encoded, durations, lengths, place, cotangent)
    mesh_sizes = [(name, lax.axis_size(name)) for name in ("dp", "seq")]
    orders = part_orders(mesh_sizes)
    places = place_maps(orders, mesh_sizes)
    owner = flat_index(mesh_sizes)
    shard_lengths = (res_master.shape[0], tf_master.shape[0])
    window_sizes = [window_rows(size, len(places[0])) for size in shard_lengths]
    *gathered, cells = gather_windows(
        orders,
        to_window(res_master, window_sizes[0], owner),
        to_window(tf_master, window_sizes[1], owner),
        cells,
    )
    results, *cuts = whole_step(
        places, shard_lengths, lengths, place, cells, time_embed, gathered
    )
    *summed, results = reduce_windows(orders, *cuts, results)
    results = results.reshape(utts_here, local_len, 2 * C)
    res_share = from_window(summed[0], shard_lengths[0], owner)
    tf_share = from_window(summed[1], shard_lengths[1], owner)
    tokens_total = utts_here * key_total * lax.axis_size("dp")
    rate = LEARN_BASE / math.sqrt(tokens_total)
    res_new, res_moment_new, res_average_new, res_low = update(
        res_master, res_moment, res_average, res_share, rate
    )
    tf_new, tf_moment_new, tf_average_new, tf_low = update(
        tf_master, tf_moment, tf_average, tf_share, rate
    )
    return (
        results[:, :, :C].astype(jnp.float32),
        results[:, :, C:].astype(jnp.float32),
        res_share,
        tf_share,
        res_new,
        tf_new,
        res_moment_new,
        tf_moment_new,
        res_average_new,
        tf_average_new,
        res_low,
        tf_low,
    )


def solution(mesh):
    placed = (
        P("dp", "seq", None),
        P("dp", None, None),
        P("dp", None),
        P("dp"),
        P("dp", None),
        P("dp", "seq", None),
        P(("dp", "seq")),
        P(("dp", "seq")),
        P(("dp", "seq")),
        P(("dp", "seq")),
        P(("dp", "seq")),
        P(("dp", "seq")),
    )
    return jax.shard_map(
        per_device,
        mesh=mesh,
        in_specs=placed,
        out_specs=(
            P("dp", "seq", None),
            P("dp", "seq", None),
            P(("dp", "seq")),
            P(("dp", "seq")),
            P(("dp", "seq")),
            P(("dp", "seq")),
            P(("dp", "seq")),
            P(("dp", "seq")),
            P(("dp", "seq")),
            P(("dp", "seq")),
            P(("dp", "seq")),
            P(("dp", "seq")),
        ),
        check_vma=False,
    )
```
